128 devices in a mesh: region: 16 (over z, x), member: 8 (over y, core).
Axes of the slice: x: 4, y: 4, z: 4, core: 2. Of those that a mesh axis runs over, the one named last changes fastest.
Arguments:
- ensemble: bfloat16 [256, 32, 64, 512], P('region', 'member'), may hold values from -6 to 6
- increment: bfloat16 [256, 64, 512], P('region'), may hold values from -6 to 6
- coords: bfloat16 [256, 2, 512], P('region'), may hold values from -4.5 to 5.5
- sent_slots: int32 [16, 16, 1], P('region'), may hold values from 0 to 15, as said below
- pair_list: int32 [512, 2], P('region'), may hold values from 0 to 15, as said below
- pair_count: int32 [16], P('region'), may hold values from 16 to 32, as said below
Outputs:
- covariance_product: float32 [256, 64, 512], P('region', 'member')
The draws below stay inside these ranges and needn't reach their ends.
Inputs may be any that keep to these rules, and one draw needn't show every extreme that they name: `sent_slots`: the k numbers of one home and owner are distinct. `pair_list`: the two slots of a row differ; every received slot is named by some live row of its owner. `pair_count`: some owner has exactly 32 live pairs and some has 16.
All inputs are finite; a program needn't handle non-finite values.
Results may differ from the reference program's by a relative error of at most 0.0028.
Values may be sent and summed in bfloat16 or wider, within the bound.
No kernel may reach another device: no remote copies, remote signals or barrier semaphores. Data moves between devices by JAX's collectives and lax.ppermute only.
A program may use at most 128 MiB of HBM per device.

```python
import jax
import jax.numpy as jnp
from jax import lax

PTS = 512
LEV = 64
BLK_DEV = 16
REQ = 1
NB = 256
MEMBERS = 32
PAIR_CAP = 32
N_REGION = 16


def draw_coords(key, part):
    first_key, second_key = jax.random.split(key, 2)
    centre = jax.random.uniform(first_key, (NB, 2, 1), jnp.float32, 0.0, 1.0)
    offset = jax.random.uniform(second_key, (NB, 2, PTS), jnp.float32, -4.0, 4.0)
    return (centre + offset).astype(jnp.bfloat16)


def draw_sent_slots(key, part):
    scores = jax.random.randint(key, (N_REGION, N_REGION, BLK_DEV), 0, 1 << 20) * BLK_DEV + jnp.arange(BLK_DEV, dtype=jnp.int32)
    ranked = jnp.argsort(scores, axis=-1)
    return ranked[:, :, :REQ].astype(jnp.int32)


def draw_pair_list(key, part):
    slot_total = N_REGION * REQ
    first_key, second_key, third_key = jax.random.split(key, 3)
    scores = jax.random.randint(first_key, (N_REGION, slot_total), 0, 1 << 20) * slot_total + jnp.arange(slot_total, dtype=jnp.int32)
    ranked = jnp.argsort(scores, axis=-1).astype(jnp.int32)
    cycle_second = jnp.roll(ranked, -1, axis=1)
    extra_first = jax.random.randint(second_key, (N_REGION, slot_total), 0, slot_total)
    extra_second = (extra_first + jax.random.randint(third_key, (N_REGION, slot_total), 1, slot_total)) % slot_total
    first_slot = jnp.concatenate([ranked, extra_first], axis=1)
    second_slot = jnp.concatenate([cycle_second, extra_second], axis=1)
    return jnp.stack([first_slot, second_slot], axis=-1).reshape(N_REGION * 2 * slot_total, 2).astype(jnp.int32)


def draw_pair_count(key, part):
    slot_total = N_REGION * REQ
    first_key, second_key, third_key = jax.random.split(key, 3)
    counts = jax.random.randint(first_key, (N_REGION,), slot_total, 2 * slot_total + 1)
    busiest = jax.random.randint(second_key, (), 0, N_REGION)
    lightest = (busiest + jax.random.randint(third_key, (), 1, N_REGION)) % N_REGION
    owners = jnp.arange(N_REGION, dtype=jnp.int32)
    counts = jnp.where(owners == busiest, 2 * slot_total, jnp.where(owners == lightest, slot_total, counts))
    return counts.astype(jnp.int32)


def block_scale(own_key, shape, cuts, least, high):
    loudness, own = 1.0, jax.random.fold_in(own_key, 6)
    for dim, shards_of in cuts:
        draws = jnp.exp(jax.random.uniform(jax.random.fold_in(own, dim), (shards_of,), jnp.float32, least / len(cuts), high / len(cuts)))
        loudness = loudness * jnp.repeat(draws, shape[dim] // shards_of).reshape([-1 if axis == dim else 1 for axis in range(len(shape))])
    return loudness


def scatter_about(own_key, extent, spread, limit, pieces=(), kind=jnp.bfloat16):
    entries = jax.random.normal(own_key, extent, jnp.float32) * spread
    if len(pieces) > 0:
        entries = block_scale(own_key, extent, pieces, -0.22, 0.18) * entries
    return jnp.clip(entries, min=-limit, max=limit).astype(kind)


def setup_inputs(seed: int = 0) -> dict:
    keys = jax.random.split(jax.random.key(seed), 7)
    ensemble = scatter_about(keys[0], (NB, MEMBERS, LEV, PTS), 1.0, 6.0, ((0, 16), (1, 8)))
    increment = scatter_about(keys[1], (NB, LEV, PTS), 1.0, 6.0, ((0, 16),))
    coords = draw_coords(jax.random.fold_in(keys[6], 71), 0)
    sent_slots = draw_sent_slots(jax.random.fold_in(keys[6], 71), 0)
    pair_list = draw_pair_list(jax.random.fold_in(keys[6], 71), 0)
    pair_count = draw_pair_count(jax.random.fold_in(keys[6], 71), 0)
    return dict(ensemble=ensemble, increment=increment, coords=coords, sent_slots=sent_slots, pair_list=pair_list, pair_count=pair_count)


def gaspari_cohn(distance):
    inside_part = (((-0.25 * distance + 0.5) * distance + 0.625) * distance - 5.0 / 3.0) * distance * distance + 1.0
    floored = jnp.maximum(distance, 1.0)
    outside_part = ((((distance / 12.0 - 0.5) * distance + 0.625) * distance + 5.0 / 3.0) * distance - 5.0) * distance + 4.0 - 2.0 / (3.0 * floored)
    return jnp.where(distance <= 1.0, inside_part, jnp.where(distance < 2.0, outside_part, 0.0))

def tile_of(left_where, right_where):
    left_float = left_where.astype(jnp.float32)
    right_float = right_where.astype(jnp.float32)
    east_gap = left_float[0][:, None] - right_float[0][None, :]
    north_gap = left_float[1][:, None] - right_float[1][None, :]
    return gaspari_cohn(jnp.sqrt(east_gap * east_gap + north_gap * north_gap)).astype(jnp.bfloat16)

def reference(ensemble, increment, coords, sent_slots, pair_list, pair_count):
    blocks, members, levels, points = ensemble.shape
    weighted = (ensemble.astype(jnp.float32) * increment[:, None].astype(jnp.float32)).astype(jnp.bfloat16)
    flat_blocks = weighted.reshape(blocks, members * levels, points)

    def diag_one(pair_entry):
        member_rows, places = pair_entry
        local_tile = tile_of(places, places)
        return lax.dot_general(member_rows, local_tile, (((1,), (1,)), ((), ())), preferred_element_type=jnp.float32)
    field_sum = lax.map(diag_one, (flat_blocks, coords))
    homes = jnp.arange(N_REGION, dtype=jnp.int32)
    block_table = homes[:, None, None] * BLK_DEV + sent_slots
    block_table = jnp.transpose(block_table, (1, 0, 2)).reshape(N_REGION, N_REGION * REQ)
    owner_of = jnp.repeat(jnp.arange(N_REGION, dtype=jnp.int32), PAIR_CAP)
    row_index = jnp.tile(jnp.arange(PAIR_CAP, dtype=jnp.int32), N_REGION)
    live_flags = row_index < pair_count[owner_of]
    first_block = block_table[owner_of, pair_list[:, 0]]
    second_block = block_table[owner_of, pair_list[:, 1]]

    def add_pair(totals, pair_entry):
        first_one, second_one, is_live = pair_entry

        def apply_pair(current):
            local_tile = tile_of(coords[first_one], coords[second_one])
            to_first = lax.dot_general(flat_blocks[second_one], local_tile, (((1,), (1,)), ((), ())), preferred_element_type=jnp.float32)
            to_second = jnp.dot(flat_blocks[first_one], local_tile, preferred_element_type=jnp.float32)
            current = current.at[first_one].add(to_first)
            return current.at[second_one].add(to_second)
        return (lax.cond(is_live, apply_pair, lambda current: current, totals), None)
    field_sum, _ = lax.scan(add_pair, field_sum, (first_block, second_block, live_flags))
    combined = lax.optimization_barrier(jnp.sum(ensemble.astype(jnp.float32) * field_sum.reshape(blocks, members, levels, points), axis=1))
    return combined / (members - 1)
```

```python
import functools

import jax
import jax.numpy as jnp
from jax import lax
from jax.experimental import pallas as pl
from jax.experimental.pallas import tpu as pltpu
from jax.sharding import PartitionSpec as P

ROWS = 16
TILE_GROUP = 4
VMEM_CAP = 56 * 1024 * 1024


def pack_kernel(slots, own, ens_ref, inc_ref, coords_ref, big_ref, small_ref):
    members, levels, points = ens_ref.shape[1:]
    parts = big_ref.shape[1]
    step = levels // parts
    for part in range(parts):
        big_ref[0, part] = ens_ref[0, :, part * step : (part + 1) * step, :]
    small_ref[0, 0:step, :] = inc_ref[0]
    small_ref[0, step : step + 2, :] = coords_ref[0]
    small_ref[0, step + 2 :, :] = jnp.zeros_like(small_ref[0, step + 2 :, :])


def pack(ensemble, increment, coords, slots, own, parts):
    blocks, members, levels, points = ensemble.shape
    step = levels // parts
    total = slots.shape[0]
    return pl.pallas_call(
        pack_kernel,
        grid_spec=pltpu.PrefetchScalarGridSpec(
            num_scalar_prefetch=2,
            grid=(total,),
            in_specs=[
                pl.BlockSpec((1, members, levels, points), lambda o, s, j: (s[o], 0, 0, 0)),
                pl.BlockSpec((1, step, points), lambda o, s, j: (s[o], j[0], 0)),
                pl.BlockSpec((1, 2, points), lambda o, s, j: (s[o], 0, 0)),
            ],
            out_specs=[
                pl.BlockSpec((1, parts, members, step, points), lambda o, s, j: (o, 0, 0, 0, 0)),
                pl.BlockSpec((1, 2 * step, points), lambda o, s, j: (o, 0, 0)),
            ],
        ),
        out_shape=[
            jax.ShapeDtypeStruct((total, parts, members, step, points), ensemble.dtype),
            jax.ShapeDtypeStruct((total, 2 * step, points), increment.dtype),
        ],
        compiler_params=pltpu.CompilerParams(vmem_limit_bytes=16 * 1024 * 1024),
        name="pack",
    )(slots, own, ensemble, increment, coords)


def gaspari_cohn(east_gap, north_gap):
    squared = jnp.maximum(east_gap * east_gap + north_gap * north_gap, 2.0**-12)
    inverse = lax.rsqrt(squared)
    z = squared * inverse
    outer = jnp.maximum(2.0 - z, 0.0)
    inner = jnp.maximum(1.0 - z, 0.0)
    outer2 = outer * outer
    inner2 = inner * inner
    shifted = z + 2.0
    first = (outer2 * outer2) * (z * shifted - 0.5)
    second = (inner2 * inner2) * (inner * shifted)
    return (first + 4.0 * second) * (inverse * (1.0 / 12.0))


def write_tile(left, right, column_ref, tile_ref):
    points = left.shape[1]
    column_ref[:, 0:8] = jnp.transpose(jnp.concatenate([left, left, left, left], axis=0))
    right_east = right[0:1]
    right_north = right[1:2]

    def chunk(index, carry):
        rows = pl.ds(pl.multiple_of(index * ROWS, ROWS), ROWS)
        east = column_ref[rows, 0:1]
        north = column_ref[rows, 1:2]
        value = gaspari_cohn(east - right_east, north - right_north)
        tile_ref[rows, :] = value.astype(tile_ref.dtype)
        return carry

    lax.fori_loop(0, points // ROWS, chunk, 0, unroll=2)


def diag_kernel(ens_ref, inc_ref, coords_ref, out_ref, column_ref, tile_ref):
    members, levels, points = ens_ref.shape[1:]
    places = coords_ref[0].astype(jnp.float32)
    write_tile(places, places, column_ref, tile_ref)
    weighted = (ens_ref[0].astype(jnp.float32) * inc_ref[0].astype(jnp.float32)[None]).astype(jnp.bfloat16)
    field = jnp.dot(
        weighted.reshape(members * levels, points), tile_ref[...], preferred_element_type=jnp.float32
    ).reshape(members, levels, points)
    out_ref[0] = jnp.sum(ens_ref[0].astype(jnp.float32) * field, axis=0)


def diag(ensemble, increment, coords):
    blocks, members, levels, points = ensemble.shape
    return pl.pallas_call(
        diag_kernel,
        grid=(blocks,),
        in_specs=[
            pl.BlockSpec((1, members, levels, points), lambda b: (b, 0, 0, 0)),
            pl.BlockSpec((1, levels, points), lambda b: (b, 0, 0)),
            pl.BlockSpec((1, 2, points), lambda b: (b, 0, 0)),
        ],
        out_specs=pl.BlockSpec((1, levels, points), lambda b: (b, 0, 0)),
        out_shape=jax.ShapeDtypeStruct((blocks, levels, points), jnp.float32),
        scratch_shapes=[
            pltpu.VMEM((points, 128), jnp.float32),
            pltpu.VMEM((points, points), jnp.bfloat16),
        ],
        compiler_params=pltpu.CompilerParams(vmem_limit_bytes=16 * 1024 * 1024),
        cost_estimate=pl.CostEstimate(flops=24_000_000_000, bytes_accessed=8_000_000, transcendentals=0),
        name="diag",
    )(ensemble, increment, coords)


def tiles_kernel(pairs, count, small_ref, out_ref, column_ref):
    step = small_ref.shape[1] // 2
    group = out_ref.shape[0]
    base = pl.program_id(0) * group
    for within in range(group):

        @pl.when(base + within < count[0])
        def _():
            first = pairs[2 * (base + within)]
            second = pairs[2 * (base + within) + 1]
            left = small_ref[first, step : step + 2, :].astype(jnp.float32)
            right = small_ref[second, step : step + 2, :].astype(jnp.float32)
            write_tile(left, right, column_ref, out_ref.at[within])


def tiles(small, pairs, count):
    slot_total, rows, points = small.shape
    cap = pairs.shape[0] // 2
    return pl.pallas_call(
        tiles_kernel,
        grid_spec=pltpu.PrefetchScalarGridSpec(
            num_scalar_prefetch=2,
            grid=(cap // TILE_GROUP,),
            in_specs=[pl.BlockSpec((slot_total, rows, points), lambda i, p, c: (0, 0, 0))],
            out_specs=pl.BlockSpec((TILE_GROUP, points, points), lambda i, p, c: (i, 0, 0)),
            scratch_shapes=[pltpu.VMEM((points, 128), jnp.float32)],
        ),
        out_shape=jax.ShapeDtypeStruct((cap, points, points), jnp.bfloat16),
        compiler_params=pltpu.CompilerParams(vmem_limit_bytes=16 * 1024 * 1024),
        cost_estimate=pl.CostEstimate(flops=30_000_000_000, bytes_accessed=17_000_000, transcendentals=0),
        name="tiles",
    )(pairs, count, small)


def apply_kernel(pairs, count, ens_ref, small_ref, tiles_ref, out_ref, weighted_ref, field_ref):
    slot_total, rows, points = ens_ref.shape
    step = small_ref.shape[1] // 2
    members = rows // step
    group = tiles_ref.shape[0]
    turn = pl.program_id(0)

    @pl.when(turn == 0)
    def _():
        for slot in range(slot_total):
            gain = small_ref[slot, 0:step, :].astype(jnp.float32)
            block = ens_ref[slot].astype(jnp.float32).reshape(members, step, points)
            weighted_ref[slot] = (block * gain[None]).astype(jnp.bfloat16).reshape(rows, points)
            field_ref[slot] = jnp.zeros((rows, points), jnp.float32)

    def one(within, carry):
        first = pairs[2 * (turn * group + within)]
        second = pairs[2 * (turn * group + within) + 1]
        tile = tiles_ref[within]
        field_ref[first] += lax.dot_general(
            weighted_ref[second], tile, (((1,), (1,)), ((), ())), preferred_element_type=jnp.float32
        )
        field_ref[second] += jnp.dot(weighted_ref[first], tile, preferred_element_type=jnp.float32)
        return carry

    lax.fori_loop(0, jnp.clip(count[0] - turn * group, 0, group), one, 0)

    @pl.when(turn == pl.num_programs(0) - 1)
    def _():
        for slot in range(slot_total):
            product = ens_ref[slot].astype(jnp.float32) * field_ref[slot]
            out_ref[slot] = jnp.sum(product.reshape(members, step, points), axis=0)


def apply_pairs(ens, small, tile_stack, pairs, count):
    slot_total, rows, points = ens.shape
    cap = tile_stack.shape[0]
    step = small.shape[1] // 2
    return pl.pallas_call(
        apply_kernel,
        grid_spec=pltpu.PrefetchScalarGridSpec(
            num_scalar_prefetch=2,
            grid=(cap // TILE_GROUP,),
            in_specs=[
                pl.BlockSpec((slot_total, rows, points), lambda i, p, c: (0, 0, 0)),
                pl.BlockSpec((slot_total, 2 * step, points), lambda i, p, c: (0, 0, 0)),
                pl.BlockSpec((TILE_GROUP, points, points), lambda i, p, c: (i, 0, 0)),
            ],
            out_specs=pl.BlockSpec((slot_total, step, points), lambda i, p, c: (0, 0, 0)),
            scratch_shapes=[
                pltpu.VMEM((slot_total, rows, points), jnp.bfloat16),
                pltpu.VMEM((slot_total, rows, points), jnp.float32),
            ],
        ),
        out_shape=jax.ShapeDtypeStruct((slot_total, step, points), jnp.float32),
        compiler_params=pltpu.CompilerParams(vmem_limit_bytes=VMEM_CAP),
        cost_estimate=pl.CostEstimate(flops=9_000_000_000, bytes_accessed=22_000_000, transcendentals=0),
        name="apply",
    )(pairs, count, ens, small, tile_stack)


def finish_kernel(slots, own_ref, back_ref, out_ref, *, scale):
    out_ref[...] = own_ref[...] * scale
    for owner in range(back_ref.shape[0]):
        slot = slots[owner]
        out_ref[slot] = out_ref[slot] + back_ref[owner] * scale


def finish(own, back, slots, scale):
    return pl.pallas_call(
        functools.partial(finish_kernel, scale=scale),
        grid_spec=pltpu.PrefetchScalarGridSpec(
            num_scalar_prefetch=1,
            grid=(1,),
            in_specs=[
                pl.BlockSpec(own.shape, lambda i, s: (0, 0, 0)),
                pl.BlockSpec(back.shape, lambda i, s: (0, 0, 0)),
            ],
            out_specs=pl.BlockSpec(own.shape, lambda i, s: (0, 0, 0)),
        ),
        out_shape=jax.ShapeDtypeStruct(own.shape, jnp.float32),
        compiler_params=pltpu.CompilerParams(vmem_limit_bytes=16 * 1024 * 1024),
        name="finish",
    )(slots, own, back)


def per_device(ensemble, increment, coords, sent_slots, pair_list, pair_count):
    blocks, members, levels, points = ensemble.shape
    regions = lax.axis_size("region")
    groups = lax.axis_size("member")
    step = levels // groups
    slots = sent_slots.reshape(-1)
    pairs = pair_list.reshape(-1)
    own = lax.axis_index("member").reshape(1).astype(jnp.int32)
    big, small = pack(ensemble, increment, coords, slots, own, groups)
    got_small = lax.all_to_all(small, "region", 0, 0, tiled=True)
    got_big = lax.all_to_all(
        big.reshape(regions * groups, members * step, points), ("region", "member"), 0, 0, tiled=True
    ).reshape(regions, groups * members * step, points)
    diagonal = diag(ensemble, increment, coords)
    diagonal = lax.psum_scatter(diagonal, "member", scatter_dimension=1, tiled=True)
    tile_stack = tiles(got_small, pairs, pair_count)
    partial = apply_pairs(got_big, got_small, tile_stack, pairs, pair_count)
    back = lax.all_to_all(partial, "region", 0, 0, tiled=True)
    return finish(diagonal, back, slots, 1.0 / (members * groups - 1))


def solution(mesh):
    in_specs = (
        P("region", "member", None, None),
        P("region", None, None),
        P("region", None, None),
        P("region", None, None),
        P("region", None),
        P("region"),
    )
    out_specs = P("region", "member", None)
    return jax.shard_map(
        per_device, mesh=mesh, in_specs=in_specs, out_specs=out_specs, check_vma=False
    )
```

```python
import functools

import jax
import jax.numpy as jnp
from jax import lax
from jax.experimental import pallas as pl
from jax.experimental.pallas import tpu as pltpu
from jax.sharding import PartitionSpec as P

LANES = 128
TILE_GROUP = 4
DEPTH = 4
MIB = 1024 * 1024
UNIT = 12.0**-0.2
UNIT2 = UNIT * UNIT
LEAST = UNIT2 * 2.0**-12


def select_kernel(slots, coords_ref, places_ref, sem):
    total = places_ref.shape[0]

    def copy(owner):
        return pltpu.make_async_copy(coords_ref.at[slots[owner]], places_ref.at[owner], sem.at[owner])

    for owner in range(total):
        copy(owner).start()
    for owner in range(total):
        copy(owner).wait()


def select(coords, slots):
    total = slots.shape[0]
    return pl.pallas_call(
        select_kernel,
        in_specs=[pl.BlockSpec(memory_space=pltpu.SMEM), pl.BlockSpec(memory_space=pl.ANY)],
        out_specs=pl.BlockSpec(memory_space=pl.ANY),
        out_shape=jax.ShapeDtypeStruct((total, *coords.shape[1:]), coords.dtype),
        scratch_shapes=[pltpu.SemaphoreType.DMA((total,))],
        compiler_params=pltpu.CompilerParams(vmem_limit_bytes=60 * MIB),
        name="select",
    )(slots, coords)


def pack_kernel(slots, own, ens_ref, inc_ref, big_ref, ens_buf, inc_buf, out_buf, in_sem, inc_sem, out_sem):
    total, members, levels, points = ens_buf.shape
    parts = out_buf.shape[1]
    step = levels // parts
    lane_chunks = points // LANES

    def ens_copy(owner):
        return pltpu.make_async_copy(ens_ref.at[slots[owner]], ens_buf.at[owner], in_sem.at[owner])

    def inc_copy(owner):
        return pltpu.make_async_copy(inc_ref.at[slots[owner]], inc_buf.at[owner], inc_sem.at[owner])

    def out_copy(owner):
        return pltpu.make_async_copy(out_buf.at[owner], big_ref.at[owner], out_sem.at[owner])

    for owner in range(total):
        ens_copy(owner).start()
        inc_copy(owner).start()
    chunk = pl.multiple_of(lax.rem(own[0], lane_chunks) * LANES, LANES)
    for owner in range(total):
        ens_copy(owner).wait()
        inc_copy(owner).wait()
        for part in range(parts):
            here = slice(part * step, (part + 1) * step)
            for lane in range(lane_chunks):
                out_buf[owner, part, lane * members * step : (lane + 1) * members * step, :] = ens_buf[
                    owner, :, here, lane * LANES : (lane + 1) * LANES
                ].reshape(members * step, LANES)
            out_buf[owner, part, members * step * lane_chunks :, :] = inc_buf[owner, here, pl.ds(chunk, LANES)]
        out_copy(owner).start()
    for owner in range(total):
        out_copy(owner).wait()


def pack(ensemble, increment, slots, own, parts):
    blocks, members, levels, points = ensemble.shape
    total = slots.shape[0]
    step = levels // parts
    rows = members * step * (points // LANES) + step
    return pl.pallas_call(
        pack_kernel,
        in_specs=[
            pl.BlockSpec(memory_space=pltpu.SMEM),
            pl.BlockSpec(memory_space=pltpu.SMEM),
            pl.BlockSpec(memory_space=pl.ANY),
            pl.BlockSpec(memory_space=pl.ANY),
        ],
        out_specs=pl.BlockSpec(memory_space=pl.ANY),
        out_shape=jax.ShapeDtypeStruct((total, parts, rows, LANES), ensemble.dtype),
        scratch_shapes=[
            pltpu.VMEM((total, members, levels, points), ensemble.dtype),
            pltpu.VMEM((total, levels, points), increment.dtype),
            pltpu.VMEM((total, parts, rows, LANES), ensemble.dtype),
            pltpu.SemaphoreType.DMA((total,)),
            pltpu.SemaphoreType.DMA((total,)),
            pltpu.SemaphoreType.DMA((total,)),
        ],
        compiler_params=pltpu.CompilerParams(vmem_limit_bytes=60 * MIB),
        name="pack",
    )(slots, own, ensemble, increment)


def three_parts(value):
    first = value.astype(jnp.bfloat16).astype(jnp.float32)
    rest = value - first
    second = rest.astype(jnp.bfloat16).astype(jnp.float32)
    return [first, second, rest - second]


def left_rows(places):
    east, north = places[0:1], places[1:2]
    one = jnp.ones_like(east)
    norm = UNIT2 * (east * east + north * north)
    rows = three_parts((-2.0 * UNIT2) * east) + three_parts((-2.0 * UNIT2) * north) + three_parts(norm)
    rows = rows + [one] * 3 + [jnp.zeros_like(east)] * 4
    return jnp.concatenate(rows, axis=0).astype(jnp.bfloat16)


def right_rows(places):
    east, north = places[0:1], places[1:2]
    one = jnp.ones_like(east)
    norm = UNIT2 * (east * east + north * north)
    rows = [east] * 3 + [north] * 3 + [one] * 3 + three_parts(norm) + [jnp.zeros_like(east)] * 4
    return jnp.concatenate(rows, axis=0).astype(jnp.bfloat16)


def tile_of(left, right):
    squared = lax.dot_general(left, right, (((0,), (0,)), ((), ())), preferred_element_type=jnp.float32)
    squared = jnp.maximum(squared, LEAST)
    inverse = lax.rsqrt(squared)
    z = squared * inverse
    outer = jnp.maximum(2.0 * UNIT - z, 0.0)
    inner = jnp.maximum(UNIT - z, 0.0)
    outer2 = outer * outer
    inner2 = inner * inner
    shifted = z + 2.0 * UNIT
    first = (outer2 * outer2) * (z * shifted - 0.5 * UNIT2)
    second = (inner2 * inner2) * (inner * shifted)
    return ((first + 4.0 * second) * inverse).astype(jnp.bfloat16)


def diag_kernel(ens_ref, inc_ref, coords_ref, out_ref):
    members, levels, points = ens_ref.shape[1:]
    rows = members * levels
    half = points // 2
    places = coords_ref[0].astype(jnp.float32)
    left, right = left_rows(places), right_rows(places)
    upper = tile_of(left[:, :half], right)
    lower = tile_of(left[:, half:], right[:, half:])
    weighted = (ens_ref[0] * inc_ref[0][None]).reshape(rows, points)
    near, far = weighted[:, :half], weighted[:, half:]
    field_near = jnp.dot(near, upper[:, :half], preferred_element_type=jnp.float32) + lax.dot_general(
        far, upper[:, half:], (((1,), (1,)), ((), ())), preferred_element_type=jnp.float32
    )
    field_far = jnp.dot(near, upper[:, half:], preferred_element_type=jnp.float32) + jnp.dot(
        far, lower, preferred_element_type=jnp.float32
    )
    block = ens_ref[0].astype(jnp.float32)
    out_ref[0, :, :half] = jnp.sum(block[:, :, :half] * field_near.reshape(members, levels, half), axis=0)
    out_ref[0, :, half:] = jnp.sum(block[:, :, half:] * field_far.reshape(members, levels, half), axis=0)


def diag(ensemble, increment, coords):
    blocks, members, levels, points = ensemble.shape
    return pl.pallas_call(
        diag_kernel,
        grid=(blocks,),
        in_specs=[
            pl.BlockSpec((1, members, levels, points), lambda b: (b, 0, 0, 0)),
            pl.BlockSpec((1, levels, points), lambda b: (b, 0, 0)),
            pl.BlockSpec((1, 2, points), lambda b: (b, 0, 0)),
        ],
        out_specs=pl.BlockSpec((1, levels, points), lambda b: (b, 0, 0)),
        out_shape=jax.ShapeDtypeStruct((blocks, levels, points), jnp.float32),
        compiler_params=pltpu.CompilerParams(vmem_limit_bytes=16 * MIB),
        cost_estimate=pl.CostEstimate(flops=20_000_000_000, bytes_accessed=8_000_000, transcendentals=0),
        name="diag",
    )(ensemble, increment, coords)


def tiles_kernel(pairs, count, places_ref, out_ref):
    group = out_ref.shape[0]
    base = pl.program_id(0) * group

    def one(within, carry):
        pair = 2 * (base + within)
        left = left_rows(places_ref[pairs[pair]].astype(jnp.float32))
        right = right_rows(places_ref[pairs[pair + 1]].astype(jnp.float32))
        out_ref[within] = tile_of(left, right)
        return carry

    lax.fori_loop(0, jnp.clip(count[0] - base, 0, group), one, 0)


def tiles(places, pairs, count):
    slot_total, _, points = places.shape
    cap = pairs.shape[0] // 2
    return pl.pallas_call(
        tiles_kernel,
        grid_spec=pltpu.PrefetchScalarGridSpec(
            num_scalar_prefetch=2,
            grid=(cap // TILE_GROUP,),
            in_specs=[pl.BlockSpec((slot_total, 2, points), lambda i, p, c: (0, 0, 0))],
            out_specs=pl.BlockSpec((TILE_GROUP, points, points), lambda i, p, c: (i, 0, 0)),
        ),
        out_shape=jax.ShapeDtypeStruct((cap, points, points), jnp.bfloat16),
        compiler_params=pltpu.CompilerParams(vmem_limit_bytes=60 * MIB),
        cost_estimate=pl.CostEstimate(flops=30_000_000_000, bytes_accessed=17_000_000, transcendentals=0),
        name="tiles",
    )(pairs, count, places)


def apply_kernel(
    pairs, count, got_ref, tiles_ref, out_ref, ens_ref, inc_ref, weighted_ref, field_ref, ring_ref, ens_sem, inc_sem, ring_sem
):
    slot_total, sources, rows, points = ens_ref.shape
    step = inc_ref.shape[2]
    lane_chunks = points // LANES
    every = sources * rows

    def ens_copies(slot):
        return [
            pltpu.make_async_copy(
                got_ref.at[slot, :, lane * rows : (lane + 1) * rows, :],
                ens_ref.at[slot, :, :, lane * LANES : (lane + 1) * LANES],
                ens_sem.at[slot, lane],
            )
            for lane in range(lane_chunks)
        ]

    inc_copy = pltpu.make_async_copy(got_ref.at[:, :lane_chunks, rows * lane_chunks :, :], inc_ref, inc_sem)
    inc_copy.start()
    for slot in range(slot_total):
        for copy in ens_copies(slot):
            copy.start()
    def ring_copy(index):
        place = lax.rem(index, DEPTH)
        return pltpu.make_async_copy(tiles_ref.at[index], ring_ref.at[place], ring_sem.at[place])

    for index in range(DEPTH):

        @pl.when(index < count[0])
        def _():
            ring_copy(index).start()

    inc_copy.wait()
    for slot in range(slot_total):
        field_ref[slot] = jnp.zeros((every, points), jnp.float32)
        for copy in ens_copies(slot):
            copy.wait()
        for lane in range(lane_chunks):
            here = slice(lane * LANES, (lane + 1) * LANES)
            gain = inc_ref[slot, lane]
            block = ens_ref[slot, :, :, here].reshape(every // step, step, LANES)
            weighted_ref[slot, :, here] = (block * gain[None]).reshape(every, LANES)

    def one(index, carry):
        first = pairs[2 * index]
        second = pairs[2 * index + 1]
        ring_copy(index).wait()
        tile = ring_ref[lax.rem(index, DEPTH)]
        field_ref[first] += lax.dot_general(
            weighted_ref[second], tile, (((1,), (1,)), ((), ())), preferred_element_type=jnp.float32
        )
        field_ref[second] += jnp.dot(weighted_ref[first], tile, preferred_element_type=jnp.float32)

        @pl.when(index + DEPTH < count[0])
        def _():
            ring_copy(index + DEPTH).start()

        return carry

    lax.fori_loop(0, count[0], one, 0)

    for slot in range(slot_total):
        product = ens_ref[slot].reshape(every, points).astype(jnp.float32) * field_ref[slot]
        out_ref[slot] = jnp.sum(product.reshape(every // step, step, points), axis=0)


def apply_pairs(got, tile_stack, pairs, count, members, step):
    slot_total, sources, rows, _ = got.shape
    cap, points, _ = tile_stack.shape
    lane_chunks = points // LANES
    every = sources * members * step
    return pl.pallas_call(
        apply_kernel,
        in_specs=[
            pl.BlockSpec(memory_space=pltpu.SMEM),
            pl.BlockSpec(memory_space=pltpu.SMEM),
            pl.BlockSpec(memory_space=pl.ANY),
            pl.BlockSpec(memory_space=pl.ANY),
        ],
        out_specs=pl.BlockSpec(memory_space=pltpu.VMEM),
        scratch_shapes=[
            pltpu.VMEM((slot_total, sources, members * step, points), jnp.bfloat16),
            pltpu.VMEM((slot_total, lane_chunks, step, LANES), jnp.bfloat16),
            pltpu.VMEM((slot_total, every, points), jnp.bfloat16),
            pltpu.VMEM((slot_total, every, points), jnp.float32),
            pltpu.VMEM((DEPTH, points, points), jnp.bfloat16),
            pltpu.SemaphoreType.DMA((slot_total, lane_chunks)),
            pltpu.SemaphoreType.DMA,
            pltpu.SemaphoreType.DMA((DEPTH,)),
        ],
        out_shape=jax.ShapeDtypeStruct((slot_total, step, points), jnp.float32),
        compiler_params=pltpu.CompilerParams(vmem_limit_bytes=60 * MIB),
        cost_estimate=pl.CostEstimate(flops=9_000_000_000, bytes_accessed=22_000_000, transcendentals=0),
        name="apply",
    )(pairs, count, got, tile_stack)


def finish_kernel(slots, own_ref, back_ref, out_ref, *, scale):
    out_ref[...] = own_ref[...] * scale
    for owner in range(back_ref.shape[0]):
        slot = slots[owner]
        out_ref[slot] = out_ref[slot] + back_ref[owner] * scale


def finish(own, back, slots, scale):
    return pl.pallas_call(
        functools.partial(finish_kernel, scale=scale),
        in_specs=[
            pl.BlockSpec(memory_space=pltpu.SMEM),
            pl.BlockSpec(memory_space=pltpu.VMEM),
            pl.BlockSpec(memory_space=pltpu.VMEM),
        ],
        out_specs=pl.BlockSpec(memory_space=pltpu.VMEM),
        out_shape=jax.ShapeDtypeStruct(own.shape, jnp.float32),
        compiler_params=pltpu.CompilerParams(vmem_limit_bytes=16 * MIB),
        name="finish",
    )(slots, own, back)


def per_device(ensemble, increment, coords, sent_slots, pair_list, pair_count):
    blocks, members, levels, points = ensemble.shape
    regions = lax.axis_size("region")
    groups = lax.axis_size("member")
    step = levels // groups
    slots = sent_slots.reshape(-1)
    pairs = pair_list.reshape(-1)
    own = lax.axis_index("member").reshape(1).astype(jnp.int32)
    places = select(coords, slots)
    own_places = lax.all_to_all(places, "region", 0, 0, tiled=True)
    big = pack(ensemble, increment, slots, own, groups)
    got = lax.all_to_all(
        big.reshape(regions * groups, -1, LANES), ("region", "member"), 0, 0, tiled=True
    ).reshape(regions, groups, -1, LANES)
    diagonal = diag(ensemble, increment, coords)
    diagonal = lax.psum_scatter(diagonal, "member", scatter_dimension=1, tiled=True)
    tile_stack = tiles(own_places, pairs, pair_count)
    partial = apply_pairs(got, tile_stack, pairs, pair_count, members, step)
    back = lax.all_to_all(partial, "region", 0, 0, tiled=True)
    return finish(diagonal, back, slots, 1.0 / (members * groups - 1))


def solution(mesh):
    in_specs = (
        P("region", "member", None, None),
        P("region", None, None),
        P("region", None, None),
        P("region", None, None),
        P("region", None),
        P("region"),
    )
    out_specs = P("region", "member", None)
    return jax.shard_map(
        per_device, mesh=mesh, in_specs=in_specs, out_specs=out_specs, check_vma=False
    )
```

```python
import functools

import jax
import jax.numpy as jnp
from jax import lax
from jax.experimental import pallas as pl
from jax.experimental.pallas import tpu as pltpu
from jax.sharding import PartitionSpec as P

LANES = 128
TILE_GROUP = 4
MIB = 1024 * 1024
UNIT = 12.0**-0.2
UNIT2 = UNIT * UNIT
LEAST = UNIT2 * 2.0**-12


def select_kernel(slots, coords_ref, places_ref, sem):
    total = places_ref.shape[0]

    def copy(owner):
        return pltpu.make_async_copy(coords_ref.at[slots[owner]], places_ref.at[owner], sem.at[owner])

    for owner in range(total):
        copy(owner).start()
    for owner in range(total):
        copy(owner).wait()


def select(coords, slots):
    total = slots.shape[0]
    return pl.pallas_call(
        select_kernel,
        in_specs=[pl.BlockSpec(memory_space=pltpu.SMEM), pl.BlockSpec(memory_space=pl.ANY)],
        out_specs=pl.BlockSpec(memory_space=pl.ANY),
        out_shape=jax.ShapeDtypeStruct((total, *coords.shape[1:]), coords.dtype),
        scratch_shapes=[pltpu.SemaphoreType.DMA((total,))],
        compiler_params=pltpu.CompilerParams(vmem_limit_bytes=60 * MIB),
        name="select",
    )(slots, coords)


def pack_kernel(slots, own, ens_ref, inc_ref, big_ref, ens_buf, inc_buf, out_buf, in_sem, inc_sem, out_sem):
    total, members, levels, points = ens_buf.shape
    parts = out_buf.shape[1]
    step = levels // parts
    lane_chunks = points // LANES

    def ens_copy(owner):
        return pltpu.make_async_copy(ens_ref.at[slots[owner]], ens_buf.at[owner], in_sem.at[owner])

    def inc_copy(owner):
        return pltpu.make_async_copy(inc_ref.at[slots[owner]], inc_buf.at[owner], inc_sem.at[owner])

    def out_copy(owner):
        return pltpu.make_async_copy(out_buf.at[owner], big_ref.at[owner], out_sem.at[owner])

    for owner in range(total):
        ens_copy(owner).start()
        inc_copy(owner).start()
    chunk = pl.multiple_of(lax.rem(own[0], lane_chunks) * LANES, LANES)
    for owner in range(total):
        ens_copy(owner).wait()
        inc_copy(owner).wait()
        for part in range(parts):
            here = slice(part * step, (part + 1) * step)
            for lane in range(lane_chunks):
                out_buf[owner, part, lane * members * step : (lane + 1) * members * step, :] = ens_buf[
                    owner, :, here, lane * LANES : (lane + 1) * LANES
                ].reshape(members * step, LANES)
            out_buf[owner, part, members * step * lane_chunks :, :] = inc_buf[owner, here, pl.ds(chunk, LANES)]
        out_copy(owner).start()
    for owner in range(total):
        out_copy(owner).wait()


def pack(ensemble, increment, slots, own, parts):
    blocks, members, levels, points = ensemble.shape
    total = slots.shape[0]
    step = levels // parts
    rows = members * step * (points // LANES) + step
    return pl.pallas_call(
        pack_kernel,
        in_specs=[
            pl.BlockSpec(memory_space=pltpu.SMEM),
            pl.BlockSpec(memory_space=pltpu.SMEM),
            pl.BlockSpec(memory_space=pl.ANY),
            pl.BlockSpec(memory_space=pl.ANY),
        ],
        out_specs=pl.BlockSpec(memory_space=pl.ANY),
        out_shape=jax.ShapeDtypeStruct((total, parts, rows, LANES), ensemble.dtype),
        scratch_shapes=[
            pltpu.VMEM((total, members, levels, points), ensemble.dtype),
            pltpu.VMEM((total, levels, points), increment.dtype),
            pltpu.VMEM((total, parts, rows, LANES), ensemble.dtype),
            pltpu.SemaphoreType.DMA((total,)),
            pltpu.SemaphoreType.DMA((total,)),
            pltpu.SemaphoreType.DMA((total,)),
        ],
        compiler_params=pltpu.CompilerParams(vmem_limit_bytes=60 * MIB),
        name="pack",
    )(slots, own, ensemble, increment)


def three_parts(value):
    first = value.astype(jnp.bfloat16).astype(jnp.float32)
    rest = value - first
    second = rest.astype(jnp.bfloat16).astype(jnp.float32)
    return [first, second, rest - second]


def left_rows(places):
    east, north = places[0:1], places[1:2]
    one = jnp.ones_like(east)
    norm = UNIT2 * (east * east + north * north)
    rows = three_parts((-2.0 * UNIT2) * east) + three_parts((-2.0 * UNIT2) * north) + three_parts(norm)
    rows = rows + [one] * 3 + [jnp.zeros_like(east)] * 4
    return jnp.concatenate(rows, axis=0).astype(jnp.bfloat16)


def right_rows(places):
    east, north = places[0:1], places[1:2]
    one = jnp.ones_like(east)
    norm = UNIT2 * (east * east + north * north)
    rows = [east] * 3 + [north] * 3 + [one] * 3 + three_parts(norm) + [jnp.zeros_like(east)] * 4
    return jnp.concatenate(rows, axis=0).astype(jnp.bfloat16)


def tile_of(left, right):
    squared = lax.dot_general(left, right, (((0,), (0,)), ((), ())), preferred_element_type=jnp.float32)
    squared = jnp.maximum(squared, LEAST)
    inverse = lax.rsqrt(squared)
    z = squared * inverse
    outer = jnp.maximum(2.0 * UNIT - z, 0.0)
    inner = jnp.maximum(UNIT - z, 0.0)
    outer2 = outer * outer
    inner2 = inner * inner
    shifted = z + 2.0 * UNIT
    first = (outer2 * outer2) * (z * shifted - 0.5 * UNIT2)
    second = (inner2 * inner2) * (inner * shifted)
    return ((first + 4.0 * second) * inverse).astype(jnp.bfloat16)


def diag_kernel(ens_ref, inc_ref, coords_ref, out_ref):
    members, levels, points = ens_ref.shape[1:]
    parts, _, step, _ = out_ref.shape
    rows = members * levels
    half = points // 2
    places = coords_ref[0].astype(jnp.float32)
    left, right = left_rows(places), right_rows(places)
    upper = tile_of(left[:, :half], right)
    lower = tile_of(left[:, half:], right[:, half:])
    weighted = (ens_ref[0] * inc_ref[0][None]).reshape(rows, points)
    near, far = weighted[:, :half], weighted[:, half:]
    field_near = jnp.dot(near, upper[:, :half], preferred_element_type=jnp.float32) + lax.dot_general(
        far, upper[:, half:], (((1,), (1,)), ((), ())), preferred_element_type=jnp.float32
    )
    field_far = jnp.dot(near, upper[:, half:], preferred_element_type=jnp.float32) + jnp.dot(
        far, lower, preferred_element_type=jnp.float32
    )
    block = ens_ref[0].astype(jnp.float32)
    sum_near = jnp.sum(block[:, :, :half] * field_near.reshape(members, levels, half), axis=0)
    sum_far = jnp.sum(block[:, :, half:] * field_far.reshape(members, levels, half), axis=0)
    out_ref[:, 0, :, :half] = sum_near.reshape(parts, step, half).astype(out_ref.dtype)
    out_ref[:, 0, :, half:] = sum_far.reshape(parts, step, half).astype(out_ref.dtype)


def diag(ensemble, increment, coords, parts):
    blocks, members, levels, points = ensemble.shape
    step = levels // parts
    return pl.pallas_call(
        diag_kernel,
        grid=(blocks,),
        in_specs=[
            pl.BlockSpec((1, members, levels, points), lambda b: (b, 0, 0, 0)),
            pl.BlockSpec((1, levels, points), lambda b: (b, 0, 0)),
            pl.BlockSpec((1, 2, points), lambda b: (b, 0, 0)),
        ],
        out_specs=pl.BlockSpec((parts, 1, step, points), lambda b: (0, b, 0, 0)),
        out_shape=jax.ShapeDtypeStruct((parts, blocks, step, points), jnp.bfloat16),
        compiler_params=pltpu.CompilerParams(vmem_limit_bytes=24 * MIB),
        cost_estimate=pl.CostEstimate(flops=20_000_000_000, bytes_accessed=8_000_000, transcendentals=0),
        name="diag",
    )(ensemble, increment, coords)


def tiles_kernel(pairs, places_ref, out_ref):
    first = pl.program_id(0) * TILE_GROUP
    for within in range(TILE_GROUP):
        pair = 2 * (first + within)
        left = left_rows(places_ref[pairs[pair]].astype(jnp.float32))
        right = right_rows(places_ref[pairs[pair + 1]].astype(jnp.float32))
        out_ref[within] = tile_of(left, right)


def tiles(places, pairs):
    slot_total, _, points = places.shape
    cap = pairs.shape[0] // 2
    return pl.pallas_call(
        tiles_kernel,
        grid_spec=pltpu.PrefetchScalarGridSpec(
            num_scalar_prefetch=1,
            grid=(cap // TILE_GROUP,),
            in_specs=[pl.BlockSpec((slot_total, 2, points), lambda i, p: (0, 0, 0))],
            out_specs=pl.BlockSpec((TILE_GROUP, points, points), lambda i, p: (i, 0, 0)),
        ),
        out_shape=jax.ShapeDtypeStruct((cap, points, points), jnp.bfloat16),
        compiler_params=pltpu.CompilerParams(vmem_limit_bytes=60 * MIB),
        cost_estimate=pl.CostEstimate(flops=30_000_000_000, bytes_accessed=17_000_000, transcendentals=0),
        name="tiles",
    )(pairs, places)


def apply_kernel(
    pairs, count, got_ref, stack_ref, out_ref,
    ens_ref, inc_ref, weighted_ref, field_ref, tiles_ref, ens_sem, inc_sem, tiles_sem,
):
    slot_total, sources, rows, points = ens_ref.shape
    step = inc_ref.shape[2]
    lane_chunks = points // LANES
    every = sources * rows

    def ens_copies(slot):
        return [
            pltpu.make_async_copy(
                got_ref.at[slot, :, lane * rows : (lane + 1) * rows, :],
                ens_ref.at[slot, :, :, lane * LANES : (lane + 1) * LANES],
                ens_sem.at[slot, lane],
            )
            for lane in range(lane_chunks)
        ]

    inc_copy = pltpu.make_async_copy(got_ref.at[:, :lane_chunks, rows * lane_chunks :, :], inc_ref, inc_sem)

    def tile_copy(index):
        return pltpu.make_async_copy(stack_ref.at[index], tiles_ref.at[index], tiles_sem.at[index])

    inc_copy.start()
    for slot in range(slot_total):
        for copy in ens_copies(slot):
            copy.start()
    for index in range(tiles_ref.shape[0]):
        tile_copy(index).start()
    inc_copy.wait()
    for slot in range(slot_total):
        field_ref[slot] = jnp.zeros((every, points), jnp.float32)
        for copy in ens_copies(slot):
            copy.wait()
        for lane in range(lane_chunks):
            here = slice(lane * LANES, (lane + 1) * LANES)
            gain = inc_ref[slot, lane]
            block = ens_ref[slot, :, :, here].reshape(every // step, step, LANES)
            weighted_ref[slot, :, here] = (block * gain[None]).reshape(every, LANES)

    def one(index, carry):
        first = pairs[2 * index]
        second = pairs[2 * index + 1]
        tile_copy(index).wait()
        tile = tiles_ref[index]
        to_first = lax.dot_general(
            weighted_ref[second], tile, (((1,), (1,)), ((), ())), preferred_element_type=jnp.float32
        )
        to_second = jnp.dot(weighted_ref[first], tile, preferred_element_type=jnp.float32)
        field_ref[first] += to_first
        field_ref[second] += to_second
        return carry

    def skip(index, carry):
        tile_copy(index).wait()
        return carry

    lax.fori_loop(0, count[0], one, 0)
    lax.fori_loop(count[0], tiles_ref.shape[0], skip, 0)

    for slot in range(slot_total):
        product = ens_ref[slot].reshape(every, points).astype(jnp.float32) * field_ref[slot]
        out_ref[slot] = jnp.sum(product.reshape(every // step, step, points), axis=0)


def apply_pairs(got, tile_stack, pairs, count, members, step):
    slot_total, sources, rows, _ = got.shape
    points = tile_stack.shape[2]
    lane_chunks = points // LANES
    every = sources * members * step
    return pl.pallas_call(
        apply_kernel,
        in_specs=[
            pl.BlockSpec(memory_space=pltpu.SMEM),
            pl.BlockSpec(memory_space=pltpu.SMEM),
            pl.BlockSpec(memory_space=pl.ANY),
            pl.BlockSpec(memory_space=pl.ANY),
        ],
        out_specs=pl.BlockSpec(memory_space=pltpu.VMEM),
        scratch_shapes=[
            pltpu.VMEM((slot_total, sources, members * step, points), jnp.bfloat16),
            pltpu.VMEM((slot_total, lane_chunks, step, LANES), jnp.bfloat16),
            pltpu.VMEM((slot_total, every, points), jnp.bfloat16),
            pltpu.VMEM((slot_total, every, points), jnp.float32),
            pltpu.VMEM(tile_stack.shape, jnp.bfloat16),
            pltpu.SemaphoreType.DMA((slot_total, lane_chunks)),
            pltpu.SemaphoreType.DMA,
            pltpu.SemaphoreType.DMA((tile_stack.shape[0],)),
        ],
        out_shape=jax.ShapeDtypeStruct((slot_total, step, points), jnp.float32),
        compiler_params=pltpu.CompilerParams(vmem_limit_bytes=60 * MIB),
        cost_estimate=pl.CostEstimate(flops=9_000_000_000, bytes_accessed=22_000_000, transcendentals=0),
        name="apply",
    )(pairs, count, got, tile_stack)


def finish_kernel(slots, parts_ref, back_ref, out_ref, *, scale):
    out_ref[...] = jnp.sum(parts_ref[...].astype(jnp.float32), axis=0) * scale
    for owner in range(back_ref.shape[0]):
        slot = slots[owner]
        out_ref[slot] = out_ref[slot] + back_ref[owner] * scale


def finish(parts, back, slots, scale):
    return pl.pallas_call(
        functools.partial(finish_kernel, scale=scale),
        in_specs=[
            pl.BlockSpec(memory_space=pltpu.SMEM),
            pl.BlockSpec(memory_space=pltpu.VMEM),
            pl.BlockSpec(memory_space=pltpu.VMEM),
        ],
        out_specs=pl.BlockSpec(memory_space=pltpu.VMEM),
        out_shape=jax.ShapeDtypeStruct(parts.shape[1:], jnp.float32),
        compiler_params=pltpu.CompilerParams(vmem_limit_bytes=16 * MIB),
        name="finish",
    )(slots, parts, back)


def per_device(ensemble, increment, coords, sent_slots, pair_list, pair_count):
    blocks, members, levels, points = ensemble.shape
    regions = lax.axis_size("region")
    groups = lax.axis_size("member")
    step = levels // groups
    slots = sent_slots.reshape(-1)
    pairs = pair_list.reshape(-1)
    own = lax.axis_index("member").reshape(1).astype(jnp.int32)
    places = select(coords, slots)
    own_places = lax.all_to_all(places, "region", 0, 0, tiled=True)
    big = pack(ensemble, increment, slots, own, groups)
    big, own_places = lax.optimization_barrier((big, own_places))
    got = lax.all_to_all(
        big.reshape(regions * groups, -1, LANES), ("region", "member"), 0, 0, tiled=True
    ).reshape(regions, groups, -1, LANES)
    diagonal = diag(ensemble, increment, coords, groups)
    tile_stack = tiles(own_places, pairs)
    got, diagonal, tile_stack = lax.optimization_barrier((got, diagonal, tile_stack))
    parts = lax.all_to_all(diagonal, "member", 0, 0, tiled=True)
    partial = apply_pairs(got, tile_stack, pairs, pair_count, members, step)
    partial, parts = lax.optimization_barrier((partial, parts))
    back = lax.all_to_all(partial, "region", 0, 0, tiled=True)
    return finish(parts, back, slots, 1.0 / (members * groups - 1))


def solution(mesh):
    in_specs = (
        P("region", "member", None, None),
        P("region", None, None),
        P("region", None, None),
        P("region", None, None),
        P("region", None),
        P("region"),
    )
    out_specs = P("region", "member", None)
    return jax.shard_map(
        per_device, mesh=mesh, in_specs=in_specs, out_specs=out_specs, check_vma=False
    )
```

```python
import functools

import jax
import jax.numpy as jnp
from jax import lax
from jax.experimental import pallas as pl
from jax.experimental.pallas import tpu as pltpu
from jax.sharding import PartitionSpec as P

LANES = 128
TILE_GROUP = 4
PAIR_GROUP = 4
MIB = 1024 * 1024
UNIT = 12.0**-0.2
UNIT2 = UNIT * UNIT
LEAST = UNIT2 * 2.0**-12


def select_kernel(slots, coords_ref, places_ref, sem):
    total = places_ref.shape[0]

    def copy(owner):
        return pltpu.make_async_copy(coords_ref.at[slots[owner]], places_ref.at[owner], sem.at[owner])

    for owner in range(total):
        copy(owner).start()
    for owner in range(total):
        copy(owner).wait()


def select(coords, slots):
    total = slots.shape[0]
    return pl.pallas_call(
        select_kernel,
        in_specs=[pl.BlockSpec(memory_space=pltpu.SMEM), pl.BlockSpec(memory_space=pl.ANY)],
        out_specs=pl.BlockSpec(memory_space=pl.ANY),
        out_shape=jax.ShapeDtypeStruct((total, *coords.shape[1:]), coords.dtype),
        scratch_shapes=[pltpu.SemaphoreType.DMA((total,))],
        compiler_params=pltpu.CompilerParams(vmem_limit_bytes=60 * MIB),
        name="select",
    )(slots, coords)


def pack_kernel(slots, own, ens_ref, inc_ref, big_ref, ens_buf, inc_buf, out_buf, in_sem, inc_sem, out_sem):
    total, members, levels, points = ens_buf.shape
    parts = out_buf.shape[1]
    step = levels // parts
    lane_chunks = points // LANES

    def ens_copy(owner):
        return pltpu.make_async_copy(ens_ref.at[slots[owner]], ens_buf.at[owner], in_sem.at[owner])

    def inc_copy(owner):
        return pltpu.make_async_copy(inc_ref.at[slots[owner]], inc_buf.at[owner], inc_sem.at[owner])

    def out_copy(owner):
        return pltpu.make_async_copy(out_buf.at[owner], big_ref.at[owner], out_sem.at[owner])

    for owner in range(total):
        ens_copy(owner).start()
        inc_copy(owner).start()
    chunk = pl.multiple_of(lax.rem(own[0], lane_chunks) * LANES, LANES)
    for owner in range(total):
        ens_copy(owner).wait()
        inc_copy(owner).wait()
        for part in range(parts):
            here = slice(part * step, (part + 1) * step)
            for lane in range(lane_chunks):
                out_buf[owner, part, lane * members * step : (lane + 1) * members * step, :] = ens_buf[
                    owner, :, here, lane * LANES : (lane + 1) * LANES
                ].reshape(members * step, LANES)
            out_buf[owner, part, members * step * lane_chunks :, :] = inc_buf[owner, here, pl.ds(chunk, LANES)]
        out_copy(owner).start()
    for owner in range(total):
        out_copy(owner).wait()


def pack(ensemble, increment, slots, own, parts):
    blocks, members, levels, points = ensemble.shape
    total = slots.shape[0]
    step = levels // parts
    rows = members * step * (points // LANES) + step
    return pl.pallas_call(
        pack_kernel,
        in_specs=[
            pl.BlockSpec(memory_space=pltpu.SMEM),
            pl.BlockSpec(memory_space=pltpu.SMEM),
            pl.BlockSpec(memory_space=pl.ANY),
            pl.BlockSpec(memory_space=pl.ANY),
        ],
        out_specs=pl.BlockSpec(memory_space=pl.ANY),
        out_shape=jax.ShapeDtypeStruct((total, parts, rows, LANES), ensemble.dtype),
        scratch_shapes=[
            pltpu.VMEM((total, members, levels, points), ensemble.dtype),
            pltpu.VMEM((total, levels, points), increment.dtype),
            pltpu.VMEM((total, parts, rows, LANES), ensemble.dtype),
            pltpu.SemaphoreType.DMA((total,)),
            pltpu.SemaphoreType.DMA((total,)),
            pltpu.SemaphoreType.DMA((total,)),
        ],
        compiler_params=pltpu.CompilerParams(vmem_limit_bytes=60 * MIB),
        name="pack",
    )(slots, own, ensemble, increment)


def three_parts(value):
    first = value.astype(jnp.bfloat16).astype(jnp.float32)
    rest = value - first
    second = rest.astype(jnp.bfloat16).astype(jnp.float32)
    return [first, second, rest - second]


def left_rows(places):
    east, north = places[0:1], places[1:2]
    one = jnp.ones_like(east)
    norm = UNIT2 * (east * east + north * north)
    rows = three_parts((-2.0 * UNIT2) * east) + three_parts((-2.0 * UNIT2) * north) + three_parts(norm)
    rows = rows + [one] * 3 + [jnp.zeros_like(east)] * 4
    return jnp.concatenate(rows, axis=0).astype(jnp.bfloat16)


def right_rows(places):
    east, north = places[0:1], places[1:2]
    one = jnp.ones_like(east)
    norm = UNIT2 * (east * east + north * north)
    rows = [east] * 3 + [north] * 3 + [one] * 3 + three_parts(norm) + [jnp.zeros_like(east)] * 4
    return jnp.concatenate(rows, axis=0).astype(jnp.bfloat16)


def tile_of(left, right):
    squared = lax.dot_general(left, right, (((0,), (0,)), ((), ())), preferred_element_type=jnp.float32)
    squared = jnp.maximum(squared, LEAST)
    inverse = lax.rsqrt(squared)
    z = squared * inverse
    outer = jnp.maximum(2.0 * UNIT - z, 0.0)
    inner = jnp.maximum(UNIT - z, 0.0)
    outer2 = outer * outer
    inner2 = inner * inner
    shifted = z + 2.0 * UNIT
    first = (outer2 * outer2) * (z * shifted - 0.5 * UNIT2)
    second = (inner2 * inner2) * (inner * shifted)
    return ((first + 4.0 * second) * inverse).astype(jnp.bfloat16)


def diag_kernel(ens_ref, inc_ref, coords_ref, out_ref):
    members, levels, points = ens_ref.shape[1:]
    parts, _, step, _ = out_ref.shape
    rows = members * levels
    half = points // 2
    places = coords_ref[0].astype(jnp.float32)
    left, right = left_rows(places), right_rows(places)
    upper = tile_of(left[:, :half], right)
    lower = tile_of(left[:, half:], right[:, half:])
    weighted = (ens_ref[0] * inc_ref[0][None]).reshape(rows, points)
    near, far = weighted[:, :half], weighted[:, half:]
    field_near = jnp.dot(near, upper[:, :half], preferred_element_type=jnp.float32) + lax.dot_general(
        far, upper[:, half:], (((1,), (1,)), ((), ())), preferred_element_type=jnp.float32
    )
    field_far = jnp.dot(near, upper[:, half:], preferred_element_type=jnp.float32) + jnp.dot(
        far, lower, preferred_element_type=jnp.float32
    )
    block = ens_ref[0].astype(jnp.float32)
    sum_near = jnp.sum(block[:, :, :half] * field_near.reshape(members, levels, half), axis=0)
    sum_far = jnp.sum(block[:, :, half:] * field_far.reshape(members, levels, half), axis=0)
    out_ref[:, 0, :, :half] = sum_near.reshape(parts, step, half).astype(out_ref.dtype)
    out_ref[:, 0, :, half:] = sum_far.reshape(parts, step, half).astype(out_ref.dtype)


def diag(ensemble, increment, coords, parts):
    blocks, members, levels, points = ensemble.shape
    step = levels // parts
    return pl.pallas_call(
        diag_kernel,
        grid=(blocks,),
        in_specs=[
            pl.BlockSpec((1, members, levels, points), lambda b: (b, 0, 0, 0)),
            pl.BlockSpec((1, levels, points), lambda b: (b, 0, 0)),
            pl.BlockSpec((1, 2, points), lambda b: (b, 0, 0)),
        ],
        out_specs=pl.BlockSpec((parts, 1, step, points), lambda b: (0, b, 0, 0)),
        out_shape=jax.ShapeDtypeStruct((parts, blocks, step, points), jnp.bfloat16),
        compiler_params=pltpu.CompilerParams(vmem_limit_bytes=60 * MIB),
        cost_estimate=pl.CostEstimate(flops=20_000_000_000, bytes_accessed=8_000_000, transcendentals=0),
        name="diag",
    )(ensemble, increment, coords)


def tiles_kernel(pairs, places_ref, out_ref):
    first = pl.program_id(0) * TILE_GROUP
    for within in range(TILE_GROUP):
        left = left_rows(places_ref[pairs[0, first + within]].astype(jnp.float32))
        right = right_rows(places_ref[pairs[1, first + within]].astype(jnp.float32))
        out_ref[within] = tile_of(left, right)


def tiles(places, pairs):
    slot_total, _, points = places.shape
    cap = pairs.shape[1]
    return pl.pallas_call(
        tiles_kernel,
        grid_spec=pltpu.PrefetchScalarGridSpec(
            num_scalar_prefetch=1,
            grid=(cap // TILE_GROUP,),
            in_specs=[pl.BlockSpec((slot_total, 2, points), lambda i, p: (0, 0, 0))],
            out_specs=pl.BlockSpec((TILE_GROUP, points, points), lambda i, p: (i, 0, 0)),
        ),
        out_shape=jax.ShapeDtypeStruct((cap, points, points), jnp.bfloat16),
        compiler_params=pltpu.CompilerParams(vmem_limit_bytes=60 * MIB),
        cost_estimate=pl.CostEstimate(flops=30_000_000_000, bytes_accessed=17_000_000, transcendentals=0),
        name="tiles",
    )(pairs, places)


def apply_kernel(
    pairs, count, got_ref, stack_ref, out_ref,
    ens_ref, inc_ref, weighted_ref, field_ref, tiles_ref, ens_sem, inc_sem, tiles_sem,
):
    slot_total, sources, rows, points = ens_ref.shape
    step = inc_ref.shape[2]
    lane_chunks = points // LANES
    every = sources * rows

    def ens_copies(slot):
        return [
            pltpu.make_async_copy(
                got_ref.at[slot, :, lane * rows : (lane + 1) * rows, :],
                ens_ref.at[slot, :, :, lane * LANES : (lane + 1) * LANES],
                ens_sem.at[slot, lane],
            )
            for lane in range(lane_chunks)
        ]

    inc_copy = pltpu.make_async_copy(got_ref.at[:, :lane_chunks, rows * lane_chunks :, :], inc_ref, inc_sem)

    def tile_copy(index):
        return pltpu.make_async_copy(stack_ref.at[index], tiles_ref.at[index], tiles_sem.at[index])

    inc_copy.start()
    for slot in range(slot_total):
        for copy in ens_copies(slot):
            copy.start()
    for index in range(tiles_ref.shape[0]):
        tile_copy(index).start()
    inc_copy.wait()
    for slot in range(slot_total):
        field_ref[slot] = jnp.zeros((every, points), jnp.float32)
        for copy in ens_copies(slot):
            copy.wait()
        for lane in range(lane_chunks):
            here = slice(lane * LANES, (lane + 1) * LANES)
            gain = inc_ref[slot, lane]
            block = ens_ref[slot, :, :, here].reshape(every // step, step, LANES)
            weighted_ref[slot, :, here] = (block * gain[None]).reshape(every, LANES)

    def some(start, number):
        products = []
        for within in range(number):
            tile_copy(start + within).wait()
        for within in range(number):
            index = start + within
            first, second = pairs[0, index], pairs[1, index]
            tile = tiles_ref[index]
            to_first = lax.dot_general(
                weighted_ref[second], tile, (((1,), (1,)), ((), ())), preferred_element_type=jnp.float32
            )
            to_second = jnp.dot(weighted_ref[first], tile, preferred_element_type=jnp.float32)
            products += [(first, to_first), (second, to_second)]
        for slot, product in products:
            field_ref[slot] += product

    def group(turn, carry):
        some(turn * PAIR_GROUP, PAIR_GROUP)
        return carry

    def one(index, carry):
        some(index, 1)
        return carry

    def skip(index, carry):
        tile_copy(index).wait()
        return carry

    groups = count[0] // PAIR_GROUP
    lax.fori_loop(0, groups, group, 0)
    lax.fori_loop(groups * PAIR_GROUP, count[0], one, 0)
    lax.fori_loop(count[0], tiles_ref.shape[0], skip, 0)

    for slot in range(slot_total):
        product = ens_ref[slot].reshape(every, points).astype(jnp.float32) * field_ref[slot]
        out_ref[slot] = jnp.sum(product.reshape(every // step, step, points), axis=0)


def apply_pairs(got, tile_stack, pairs, count, members, step):
    slot_total, sources, rows, _ = got.shape
    points = tile_stack.shape[2]
    lane_chunks = points // LANES
    every = sources * members * step
    return pl.pallas_call(
        apply_kernel,
        in_specs=[
            pl.BlockSpec(memory_space=pltpu.SMEM),
            pl.BlockSpec(memory_space=pltpu.SMEM),
            pl.BlockSpec(memory_space=pl.ANY),
            pl.BlockSpec(memory_space=pl.ANY),
        ],
        out_specs=pl.BlockSpec(memory_space=pltpu.VMEM),
        scratch_shapes=[
            pltpu.VMEM((slot_total, sources, members * step, points), jnp.bfloat16),
            pltpu.VMEM((slot_total, lane_chunks, step, LANES), jnp.bfloat16),
            pltpu.VMEM((slot_total, every, points), jnp.bfloat16),
            pltpu.VMEM((slot_total, every, points), jnp.float32),
            pltpu.VMEM(tile_stack.shape, jnp.bfloat16),
            pltpu.SemaphoreType.DMA((slot_total, lane_chunks)),
            pltpu.SemaphoreType.DMA,
            pltpu.SemaphoreType.DMA((tile_stack.shape[0],)),
        ],
        out_shape=jax.ShapeDtypeStruct((slot_total, step, points), jnp.float32),
        compiler_params=pltpu.CompilerParams(vmem_limit_bytes=60 * MIB),
        cost_estimate=pl.CostEstimate(flops=9_000_000_000, bytes_accessed=22_000_000, transcendentals=0),
        name="apply",
    )(pairs, count, got, tile_stack)


def finish_kernel(slots, parts_ref, back_ref, out_ref, *, scale):
    out_ref[...] = jnp.sum(parts_ref[...].astype(jnp.float32), axis=0) * scale
    for owner in range(back_ref.shape[0]):
        slot = slots[owner]
        out_ref[slot] = out_ref[slot] + back_ref[owner] * scale


def finish(parts, back, slots, scale):
    return pl.pallas_call(
        functools.partial(finish_kernel, scale=scale),
        in_specs=[
            pl.BlockSpec(memory_space=pltpu.SMEM),
            pl.BlockSpec(memory_space=pltpu.VMEM),
            pl.BlockSpec(memory_space=pltpu.VMEM),
        ],
        out_specs=pl.BlockSpec(memory_space=pltpu.VMEM),
        out_shape=jax.ShapeDtypeStruct(parts.shape[1:], jnp.float32),
        compiler_params=pltpu.CompilerParams(vmem_limit_bytes=16 * MIB),
        name="finish",
    )(slots, parts, back)


def per_device(ensemble, increment, coords, sent_slots, pair_list, pair_count):
    blocks, members, levels, points = ensemble.shape
    regions = lax.axis_size("region")
    groups = lax.axis_size("member")
    step = levels // groups
    slots = sent_slots.reshape(-1)
    pairs = pair_list.T
    own = lax.axis_index("member").reshape(1).astype(jnp.int32)
    places = select(coords, slots)
    own_places = lax.all_to_all(places, "region", 0, 0, tiled=True)
    big = pack(ensemble, increment, slots, own, groups)
    big, own_places = lax.optimization_barrier((big, own_places))
    got = lax.all_to_all(
        big.reshape(regions * groups, -1, LANES), ("region", "member"), 0, 0, tiled=True
    ).reshape(regions, groups, -1, LANES)
    diagonal = diag(ensemble, increment, coords, groups)
    tile_stack = tiles(own_places, pairs)
    got, diagonal, tile_stack = lax.optimization_barrier((got, diagonal, tile_stack))
    parts = lax.all_to_all(diagonal, "member", 0, 0, tiled=True)
    partial = apply_pairs(got, tile_stack, pairs, pair_count, members, step)
    partial, parts = lax.optimization_barrier((partial, parts))
    back = lax.all_to_all(partial, "region", 0, 0, tiled=True)
    return finish(parts, back, slots, 1.0 / (members * groups - 1))


def solution(mesh):
    in_specs = (
        P("region", "member", None, None),
        P("region", None, None),
        P("region", None, None),
        P("region", None, None),
        P("region", None),
        P("region"),
    )
    out_specs = P("region", "member", None)
    return jax.shard_map(
        per_device, mesh=mesh, in_specs=in_specs, out_specs=out_specs, check_vma=False
    )
```

```python
import functools

import jax
import jax.numpy as jnp
from jax import lax
from jax.experimental import pallas as pl
from jax.experimental.pallas import tpu as pltpu
from jax.sharding import PartitionSpec as P

LANES = 128
PAIR_GROUP = 4
MIB = 1024 * 1024
UNIT = 12.0**-0.2
UNIT2 = UNIT * UNIT
LEAST = UNIT2 * 2.0**-12


def select_kernel(slots, coords_ref, places_ref, sem):
    total = places_ref.shape[0]

    def copy(owner):
        return pltpu.make_async_copy(coords_ref.at[slots[owner]], places_ref.at[owner], sem.at[owner])

    for owner in range(total):
        copy(owner).start()
    for owner in range(total):
        copy(owner).wait()


def select(coords, slots):
    total = slots.shape[0]
    return pl.pallas_call(
        select_kernel,
        in_specs=[pl.BlockSpec(memory_space=pltpu.SMEM), pl.BlockSpec(memory_space=pl.ANY)],
        out_specs=pl.BlockSpec(memory_space=pl.ANY),
        out_shape=jax.ShapeDtypeStruct((total, *coords.shape[1:]), coords.dtype),
        scratch_shapes=[pltpu.SemaphoreType.DMA((total,))],
        compiler_params=pltpu.CompilerParams(vmem_limit_bytes=60 * MIB),
        name="select",
    )(slots, coords)


def pack_kernel(slots, own, ens_ref, inc_ref, big_ref, ens_buf, inc_buf, out_buf, in_sem, inc_sem, out_sem):
    total, members, levels, points = ens_buf.shape
    parts = out_buf.shape[1]
    step = levels // parts
    lane_chunks = points // LANES

    def ens_copy(owner):
        return pltpu.make_async_copy(ens_ref.at[slots[owner]], ens_buf.at[owner], in_sem.at[owner])

    def inc_copy(owner):
        return pltpu.make_async_copy(inc_ref.at[slots[owner]], inc_buf.at[owner], inc_sem.at[owner])

    def out_copy(owner):
        return pltpu.make_async_copy(out_buf.at[owner], big_ref.at[owner], out_sem.at[owner])

    for owner in range(total):
        ens_copy(owner).start()
        inc_copy(owner).start()
    chunk = pl.multiple_of(lax.rem(own[0], lane_chunks) * LANES, LANES)
    for owner in range(total):
        ens_copy(owner).wait()
        inc_copy(owner).wait()
        for part in range(parts):
            here = slice(part * step, (part + 1) * step)
            for lane in range(lane_chunks):
                out_buf[owner, part, lane * members * step : (lane + 1) * members * step, :] = ens_buf[
                    owner, :, here, lane * LANES : (lane + 1) * LANES
                ].reshape(members * step, LANES)
            out_buf[owner, part, members * step * lane_chunks :, :] = inc_buf[owner, here, pl.ds(chunk, LANES)]
        out_copy(owner).start()
    for owner in range(total):
        out_copy(owner).wait()


def pack(ensemble, increment, slots, own, parts):
    blocks, members, levels, points = ensemble.shape
    total = slots.shape[0]
    step = levels // parts
    rows = members * step * (points // LANES) + step
    return pl.pallas_call(
        pack_kernel,
        in_specs=[
            pl.BlockSpec(memory_space=pltpu.SMEM),
            pl.BlockSpec(memory_space=pltpu.SMEM),
            pl.BlockSpec(memory_space=pl.ANY),
            pl.BlockSpec(memory_space=pl.ANY),
        ],
        out_specs=pl.BlockSpec(memory_space=pl.ANY),
        out_shape=jax.ShapeDtypeStruct((total, parts, rows, LANES), ensemble.dtype),
        scratch_shapes=[
            pltpu.VMEM((total, members, levels, points), ensemble.dtype),
            pltpu.VMEM((total, levels, points), increment.dtype),
            pltpu.VMEM((total, parts, rows, LANES), ensemble.dtype),
            pltpu.SemaphoreType.DMA((total,)),
            pltpu.SemaphoreType.DMA((total,)),
            pltpu.SemaphoreType.DMA((total,)),
        ],
        compiler_params=pltpu.CompilerParams(vmem_limit_bytes=60 * MIB),
        name="pack",
    )(slots, own, ensemble, increment)


def three_parts(value):
    first = value.astype(jnp.bfloat16).astype(jnp.float32)
    rest = value - first
    second = rest.astype(jnp.bfloat16).astype(jnp.float32)
    return [first, second, rest - second]


def left_rows(places):
    east, north = places[0:1], places[1:2]
    one = jnp.ones_like(east)
    norm = UNIT2 * (east * east + north * north)
    rows = three_parts((-2.0 * UNIT2) * east) + three_parts((-2.0 * UNIT2) * north) + three_parts(norm)
    rows = rows + [one] * 3 + [jnp.zeros_like(east)] * 4
    return jnp.concatenate(rows, axis=0).astype(jnp.bfloat16)


def right_rows(places):
    east, north = places[0:1], places[1:2]
    one = jnp.ones_like(east)
    norm = UNIT2 * (east * east + north * north)
    rows = [east] * 3 + [north] * 3 + [one] * 3 + three_parts(norm) + [jnp.zeros_like(east)] * 4
    return jnp.concatenate(rows, axis=0).astype(jnp.bfloat16)


def tile_of(left, right):
    squared = lax.dot_general(left, right, (((0,), (0,)), ((), ())), preferred_element_type=jnp.float32)
    squared = jnp.maximum(squared, LEAST)
    inverse = lax.rsqrt(squared)
    z = squared * inverse
    outer = jnp.maximum(2.0 * UNIT - z, 0.0)
    inner = jnp.maximum(UNIT - z, 0.0)
    outer2 = outer * outer
    inner2 = inner * inner
    shifted = z + 2.0 * UNIT
    first = (outer2 * outer2) * (z * shifted - 0.5 * UNIT2)
    second = (inner2 * inner2) * (inner * shifted)
    return ((first + 4.0 * second) * inverse).astype(jnp.bfloat16)


def diag_kernel(core, ens_ref, inc_ref, coords_ref, keep_ref, send_ref, sum_ref):
    members, levels, points = ens_ref.shape[1:]
    parts, _, step, _ = keep_ref.shape
    rows = members * levels
    half = points // 2
    places = coords_ref[0].astype(jnp.float32)
    left, right = left_rows(places), right_rows(places)
    upper = tile_of(left[:, :half], right)
    lower = tile_of(left[:, half:], right[:, half:])
    weighted = (ens_ref[0] * inc_ref[0][None]).reshape(rows, points)
    near, far = weighted[:, :half], weighted[:, half:]
    field_near = jnp.dot(near, upper[:, :half], preferred_element_type=jnp.float32) + lax.dot_general(
        far, upper[:, half:], (((1,), (1,)), ((), ())), preferred_element_type=jnp.float32
    )
    field_far = jnp.dot(near, upper[:, half:], preferred_element_type=jnp.float32) + jnp.dot(
        far, lower, preferred_element_type=jnp.float32
    )
    block = ens_ref[0].astype(jnp.float32)
    sum_ref[:, :half] = jnp.sum(block[:, :, :half] * field_near.reshape(members, levels, half), axis=0)
    sum_ref[:, half:] = jnp.sum(block[:, :, half:] * field_far.reshape(members, levels, half), axis=0)
    for part in range(parts):
        mine = pl.multiple_of((2 * part + core[0]) * step, step)
        other = pl.multiple_of((2 * part + 1 - core[0]) * step, step)
        keep_ref[part, 0] = sum_ref[pl.ds(mine, step), :]
        send_ref[part, 0] = sum_ref[pl.ds(other, step), :]


def diag(ensemble, increment, coords, core, parts):
    blocks, members, levels, points = ensemble.shape
    step = levels // (2 * parts)
    out = jax.ShapeDtypeStruct((parts, blocks, step, points), jnp.float32)
    return pl.pallas_call(
        diag_kernel,
        grid_spec=pltpu.PrefetchScalarGridSpec(
            num_scalar_prefetch=1,
            grid=(blocks,),
            in_specs=[
                pl.BlockSpec((1, members, levels, points), lambda b, c: (b, 0, 0, 0)),
                pl.BlockSpec((1, levels, points), lambda b, c: (b, 0, 0)),
                pl.BlockSpec((1, 2, points), lambda b, c: (b, 0, 0)),
            ],
            out_specs=[pl.BlockSpec((parts, 1, step, points), lambda b, c: (0, b, 0, 0))] * 2,
            scratch_shapes=[pltpu.VMEM((levels, points), jnp.float32)],
        ),
        out_shape=[out, out],
        compiler_params=pltpu.CompilerParams(vmem_limit_bytes=60 * MIB),
        cost_estimate=pl.CostEstimate(flops=20_000_000_000, bytes_accessed=8_000_000, transcendentals=0),
        name="diag",
    )(core, ensemble, increment, coords)


def merge_kernel(row, keep_ref, got_ref, own_ref, *send_refs):
    parts = keep_ref.shape[0]
    own_ref[...] = keep_ref[row[0]] + got_ref[row[0]]
    for shift, send_ref in enumerate(send_refs, 1):
        there = lax.rem(row[0] + shift, parts)
        send_ref[...] = (keep_ref[there] + got_ref[there]).astype(send_ref.dtype)


def merge(keep, got, row):
    parts = keep.shape[0]
    out = [jax.ShapeDtypeStruct(keep.shape[1:], jnp.float32)]
    out += [jax.ShapeDtypeStruct(keep.shape[1:], jnp.bfloat16)] * (parts - 1)
    return pl.pallas_call(
        merge_kernel,
        in_specs=[pl.BlockSpec(memory_space=pltpu.SMEM)] + [pl.BlockSpec(memory_space=pltpu.VMEM)] * 2,
        out_specs=[pl.BlockSpec(memory_space=pltpu.VMEM)] * parts,
        out_shape=out,
        compiler_params=pltpu.CompilerParams(vmem_limit_bytes=16 * MIB),
        name="merge",
    )(row, keep, got)


def tiles_kernel(pairs, first, places_ref, out_ref):
    for within in range(out_ref.shape[0]):
        index = first[0] + within
        left = left_rows(places_ref[pairs[0, index]].astype(jnp.float32))
        right = right_rows(places_ref[pairs[1, index]].astype(jnp.float32))
        out_ref[within] = tile_of(left, right)


def tiles(places, pairs, first):
    points = places.shape[2]
    return pl.pallas_call(
        tiles_kernel,
        in_specs=[
            pl.BlockSpec(memory_space=pltpu.SMEM),
            pl.BlockSpec(memory_space=pltpu.SMEM),
            pl.BlockSpec(memory_space=pltpu.VMEM),
        ],
        out_specs=pl.BlockSpec(memory_space=pltpu.VMEM),
        out_shape=jax.ShapeDtypeStruct((PAIR_GROUP, points, points), jnp.bfloat16),
        compiler_params=pltpu.CompilerParams(vmem_limit_bytes=60 * MIB),
        cost_estimate=pl.CostEstimate(flops=4_000_000_000, bytes_accessed=2_000_000, transcendentals=0),
        name="tiles",
    )(pairs, first, places)


def apply_kernel(
    pairs, count, core, got_ref, *refs,
):
    *stacks, out_ref, ens_ref, inc_ref, weighted_ref, field_ref, tiles_ref, ens_sem, inc_sem, tiles_sem = refs
    slot_total, sources, rows, points = ens_ref.shape
    step = inc_ref.shape[2]
    groups = len(stacks)
    lane_chunks = points // LANES
    every = sources * rows

    def ens_copies(slot):
        return [
            pltpu.make_async_copy(
                got_ref.at[slot, :, lane * rows : (lane + 1) * rows, :],
                ens_ref.at[slot, :, :, lane * LANES : (lane + 1) * LANES],
                ens_sem.at[slot, lane],
            )
            for lane in range(lane_chunks)
        ]

    inc_copy = pltpu.make_async_copy(got_ref.at[:, :lane_chunks, rows * lane_chunks :, :], inc_ref, inc_sem)

    def tile_copy(group):
        return pltpu.make_async_copy(stacks[group], tiles_ref.at[group], tiles_sem.at[group])

    inc_copy.start()
    for slot in range(slot_total):
        for copy in ens_copies(slot):
            copy.start()
    for group in range(groups):
        tile_copy(group).start()
    inc_copy.wait()
    for slot in range(slot_total):
        field_ref[slot] = jnp.zeros((every, points), jnp.float32)
        for copy in ens_copies(slot):
            copy.wait()
        for lane in range(lane_chunks):
            here = slice(lane * LANES, (lane + 1) * LANES)
            gain = inc_ref[slot, lane]
            block = ens_ref[slot, :, :, here].reshape(every // step, step, LANES)
            weighted_ref[slot, :, here] = (block * gain[None]).reshape(every, LANES)

    def some(group, row, within, number):
        products = []
        for each in range(number):
            first, second = pairs[0, row + each], pairs[1, row + each]
            tile = tiles_ref[group, within + each]
            to_first = lax.dot_general(
                weighted_ref[second], tile, (((1,), (1,)), ((), ())), preferred_element_type=jnp.float32
            )
            to_second = jnp.dot(weighted_ref[first], tile, preferred_element_type=jnp.float32)
            products += [(first, to_first), (second, to_second)]
        for slot, product in products:
            field_ref[slot] += product

    def turn(group, carry):
        away = core[0] * (groups // 2)
        row = PAIR_GROUP * jnp.where(group < groups // 2, group + away, group - away)
        live = count[0] - row
        pltpu.make_async_copy(stacks[0], tiles_ref.at[group], tiles_sem.at[group]).wait()

        @pl.when(live >= PAIR_GROUP)
        def _():
            some(group, row, 0, PAIR_GROUP)

        @pl.when(live < PAIR_GROUP)
        def _():
            def one(within, inner):
                some(group, row + within, within, 1)
                return inner

            lax.fori_loop(0, jnp.maximum(live, 0), one, 0)

        return carry

    lax.fori_loop(0, groups, turn, 0)

    for slot in range(slot_total):
        product = ens_ref[slot].reshape(every, points).astype(jnp.float32) * field_ref[slot]
        out_ref[slot] = jnp.sum(product.reshape(every // step, step, points), axis=0)


def apply_pairs(got, stacks, pairs, count, core, members, step):
    slot_total, sources, rows, _ = got.shape
    points = stacks[0].shape[2]
    lane_chunks = points // LANES
    every = sources * members * step
    return pl.pallas_call(
        apply_kernel,
        in_specs=[
            pl.BlockSpec(memory_space=pltpu.SMEM),
            pl.BlockSpec(memory_space=pltpu.SMEM),
            pl.BlockSpec(memory_space=pltpu.SMEM),
            pl.BlockSpec(memory_space=pl.ANY),
            *[pl.BlockSpec(memory_space=pl.ANY)] * len(stacks),
        ],
        out_specs=pl.BlockSpec(memory_space=pltpu.VMEM),
        scratch_shapes=[
            pltpu.VMEM((slot_total, sources, members * step, points), jnp.bfloat16),
            pltpu.VMEM((slot_total, lane_chunks, step, LANES), jnp.bfloat16),
            pltpu.VMEM((slot_total, every, points), jnp.bfloat16),
            pltpu.VMEM((slot_total, every, points), jnp.float32),
            pltpu.VMEM((len(stacks), *stacks[0].shape), jnp.bfloat16),
            pltpu.SemaphoreType.DMA((slot_total, lane_chunks)),
            pltpu.SemaphoreType.DMA,
            pltpu.SemaphoreType.DMA((len(stacks),)),
        ],
        out_shape=jax.ShapeDtypeStruct((slot_total, step, points), jnp.float32),
        compiler_params=pltpu.CompilerParams(vmem_limit_bytes=60 * MIB),
        cost_estimate=pl.CostEstimate(flops=9_000_000_000, bytes_accessed=22_000_000, transcendentals=0),
        name="apply",
    )(pairs, count, core, got, *stacks)


def finish_kernel(slots, own_ref, *refs, scale):
    *part_refs, back_ref, out_ref = refs
    total = own_ref[...]
    for part_ref in part_refs:
        total = total + part_ref[...].astype(jnp.float32)
    out_ref[...] = total * scale
    for owner in range(back_ref.shape[0]):
        slot = slots[owner]
        out_ref[slot] = out_ref[slot] + back_ref[owner] * scale


def finish(own, parts, back, slots, scale):
    return pl.pallas_call(
        functools.partial(finish_kernel, scale=scale),
        in_specs=[pl.BlockSpec(memory_space=pltpu.SMEM)] + [pl.BlockSpec(memory_space=pltpu.VMEM)] * (len(parts) + 2),
        out_specs=pl.BlockSpec(memory_space=pltpu.VMEM),
        out_shape=jax.ShapeDtypeStruct(own.shape, jnp.float32),
        compiler_params=pltpu.CompilerParams(vmem_limit_bytes=16 * MIB),
        name="finish",
    )(slots, own, *parts, back)


def per_device(ensemble, increment, coords, sent_slots, pair_list, pair_count):
    blocks, members, levels, points = ensemble.shape
    regions = lax.axis_size("region")
    groups = lax.axis_size("member")
    step = levels // groups
    slots = sent_slots.reshape(-1)
    pairs = pair_list.T
    own = lax.axis_index("member").reshape(1).astype(jnp.int32)
    places = select(coords, slots)
    own_places = lax.all_to_all(places, "region", 0, 0, tiled=True)
    big = pack(ensemble, increment, slots, own, groups)
    big, own_places = lax.optimization_barrier((big, own_places))
    got = lax.all_to_all(
        big.reshape(regions * groups, -1, LANES), ("region", "member"), 0, 0, tiled=True
    ).reshape(regions, groups, -1, LANES)
    swap = [(i, i ^ 1) for i in range(groups)]
    core, row = own & 1, own >> 1
    rows = groups // 2
    share = pairs.shape[1] // 2
    mine = [tiles(own_places, pairs, core * share + start) for start in range(0, share, PAIR_GROUP)]
    theirs = [lax.ppermute(stack, "member", swap) for stack in mine]
    keep, send = diag(ensemble, increment, coords, core, rows)
    merged = merge(keep, lax.ppermute(send, "member", swap), row)
    parts = [
        lax.ppermute(part, "member", [(i, (i + 2 * shift) % groups) for i in range(groups)])
        for shift, part in enumerate(merged[1:], 1)
    ]
    got, parts = lax.optimization_barrier((got, parts))
    partial = apply_pairs(got, mine + theirs, pairs, pair_count, core, members, step)
    back = lax.all_to_all(partial, "region", 0, 0, tiled=True)
    return finish(merged[0], parts, back, slots, 1.0 / (members * groups - 1))


def solution(mesh):
    in_specs = (
        P("region", "member", None, None),
        P("region", None, None),
        P("region", None, None),
        P("region", None, None),
        P("region", None),
        P("region"),
    )
    out_specs = P("region", "member", None)
    return jax.shard_map(
        per_device, mesh=mesh, in_specs=in_specs, out_specs=out_specs, check_vma=False
    )
```

```python
import functools
import math

import jax
import jax.numpy as jnp
from jax import lax
from jax.experimental import pallas as pl
from jax.experimental.pallas import tpu as pltpu
from jax.sharding import PartitionSpec as P

LANES = 128
PAIR_GROUP = 4
MIB = 1024 * 1024
UNIT = 12.0**-0.2
UNIT2 = UNIT * UNIT
LEAST = UNIT2 * 2.0**-12


def pack_kernel(
    slots, own, ens_ref, inc_ref, coords_ref, big_ref, places_ref, ens_buf, inc_buf, out_buf, in_sem, inc_sem, out_sem, places_sem
):
    total, members, levels, points = ens_buf.shape
    parts = out_buf.shape[1]
    step = levels // parts
    lane_chunks = points // LANES

    def ens_copy(owner):
        return pltpu.make_async_copy(ens_ref.at[slots[owner]], ens_buf.at[owner], in_sem.at[owner])

    def inc_copy(owner):
        return pltpu.make_async_copy(inc_ref.at[slots[owner]], inc_buf.at[owner], inc_sem.at[owner])

    def out_copy(owner):
        return pltpu.make_async_copy(out_buf.at[owner], big_ref.at[owner], out_sem.at[owner])

    def places_copy(owner):
        return pltpu.make_async_copy(coords_ref.at[slots[owner]], places_ref.at[owner], places_sem.at[owner])

    for owner in range(total):
        ens_copy(owner).start()
        inc_copy(owner).start()
    for owner in range(total):
        places_copy(owner).start()
    chunk = pl.multiple_of(lax.rem(own[0], lane_chunks) * LANES, LANES)
    for owner in range(total):
        ens_copy(owner).wait()
        inc_copy(owner).wait()
        for part in range(parts):
            here = slice(part * step, (part + 1) * step)
            for lane in range(lane_chunks):
                out_buf[owner, part, lane * members * step : (lane + 1) * members * step, :] = ens_buf[
                    owner, :, here, lane * LANES : (lane + 1) * LANES
                ].reshape(members * step, LANES)
            out_buf[owner, part, members * step * lane_chunks :, :] = inc_buf[owner, here, pl.ds(chunk, LANES)]
        out_copy(owner).start()
    for owner in range(total):
        places_copy(owner).wait()
        out_copy(owner).wait()


def pack(ensemble, increment, coords, slots, own, parts):
    blocks, members, levels, points = ensemble.shape
    total = slots.shape[0]
    step = levels // parts
    rows = members * step * (points // LANES) + step
    return pl.pallas_call(
        pack_kernel,
        in_specs=[
            pl.BlockSpec(memory_space=pltpu.SMEM),
            pl.BlockSpec(memory_space=pltpu.SMEM),
            pl.BlockSpec(memory_space=pl.ANY),
            pl.BlockSpec(memory_space=pl.ANY),
            pl.BlockSpec(memory_space=pl.ANY),
        ],
        out_specs=[pl.BlockSpec(memory_space=pl.ANY)] * 2,
        out_shape=[
            jax.ShapeDtypeStruct((total, parts, rows, LANES), ensemble.dtype),
            jax.ShapeDtypeStruct((total, *coords.shape[1:]), coords.dtype),
        ],
        scratch_shapes=[
            pltpu.VMEM((total, members, levels, points), ensemble.dtype),
            pltpu.VMEM((total, levels, points), increment.dtype),
            pltpu.VMEM((total, parts, rows, LANES), ensemble.dtype),
            pltpu.SemaphoreType.DMA((total,)),
            pltpu.SemaphoreType.DMA((total,)),
            pltpu.SemaphoreType.DMA((total,)),
            pltpu.SemaphoreType.DMA((total,)),
        ],
        compiler_params=pltpu.CompilerParams(vmem_limit_bytes=60 * MIB),
        name="pack",
    )(slots, own, ensemble, increment, coords)


def in_hbm(value):
    return pltpu.with_memory_space_constraint(value, pltpu.HBM)


def three_parts(value):
    first = value.astype(jnp.bfloat16).astype(jnp.float32)
    rest = value - first
    second = rest.astype(jnp.bfloat16).astype(jnp.float32)
    return [first, second, rest - second]


def left_rows(places):
    east, north = places[0:1], places[1:2]
    one = jnp.ones_like(east)
    norm = UNIT2 * (east * east + north * north)
    rows = three_parts((-2.0 * UNIT2) * east) + three_parts((-2.0 * UNIT2) * north) + three_parts(norm)
    rows = rows + [one] * 3 + [jnp.zeros_like(east)] * 4
    return jnp.concatenate(rows, axis=0).astype(jnp.bfloat16)


def right_rows(places):
    east, north = places[0:1], places[1:2]
    one = jnp.ones_like(east)
    norm = UNIT2 * (east * east + north * north)
    rows = [east] * 3 + [north] * 3 + [one] * 3 + three_parts(norm) + [jnp.zeros_like(east)] * 4
    return jnp.concatenate(rows, axis=0).astype(jnp.bfloat16)


def tile_of(left, right):
    squared = lax.dot_general(left, right, (((0,), (0,)), ((), ())), preferred_element_type=jnp.float32)
    squared = jnp.maximum(squared, LEAST)
    inverse = lax.rsqrt(squared)
    z = squared * inverse
    outer = jnp.maximum(2.0 * UNIT - z, 0.0)
    inner = jnp.maximum(UNIT - z, 0.0)
    outer2 = outer * outer
    inner2 = inner * inner
    shifted = z + 2.0 * UNIT
    first = (outer2 * outer2) * (z * shifted - 0.5 * UNIT2)
    second = (inner2 * inner2) * (inner * shifted)
    return ((first + 4.0 * second) * inverse).astype(jnp.bfloat16)


def diag_kernel(core, ens_ref, inc_ref, coords_ref, keep_ref, send_ref, sum_ref):
    members, levels, points = ens_ref.shape[1:]
    parts, _, step, _ = keep_ref.shape
    rows = members * levels
    half = points // 2
    places = coords_ref[0].astype(jnp.float32)
    left, right = left_rows(places), right_rows(places)
    upper = tile_of(left[:, :half], right)
    lower = tile_of(left[:, half:], right[:, half:])
    weighted = (ens_ref[0] * inc_ref[0][None]).reshape(rows, points)
    near, far = weighted[:, :half], weighted[:, half:]
    field_near = jnp.dot(near, upper[:, :half], preferred_element_type=jnp.float32) + lax.dot_general(
        far, upper[:, half:], (((1,), (1,)), ((), ())), preferred_element_type=jnp.float32
    )
    field_far = jnp.dot(near, upper[:, half:], preferred_element_type=jnp.float32) + jnp.dot(
        far, lower, preferred_element_type=jnp.float32
    )
    block = ens_ref[0].astype(jnp.float32)
    sum_ref[:, :half] = jnp.sum(block[:, :, :half] * field_near.reshape(members, levels, half), axis=0)
    sum_ref[:, half:] = jnp.sum(block[:, :, half:] * field_far.reshape(members, levels, half), axis=0)
    for part in range(parts):
        mine = pl.multiple_of((2 * part + core[0]) * step, step)
        other = pl.multiple_of((2 * part + 1 - core[0]) * step, step)
        keep_ref[part, 0] = sum_ref[pl.ds(mine, step), :]
        send_ref[part, 0] = sum_ref[pl.ds(other, step), :]


def diag(ensemble, increment, coords, core, parts, start, blocks):
    _, members, levels, points = ensemble.shape
    step = levels // (2 * parts)
    out = jax.ShapeDtypeStruct((parts, blocks, step, points), jnp.float32)
    return pl.pallas_call(
        diag_kernel,
        grid_spec=pltpu.PrefetchScalarGridSpec(
            num_scalar_prefetch=1,
            grid=(blocks,),
            in_specs=[
                pl.BlockSpec((1, members, levels, points), lambda b, c: (start + b, 0, 0, 0)),
                pl.BlockSpec((1, levels, points), lambda b, c: (start + b, 0, 0)),
                pl.BlockSpec((1, 2, points), lambda b, c: (start + b, 0, 0)),
            ],
            out_specs=[pl.BlockSpec((parts, 1, step, points), lambda b, c: (0, b, 0, 0))] * 2,
            scratch_shapes=[pltpu.VMEM((levels, points), jnp.float32)],
        ),
        out_shape=[out, out],
        compiler_params=pltpu.CompilerParams(vmem_limit_bytes=60 * MIB),
        cost_estimate=pl.CostEstimate(flops=10_000_000_000, bytes_accessed=8_000_000, transcendentals=0),
        name="diag",
    )(core, ensemble, increment, coords)


def merge_kernel(row, near_keep, far_keep, near_got, far_got, own_ref, *send_refs):
    parts, blocks = near_keep.shape[:2]
    for half, (keep_ref, got_ref) in enumerate([(near_keep, near_got), (far_keep, far_got)]):
        here = slice(half * blocks, (half + 1) * blocks)
        own_ref[here] = keep_ref[row[0]] + got_ref[row[0]]
        for shift, send_ref in enumerate(send_refs, 1):
            there = lax.rem(row[0] + shift, parts)
            send_ref[here] = (keep_ref[there] + got_ref[there]).astype(send_ref.dtype)


def merge(keep, got, row):
    parts, blocks, step, points = keep[0].shape
    out = [jax.ShapeDtypeStruct((2 * blocks, step, points), jnp.float32)]
    out += [jax.ShapeDtypeStruct((2 * blocks, step, points), jnp.bfloat16)] * (parts - 1)
    return pl.pallas_call(
        merge_kernel,
        in_specs=[pl.BlockSpec(memory_space=pltpu.SMEM)] + [pl.BlockSpec(memory_space=pltpu.VMEM)] * 4,
        out_specs=[pl.BlockSpec(memory_space=pltpu.VMEM)] * parts,
        out_shape=out,
        compiler_params=pltpu.CompilerParams(vmem_limit_bytes=16 * MIB),
        name="merge",
    )(row, *keep, *got)


def route_kernel(slot, here_ref, *refs):
    side = (len(refs) + 1) // 2
    near, out_refs = (here_ref, *refs[: side - 1]), refs[side - 1 :]
    for turn, out_ref in enumerate(out_refs):
        owner = lax.rem(slot[0] + turn, side) * side + slot[1]
        for back, near_ref in enumerate(near):
            out_ref[back] = near_ref[owner]


def route(here, near, slot):
    side = len(near) + 1
    out = jax.ShapeDtypeStruct((side, *here.shape[1:]), here.dtype)
    return pl.pallas_call(
        route_kernel,
        in_specs=[pl.BlockSpec(memory_space=pltpu.SMEM)] + [pl.BlockSpec(memory_space=pltpu.VMEM)] * side,
        out_specs=[pl.BlockSpec(memory_space=pltpu.VMEM)] * side,
        out_shape=[out] * side,
        compiler_params=pltpu.CompilerParams(vmem_limit_bytes=16 * MIB),
        name="route",
    )(slot, here, *near)


def tiles_kernel(pairs, first, slot, *refs):
    *places_refs, out_ref, tile_ref, sem = refs
    side = len(places_refs)

    def copy(within):
        return pltpu.make_async_copy(tile_ref.at[within], out_ref.at[within], sem.at[within])

    def places_of(home, stage_ref):
        turn = lax.rem(slot[0] + side - home // side, side)
        back = lax.rem(slot[1] + side - lax.rem(home, side), side)
        for index, places_ref in enumerate(places_refs):

            @pl.when(turn == index)
            def _():
                stage_ref[...] = places_ref[back].astype(jnp.float32)

    def work(stage_ref):
        for within in range(tile_ref.shape[0]):
            places_of(pairs[0, first[0] + within], stage_ref.at[within, 0])
            places_of(pairs[1, first[0] + within], stage_ref.at[within, 1])
        for within in range(tile_ref.shape[0]):
            tile_ref[within] = tile_of(left_rows(stage_ref[within, 0]), right_rows(stage_ref[within, 1]))
            copy(within).start()
        for within in range(tile_ref.shape[0]):
            copy(within).wait()

    pl.run_scoped(work, pltpu.VMEM((tile_ref.shape[0], 2, *places_refs[0].shape[1:]), jnp.float32))


def tiles(places, pairs, first, slot):
    points = places[0].shape[2]
    shape = (PAIR_GROUP, points, points)
    return pl.pallas_call(
        tiles_kernel,
        in_specs=[pl.BlockSpec(memory_space=pltpu.SMEM)] * 3
        + [pl.BlockSpec(memory_space=pltpu.VMEM)] * len(places),
        out_specs=pl.BlockSpec(memory_space=pl.ANY),
        out_shape=jax.ShapeDtypeStruct(shape, jnp.bfloat16),
        scratch_shapes=[pltpu.VMEM(shape, jnp.bfloat16), pltpu.SemaphoreType.DMA((PAIR_GROUP,))],
        compiler_params=pltpu.CompilerParams(vmem_limit_bytes=16 * MIB),
        cost_estimate=pl.CostEstimate(flops=4_000_000_000, bytes_accessed=2_000_000, transcendentals=0),
        name="tiles",
    )(pairs, first, slot, *places)


def apply_kernel(
    pairs, count, core, got_ref, *refs,
):
    *stacks, out_ref, ens_ref, inc_ref, weighted_ref, field_ref, tiles_ref, ens_sem, inc_sem, tiles_sem = refs
    slot_total, sources, rows, points = ens_ref.shape
    step = inc_ref.shape[2]
    groups = len(stacks)
    lane_chunks = points // LANES
    every = sources * rows

    def ens_copies(slot):
        return [
            pltpu.make_async_copy(
                got_ref.at[slot, :, lane * rows : (lane + 1) * rows, :],
                ens_ref.at[slot, :, :, lane * LANES : (lane + 1) * LANES],
                ens_sem.at[slot, lane],
            )
            for lane in range(lane_chunks)
        ]

    inc_copy = pltpu.make_async_copy(got_ref.at[:, :lane_chunks, rows * lane_chunks :, :], inc_ref, inc_sem)

    def tile_copy(group):
        return pltpu.make_async_copy(stacks[group], tiles_ref.at[group], tiles_sem.at[group])

    inc_copy.start()
    for slot in range(slot_total):
        for copy in ens_copies(slot):
            copy.start()
    for group in range(groups):
        tile_copy(group).start()
    inc_copy.wait()
    for slot in range(slot_total):
        field_ref[slot] = jnp.zeros((every, points), jnp.float32)
        for copy in ens_copies(slot):
            copy.wait()
        for lane in range(lane_chunks):
            here = slice(lane * LANES, (lane + 1) * LANES)
            gain = inc_ref[slot, lane]
            block = ens_ref[slot, :, :, here].reshape(every // step, step, LANES)
            weighted_ref[slot, :, here] = (block * gain[None]).reshape(every, LANES)

    def some(group, row, within, number):
        products = []
        for each in range(number):
            first, second = pairs[0, row + each], pairs[1, row + each]
            tile = tiles_ref[group, within + each]
            to_first = lax.dot_general(
                weighted_ref[second], tile, (((1,), (1,)), ((), ())), preferred_element_type=jnp.float32
            )
            to_second = jnp.dot(weighted_ref[first], tile, preferred_element_type=jnp.float32)
            products += [(first, to_first), (second, to_second)]
        for slot, product in products:
            field_ref[slot] += product

    def turn(group, carry):
        away = core[0] * (groups // 2)
        row = PAIR_GROUP * jnp.where(group < groups // 2, group + away, group - away)
        live = count[0] - row
        pltpu.make_async_copy(stacks[0], tiles_ref.at[group], tiles_sem.at[group]).wait()

        @pl.when(live >= PAIR_GROUP)
        def _():
            some(group, row, 0, PAIR_GROUP)

        @pl.when(live < PAIR_GROUP)
        def _():
            def one(within, inner):
                some(group, row + within, within, 1)
                return inner

            lax.fori_loop(0, jnp.maximum(live, 0), one, 0)

        return carry

    lax.fori_loop(0, groups, turn, 0)

    for slot in range(slot_total):
        product = ens_ref[slot].reshape(every, points).astype(jnp.float32) * field_ref[slot]
        out_ref[slot] = jnp.sum(product.reshape(every // step, step, points), axis=0)


def apply_pairs(got, stacks, pairs, count, core, members, step):
    slot_total, sources, rows, _ = got.shape
    points = stacks[0].shape[2]
    lane_chunks = points // LANES
    every = sources * members * step
    return pl.pallas_call(
        apply_kernel,
        in_specs=[
            pl.BlockSpec(memory_space=pltpu.SMEM),
            pl.BlockSpec(memory_space=pltpu.SMEM),
            pl.BlockSpec(memory_space=pltpu.SMEM),
            pl.BlockSpec(memory_space=pl.ANY),
            *[pl.BlockSpec(memory_space=pl.ANY)] * len(stacks),
        ],
        out_specs=pl.BlockSpec(memory_space=pltpu.VMEM),
        scratch_shapes=[
            pltpu.VMEM((slot_total, sources, members * step, points), jnp.bfloat16),
            pltpu.VMEM((slot_total, lane_chunks, step, LANES), jnp.bfloat16),
            pltpu.VMEM((slot_total, every, points), jnp.bfloat16),
            pltpu.VMEM((slot_total, every, points), jnp.float32),
            pltpu.VMEM((len(stacks), *stacks[0].shape), jnp.bfloat16),
            pltpu.SemaphoreType.DMA((slot_total, lane_chunks)),
            pltpu.SemaphoreType.DMA,
            pltpu.SemaphoreType.DMA((len(stacks),)),
        ],
        out_shape=jax.ShapeDtypeStruct((slot_total, step, points), jnp.float32),
        compiler_params=pltpu.CompilerParams(vmem_limit_bytes=60 * MIB),
        cost_estimate=pl.CostEstimate(flops=9_000_000_000, bytes_accessed=22_000_000, transcendentals=0),
        name="apply",
    )(pairs, count, core, got, *stacks)


def finish_kernel(slots, own_ref, *refs, scale):
    *part_refs, back_ref, out_ref = refs
    total = own_ref[...]
    for part_ref in part_refs:
        total = total + part_ref[...].astype(jnp.float32)
    out_ref[...] = total * scale
    for owner in range(back_ref.shape[0]):
        slot = slots[owner]
        out_ref[slot] = out_ref[slot] + back_ref[owner] * scale


def finish(own, parts, back, slots, scale):
    return pl.pallas_call(
        functools.partial(finish_kernel, scale=scale),
        in_specs=[pl.BlockSpec(memory_space=pltpu.SMEM)] + [pl.BlockSpec(memory_space=pltpu.VMEM)] * (len(parts) + 2),
        out_specs=pl.BlockSpec(memory_space=pltpu.VMEM),
        out_shape=jax.ShapeDtypeStruct(own.shape, jnp.float32),
        compiler_params=pltpu.CompilerParams(vmem_limit_bytes=16 * MIB),
        name="finish",
    )(slots, own, *parts, back)


def per_device(ensemble, increment, coords, sent_slots, pair_list, pair_count):
    blocks, members, levels, points = ensemble.shape
    regions = lax.axis_size("region")
    groups = lax.axis_size("member")
    step = levels // groups
    slots = sent_slots.reshape(-1)
    pairs = pair_list.T
    own = lax.axis_index("member").reshape(1).astype(jnp.int32)
    core, row = own & 1, own >> 1
    rows = groups // 2
    side = math.isqrt(regions)
    region = lax.axis_index("region").astype(jnp.int32)
    slot = jnp.stack([region // side, lax.rem(region, side)])
    big, places = pack(ensemble, increment, coords, slots, own, groups)
    got = lax.all_to_all(
        big.reshape(regions * groups, -1, LANES), ("region", "member"), 0, 0, tiled=True
    ).reshape(regions, groups, -1, LANES)

    near = [
        lax.ppermute(places, "region", [(i, i - i % side + (i + hop) % side) for i in range(regions)])
        for hop in range(1, side)
    ]
    halves = [diag(ensemble, increment, coords, core, rows, 0, blocks // 2)]
    near, halves[0] = lax.optimization_barrier((near, halves[0]))
    own_places, *sent = route(places, near, slot)
    own_places = [own_places] + [
        lax.ppermute(part, "region", [(i, (i + hop * side) % regions) for i in range(regions)])
        for hop, part in enumerate(sent, 1)
    ]
    increment_later, _ = lax.optimization_barrier((increment, sent[0]))
    halves.append(diag(ensemble, increment_later, coords, core, rows, blocks // 2, blocks // 2))
    own_places, halves[1] = lax.optimization_barrier((own_places, halves[1]))

    swap = [(i, i ^ 1) for i in range(groups)]
    merged = merge(
        [keep for keep, _ in halves], [lax.ppermute(send, "member", swap) for _, send in halves], row
    )
    parts = [
        lax.ppermute(part, "member", [(i, (i + 2 * hop) % groups) for i in range(groups)])
        for hop, part in enumerate(merged[1:], 1)
    ]
    share = pairs.shape[1] // 2
    mine = []
    for start in range(0, share, PAIR_GROUP):
        if len(mine) == 1:
            own_places, merged = lax.optimization_barrier((own_places, merged))
        if len(mine) == 2:
            own_places, parts = lax.optimization_barrier((own_places, parts))
        mine.append(tiles(own_places, pairs, core * share + start, slot))
    theirs = [lax.ppermute(stack, "member", swap) for stack in mine]
    got, mine, theirs = in_hbm(got), [in_hbm(x) for x in mine], [in_hbm(x) for x in theirs]
    partial = apply_pairs(got, mine + theirs, pairs, pair_count, core, members, step)
    back = lax.all_to_all(partial, "region", 0, 0, tiled=True)
    return finish(merged[0], parts, back, slots, 1.0 / (members * groups - 1))


def solution(mesh):
    in_specs = (
        P("region", "member", None, None),
        P("region", None, None),
        P("region", None, None),
        P("region", None, None),
        P("region", None),
        P("region"),
    )
    out_specs = P("region", "member", None)
    return jax.shard_map(
        per_device, mesh=mesh, in_specs=in_specs, out_specs=out_specs, check_vma=False
    )
```

```python
import functools

import jax
import jax.numpy as jnp
from jax import lax
from jax.experimental import pallas as pl
from jax.experimental.pallas import tpu as pltpu
from jax.sharding import PartitionSpec as P

LANES = 128
PAIR_GROUP = 4
MIB = 1024 * 1024
UNIT = 12.0**-0.2
UNIT2 = UNIT * UNIT
LEAST = UNIT2 * 2.0**-12


def select_kernel(slots, coords_ref, places_ref, sem):
    total = places_ref.shape[0]

    def copy(owner):
        return pltpu.make_async_copy(coords_ref.at[slots[owner]], places_ref.at[owner], sem.at[owner])

    for owner in range(total):
        copy(owner).start()
    for owner in range(total):
        copy(owner).wait()


def select(coords, slots):
    total = slots.shape[0]
    return pl.pallas_call(
        select_kernel,
        in_specs=[pl.BlockSpec(memory_space=pltpu.SMEM), pl.BlockSpec(memory_space=pl.ANY)],
        out_specs=pl.BlockSpec(memory_space=pl.ANY),
        out_shape=jax.ShapeDtypeStruct((total, *coords.shape[1:]), coords.dtype),
        scratch_shapes=[pltpu.SemaphoreType.DMA((total,))],
        compiler_params=pltpu.CompilerParams(vmem_limit_bytes=60 * MIB),
        name="select",
    )(slots, coords)


def pack_kernel(slots, own, ens_ref, inc_ref, big_ref, ens_buf, inc_buf, out_buf, in_sem, inc_sem, out_sem):
    total, members, levels, points = ens_buf.shape
    parts = out_buf.shape[1]
    step = levels // parts
    lane_chunks = points // LANES

    def ens_copy(owner):
        return pltpu.make_async_copy(ens_ref.at[slots[owner]], ens_buf.at[owner], in_sem.at[owner])

    def inc_copy(owner):
        return pltpu.make_async_copy(inc_ref.at[slots[owner]], inc_buf.at[owner], inc_sem.at[owner])

    def out_copy(owner):
        return pltpu.make_async_copy(out_buf.at[owner], big_ref.at[owner], out_sem.at[owner])

    for owner in range(total):
        ens_copy(owner).start()
        inc_copy(owner).start()
    chunk = pl.multiple_of(lax.rem(own[0], lane_chunks) * LANES, LANES)
    for owner in range(total):
        ens_copy(owner).wait()
        inc_copy(owner).wait()
        for part in range(parts):
            here = slice(part * step, (part + 1) * step)
            for lane in range(lane_chunks):
                out_buf[owner, part, lane * members * step : (lane + 1) * members * step, :] = ens_buf[
                    owner, :, here, lane * LANES : (lane + 1) * LANES
                ].reshape(members * step, LANES)
            out_buf[owner, part, members * step * lane_chunks :, :] = inc_buf[owner, here, pl.ds(chunk, LANES)]
        out_copy(owner).start()
    for owner in range(total):
        out_copy(owner).wait()


def pack(ensemble, increment, slots, own, parts):
    blocks, members, levels, points = ensemble.shape
    total = slots.shape[0]
    step = levels // parts
    rows = members * step * (points // LANES) + step
    return pl.pallas_call(
        pack_kernel,
        in_specs=[
            pl.BlockSpec(memory_space=pltpu.SMEM),
            pl.BlockSpec(memory_space=pltpu.SMEM),
            pl.BlockSpec(memory_space=pl.ANY),
            pl.BlockSpec(memory_space=pl.ANY),
        ],
        out_specs=pl.BlockSpec(memory_space=pl.ANY),
        out_shape=jax.ShapeDtypeStruct((total, parts, rows, LANES), ensemble.dtype),
        scratch_shapes=[
            pltpu.VMEM((total, members, levels, points), ensemble.dtype),
            pltpu.VMEM((total, levels, points), increment.dtype),
            pltpu.VMEM((total, parts, rows, LANES), ensemble.dtype),
            pltpu.SemaphoreType.DMA((total,)),
            pltpu.SemaphoreType.DMA((total,)),
            pltpu.SemaphoreType.DMA((total,)),
        ],
        compiler_params=pltpu.CompilerParams(vmem_limit_bytes=60 * MIB),
        name="pack",
    )(slots, own, ensemble, increment)


def in_hbm(value):
    return pltpu.with_memory_space_constraint(value, pltpu.HBM)


def three_parts(value):
    first = value.astype(jnp.bfloat16).astype(jnp.float32)
    rest = value - first
    second = rest.astype(jnp.bfloat16).astype(jnp.float32)
    return [first, second, rest - second]


def left_rows(places):
    east, north = places[0:1], places[1:2]
    one = jnp.ones_like(east)
    norm = UNIT2 * (east * east + north * north)
    rows = three_parts((-2.0 * UNIT2) * east) + three_parts((-2.0 * UNIT2) * north) + three_parts(norm)
    rows = rows + [one] * 3 + [jnp.zeros_like(east)] * 4
    return jnp.concatenate(rows, axis=0).astype(jnp.bfloat16)


def right_rows(places):
    east, north = places[0:1], places[1:2]
    one = jnp.ones_like(east)
    norm = UNIT2 * (east * east + north * north)
    rows = [east] * 3 + [north] * 3 + [one] * 3 + three_parts(norm) + [jnp.zeros_like(east)] * 4
    return jnp.concatenate(rows, axis=0).astype(jnp.bfloat16)


def tile_of(left, right):
    squared = lax.dot_general(left, right, (((0,), (0,)), ((), ())), preferred_element_type=jnp.float32)
    squared = jnp.maximum(squared, LEAST)
    inverse = lax.rsqrt(squared)
    z = squared * inverse
    outer = jnp.maximum(2.0 * UNIT - z, 0.0)
    inner = jnp.maximum(UNIT - z, 0.0)
    outer2 = outer * outer
    inner2 = inner * inner
    shifted = z + 2.0 * UNIT
    first = (outer2 * outer2) * (z * shifted - 0.5 * UNIT2)
    second = (inner2 * inner2) * (inner * shifted)
    return ((first + 4.0 * second) * inverse).astype(jnp.bfloat16)


def diag_kernel(core, ens_ref, inc_ref, coords_ref, keep_ref, send_ref, sum_ref):
    members, levels, points = ens_ref.shape[1:]
    parts, _, step, _ = keep_ref.shape
    rows = members * levels
    half = points // 2
    places = coords_ref[0].astype(jnp.float32)
    left, right = left_rows(places), right_rows(places)
    upper = tile_of(left[:, :half], right)
    lower = tile_of(left[:, half:], right[:, half:])
    weighted = (ens_ref[0] * inc_ref[0][None]).reshape(rows, points)
    near, far = weighted[:, :half], weighted[:, half:]
    field_near = jnp.dot(near, upper[:, :half], preferred_element_type=jnp.float32) + lax.dot_general(
        far, upper[:, half:], (((1,), (1,)), ((), ())), preferred_element_type=jnp.float32
    )
    field_far = jnp.dot(near, upper[:, half:], preferred_element_type=jnp.float32) + jnp.dot(
        far, lower, preferred_element_type=jnp.float32
    )
    block = ens_ref[0].astype(jnp.float32)
    sum_ref[:, :half] = jnp.sum(block[:, :, :half] * field_near.reshape(members, levels, half), axis=0)
    sum_ref[:, half:] = jnp.sum(block[:, :, half:] * field_far.reshape(members, levels, half), axis=0)
    for part in range(parts):
        mine = pl.multiple_of((2 * part + core[0]) * step, step)
        other = pl.multiple_of((2 * part + 1 - core[0]) * step, step)
        keep_ref[part, 0] = sum_ref[pl.ds(mine, step), :]
        send_ref[part, 0] = sum_ref[pl.ds(other, step), :]


def diag(ensemble, increment, coords, core, parts):
    blocks, members, levels, points = ensemble.shape
    step = levels // (2 * parts)
    out = jax.ShapeDtypeStruct((parts, blocks, step, points), jnp.float32)
    return pl.pallas_call(
        diag_kernel,
        grid_spec=pltpu.PrefetchScalarGridSpec(
            num_scalar_prefetch=1,
            grid=(blocks,),
            in_specs=[
                pl.BlockSpec((1, members, levels, points), lambda b, c: (b, 0, 0, 0)),
                pl.BlockSpec((1, levels, points), lambda b, c: (b, 0, 0)),
                pl.BlockSpec((1, 2, points), lambda b, c: (b, 0, 0)),
            ],
            out_specs=[pl.BlockSpec((parts, 1, step, points), lambda b, c: (0, b, 0, 0))] * 2,
            scratch_shapes=[pltpu.VMEM((levels, points), jnp.float32)],
        ),
        out_shape=[out, out],
        compiler_params=pltpu.CompilerParams(vmem_limit_bytes=60 * MIB),
        cost_estimate=pl.CostEstimate(flops=20_000_000_000, bytes_accessed=8_000_000, transcendentals=0),
        name="diag",
    )(core, ensemble, increment, coords)


def merge_kernel(row, keep_ref, got_ref, own_ref, *send_refs):
    parts = keep_ref.shape[0]
    own_ref[...] = keep_ref[row[0]] + got_ref[row[0]]
    for shift, send_ref in enumerate(send_refs, 1):
        there = lax.rem(row[0] + shift, parts)
        send_ref[...] = (keep_ref[there] + got_ref[there]).astype(send_ref.dtype)


def merge(keep, got, row):
    parts = keep.shape[0]
    out = [jax.ShapeDtypeStruct(keep.shape[1:], jnp.float32)]
    out += [jax.ShapeDtypeStruct(keep.shape[1:], jnp.bfloat16)] * (parts - 1)
    return pl.pallas_call(
        merge_kernel,
        in_specs=[pl.BlockSpec(memory_space=pltpu.SMEM)] + [pl.BlockSpec(memory_space=pltpu.VMEM)] * 2,
        out_specs=[pl.BlockSpec(memory_space=pltpu.VMEM)] * parts,
        out_shape=out,
        compiler_params=pltpu.CompilerParams(vmem_limit_bytes=16 * MIB),
        name="merge",
    )(row, keep, got)


def tiles_kernel(pairs, first, places_ref, out_ref, tile_ref, sem):
    def copy(within):
        return pltpu.make_async_copy(tile_ref.at[within], out_ref.at[within], sem.at[within])

    for within in range(tile_ref.shape[0]):
        index = first[0] + within
        left = left_rows(places_ref[pairs[0, index]].astype(jnp.float32))
        right = right_rows(places_ref[pairs[1, index]].astype(jnp.float32))
        tile_ref[within] = tile_of(left, right)
        copy(within).start()
    for within in range(tile_ref.shape[0]):
        copy(within).wait()


def tiles(places, pairs, first):
    shape = (PAIR_GROUP, places.shape[2], places.shape[2])
    return pl.pallas_call(
        tiles_kernel,
        in_specs=[
            pl.BlockSpec(memory_space=pltpu.SMEM),
            pl.BlockSpec(memory_space=pltpu.SMEM),
            pl.BlockSpec(memory_space=pltpu.VMEM),
        ],
        out_specs=pl.BlockSpec(memory_space=pl.ANY),
        out_shape=pltpu.HBM(shape, jnp.bfloat16),
        scratch_shapes=[pltpu.VMEM(shape, jnp.bfloat16), pltpu.SemaphoreType.DMA((PAIR_GROUP,))],
        compiler_params=pltpu.CompilerParams(vmem_limit_bytes=60 * MIB),
        cost_estimate=pl.CostEstimate(flops=4_000_000_000, bytes_accessed=2_000_000, transcendentals=0),
        name="tiles",
    )(pairs, first, places)


def apply_kernel(
    pairs, count, core, got_ref, *refs,
):
    *stacks, out_ref, ens_ref, inc_ref, weighted_ref, field_ref, tiles_ref, ens_sem, inc_sem, tiles_sem = refs
    slot_total, sources, rows, points = ens_ref.shape
    step = inc_ref.shape[2]
    groups = len(stacks)
    lane_chunks = points // LANES
    every = sources * rows

    def ens_copies(slot):
        return [
            pltpu.make_async_copy(
                got_ref.at[slot, :, lane * rows : (lane + 1) * rows, :],
                ens_ref.at[slot, :, :, lane * LANES : (lane + 1) * LANES],
                ens_sem.at[slot, lane],
            )
            for lane in range(lane_chunks)
        ]

    inc_copy = pltpu.make_async_copy(got_ref.at[:, :lane_chunks, rows * lane_chunks :, :], inc_ref, inc_sem)

    def tile_copy(group):
        return pltpu.make_async_copy(stacks[group], tiles_ref.at[group], tiles_sem.at[group])

    inc_copy.start()
    for slot in range(slot_total):
        for copy in ens_copies(slot):
            copy.start()
    for group in range(groups):
        tile_copy(group).start()
    inc_copy.wait()
    for slot in range(slot_total):
        field_ref[slot] = jnp.zeros((every, points), jnp.float32)
        for copy in ens_copies(slot):
            copy.wait()
        for lane in range(lane_chunks):
            here = slice(lane * LANES, (lane + 1) * LANES)
            gain = inc_ref[slot, lane]
            block = ens_ref[slot, :, :, here].reshape(every // step, step, LANES)
            weighted_ref[slot, :, here] = (block * gain[None]).reshape(every, LANES)

    def some(group, row, within, number):
        products = []
        for each in range(number):
            first, second = pairs[0, row + each], pairs[1, row + each]
            tile = tiles_ref[group, within + each]
            to_first = lax.dot_general(
                weighted_ref[second], tile, (((1,), (1,)), ((), ())), preferred_element_type=jnp.float32
            )
            to_second = jnp.dot(weighted_ref[first], tile, preferred_element_type=jnp.float32)
            products += [(first, to_first), (second, to_second)]
        for slot, product in products:
            field_ref[slot] += product

    def turn(group, carry):
        away = core[0] * (groups // 2)
        row = PAIR_GROUP * jnp.where(group < groups // 2, group + away, group - away)
        live = count[0] - row
        pltpu.make_async_copy(stacks[0], tiles_ref.at[group], tiles_sem.at[group]).wait()

        @pl.when(live >= PAIR_GROUP)
        def _():
            some(group, row, 0, PAIR_GROUP)

        @pl.when(live < PAIR_GROUP)
        def _():
            def one(within, inner):
                some(group, row + within, within, 1)
                return inner

            lax.fori_loop(0, jnp.maximum(live, 0), one, 0)

        return carry

    lax.fori_loop(0, groups, turn, 0)

    for slot in range(slot_total):
        product = ens_ref[slot].reshape(every, points).astype(jnp.float32) * field_ref[slot]
        out_ref[slot] = jnp.sum(product.reshape(every // step, step, points), axis=0)


def apply_pairs(got, stacks, pairs, count, core, members, step):
    slot_total, sources, rows, _ = got.shape
    points = stacks[0].shape[2]
    lane_chunks = points // LANES
    every = sources * members * step
    return pl.pallas_call(
        apply_kernel,
        in_specs=[
            pl.BlockSpec(memory_space=pltpu.SMEM),
            pl.BlockSpec(memory_space=pltpu.SMEM),
            pl.BlockSpec(memory_space=pltpu.SMEM),
            pl.BlockSpec(memory_space=pl.ANY),
            *[pl.BlockSpec(memory_space=pl.ANY)] * len(stacks),
        ],
        out_specs=pl.BlockSpec(memory_space=pltpu.VMEM),
        scratch_shapes=[
            pltpu.VMEM((slot_total, sources, members * step, points), jnp.bfloat16),
            pltpu.VMEM((slot_total, lane_chunks, step, LANES), jnp.bfloat16),
            pltpu.VMEM((slot_total, every, points), jnp.bfloat16),
            pltpu.VMEM((slot_total, every, points), jnp.float32),
            pltpu.VMEM((len(stacks), *stacks[0].shape), jnp.bfloat16),
            pltpu.SemaphoreType.DMA((slot_total, lane_chunks)),
            pltpu.SemaphoreType.DMA,
            pltpu.SemaphoreType.DMA((len(stacks),)),
        ],
        out_shape=jax.ShapeDtypeStruct((slot_total, step, points), jnp.float32),
        compiler_params=pltpu.CompilerParams(vmem_limit_bytes=60 * MIB),
        cost_estimate=pl.CostEstimate(flops=9_000_000_000, bytes_accessed=22_000_000, transcendentals=0),
        name="apply",
    )(pairs, count, core, got, *stacks)


def finish_kernel(slots, own_ref, *refs, scale):
    *part_refs, back_ref, out_ref = refs
    total = own_ref[...]
    for part_ref in part_refs:
        total = total + part_ref[...].astype(jnp.float32)
    out_ref[...] = total * scale
    for owner in range(back_ref.shape[0]):
        slot = slots[owner]
        out_ref[slot] = out_ref[slot] + back_ref[owner] * scale


def finish(own, parts, back, slots, scale):
    return pl.pallas_call(
        functools.partial(finish_kernel, scale=scale),
        in_specs=[pl.BlockSpec(memory_space=pltpu.SMEM)] + [pl.BlockSpec(memory_space=pltpu.VMEM)] * (len(parts) + 2),
        out_specs=pl.BlockSpec(memory_space=pltpu.VMEM),
        out_shape=jax.ShapeDtypeStruct(own.shape, jnp.float32),
        compiler_params=pltpu.CompilerParams(vmem_limit_bytes=16 * MIB),
        name="finish",
    )(slots, own, *parts, back)


def per_device(ensemble, increment, coords, sent_slots, pair_list, pair_count):
    blocks, members, levels, points = ensemble.shape
    regions = lax.axis_size("region")
    groups = lax.axis_size("member")
    step = levels // groups
    slots = sent_slots.reshape(-1)
    pairs = pair_list.T
    own = lax.axis_index("member").reshape(1).astype(jnp.int32)
    places = select(coords, slots)
    own_places = lax.all_to_all(places, "region", 0, 0, tiled=True)
    big = pack(ensemble, increment, slots, own, groups)
    big, own_places = lax.optimization_barrier((big, own_places))
    got = lax.all_to_all(
        big.reshape(regions * groups, -1, LANES), ("region", "member"), 0, 0, tiled=True
    ).reshape(regions, groups, -1, LANES)
    swap = [(i, i ^ 1) for i in range(groups)]
    core, row = own & 1, own >> 1
    rows = groups // 2
    share = pairs.shape[1] // 2
    keep, send = diag(ensemble, increment, coords, core, rows)
    merged = merge(keep, lax.ppermute(send, "member", swap), row)
    own_places, _ = lax.optimization_barrier((own_places, send))
    mine = [tiles(own_places, pairs, core * share + start) for start in range(0, share, PAIR_GROUP)]
    theirs = [lax.ppermute(stack, "member", swap) for stack in mine]
    got, merged = lax.optimization_barrier((got, merged))
    stacks = [in_hbm(stack) for stack in mine + theirs]
    partial = apply_pairs(in_hbm(got), stacks, pairs, pair_count, core, members, step)
    partial, merged = lax.optimization_barrier((partial, merged))
    parts = [
        lax.ppermute(part, "member", [(i, (i + 2 * hop) % groups) for i in range(groups)])
        for hop, part in enumerate(merged[1:], 1)
    ]
    back = lax.all_to_all(partial, "region", 0, 0, tiled=True)
    return finish(merged[0], parts, back, slots, 1.0 / (members * groups - 1))


def solution(mesh):
    in_specs = (
        P("region", "member", None, None),
        P("region", None, None),
        P("region", None, None),
        P("region", None, None),
        P("region", None),
        P("region"),
    )
    out_specs = P("region", "member", None)
    return jax.shard_map(
        per_device, mesh=mesh, in_specs=in_specs, out_specs=out_specs, check_vma=False
    )
```

```python
import functools

import jax
import jax.numpy as jnp
from jax import lax
from jax.experimental import pallas as pl
from jax.experimental.pallas import tpu as pltpu
from jax.sharding import PartitionSpec as P

LANES = 128
PAIR_GROUP = 4
AFTER_MERGE = 1
AFTER_TOTAL = 3
MIB = 1024 * 1024
UNIT = 12.0**-0.2
UNIT2 = UNIT * UNIT
LEAST = UNIT2 * 2.0**-12


def select_kernel(slots, coords_ref, places_ref, sem):
    total = places_ref.shape[0]

    def copy(owner):
        return pltpu.make_async_copy(coords_ref.at[slots[owner]], places_ref.at[owner], sem.at[owner])

    for owner in range(total):
        copy(owner).start()
    for owner in range(total):
        copy(owner).wait()


def select(coords, slots):
    total = slots.shape[0]
    return pl.pallas_call(
        select_kernel,
        in_specs=[pl.BlockSpec(memory_space=pltpu.SMEM), pl.BlockSpec(memory_space=pl.ANY)],
        out_specs=pl.BlockSpec(memory_space=pl.ANY),
        out_shape=jax.ShapeDtypeStruct((total, *coords.shape[1:]), coords.dtype),
        scratch_shapes=[pltpu.SemaphoreType.DMA((total,))],
        compiler_params=pltpu.CompilerParams(vmem_limit_bytes=60 * MIB),
        name="select",
    )(slots, coords)


def pack_kernel(slots, own, ens_ref, inc_ref, big_ref, ens_buf, inc_buf, out_buf, in_sem, inc_sem, out_sem):
    total, members, levels, points = ens_buf.shape
    parts = out_buf.shape[1]
    step = levels // parts
    lane_chunks = points // LANES

    def ens_copy(owner):
        return pltpu.make_async_copy(ens_ref.at[slots[owner]], ens_buf.at[owner], in_sem.at[owner])

    def inc_copy(owner):
        return pltpu.make_async_copy(inc_ref.at[slots[owner]], inc_buf.at[owner], inc_sem.at[owner])

    def out_copy(owner):
        return pltpu.make_async_copy(out_buf.at[owner], big_ref.at[owner], out_sem.at[owner])

    for owner in range(total):
        ens_copy(owner).start()
        inc_copy(owner).start()
    chunk = pl.multiple_of(lax.rem(own[0], lane_chunks) * LANES, LANES)
    for owner in range(total):
        ens_copy(owner).wait()
        inc_copy(owner).wait()
        for part in range(parts):
            here = slice(part * step, (part + 1) * step)
            for lane in range(lane_chunks):
                out_buf[owner, part, lane * members * step : (lane + 1) * members * step, :] = ens_buf[
                    owner, :, here, lane * LANES : (lane + 1) * LANES
                ].reshape(members * step, LANES)
            out_buf[owner, part, members * step * lane_chunks :, :] = inc_buf[owner, here, pl.ds(chunk, LANES)]
        out_copy(owner).start()
    for owner in range(total):
        out_copy(owner).wait()


def pack(ensemble, increment, slots, own, parts):
    blocks, members, levels, points = ensemble.shape
    total = slots.shape[0]
    step = levels // parts
    rows = members * step * (points // LANES) + step
    return pl.pallas_call(
        pack_kernel,
        in_specs=[
            pl.BlockSpec(memory_space=pltpu.SMEM),
            pl.BlockSpec(memory_space=pltpu.SMEM),
            pl.BlockSpec(memory_space=pl.ANY),
            pl.BlockSpec(memory_space=pl.ANY),
        ],
        out_specs=pl.BlockSpec(memory_space=pl.ANY),
        out_shape=jax.ShapeDtypeStruct((total, parts, rows, LANES), ensemble.dtype),
        scratch_shapes=[
            pltpu.VMEM((total, members, levels, points), ensemble.dtype),
            pltpu.VMEM((total, levels, points), increment.dtype),
            pltpu.VMEM((total, parts, rows, LANES), ensemble.dtype),
            pltpu.SemaphoreType.DMA((total,)),
            pltpu.SemaphoreType.DMA((total,)),
            pltpu.SemaphoreType.DMA((total,)),
        ],
        compiler_params=pltpu.CompilerParams(vmem_limit_bytes=60 * MIB),
        name="pack",
    )(slots, own, ensemble, increment)


def in_hbm(value):
    return pltpu.with_memory_space_constraint(value, pltpu.HBM)


def three_parts(value):
    first = value.astype(jnp.bfloat16).astype(jnp.float32)
    rest = value - first
    second = rest.astype(jnp.bfloat16).astype(jnp.float32)
    return [first, second, rest - second]


def left_rows(places):
    east, north = places[0:1], places[1:2]
    one = jnp.ones_like(east)
    norm = UNIT2 * (east * east + north * north)
    rows = three_parts((-2.0 * UNIT2) * east) + three_parts((-2.0 * UNIT2) * north) + three_parts(norm)
    rows = rows + [one] * 3 + [jnp.zeros_like(east)] * 4
    return jnp.concatenate(rows, axis=0).astype(jnp.bfloat16)


def right_rows(places):
    east, north = places[0:1], places[1:2]
    one = jnp.ones_like(east)
    norm = UNIT2 * (east * east + north * north)
    rows = [east] * 3 + [north] * 3 + [one] * 3 + three_parts(norm) + [jnp.zeros_like(east)] * 4
    return jnp.concatenate(rows, axis=0).astype(jnp.bfloat16)


def tile_of(left, right):
    squared = lax.dot_general(left, right, (((0,), (0,)), ((), ())), preferred_element_type=jnp.float32)
    squared = jnp.maximum(squared, LEAST)
    inverse = lax.rsqrt(squared)
    z = squared * inverse
    outer = jnp.maximum(2.0 * UNIT - z, 0.0)
    inner = jnp.maximum(UNIT - z, 0.0)
    outer2 = outer * outer
    inner2 = inner * inner
    shifted = z + 2.0 * UNIT
    first = (outer2 * outer2) * (z * shifted - 0.5 * UNIT2)
    second = (inner2 * inner2) * (inner * shifted)
    return ((first + 4.0 * second) * inverse).astype(jnp.bfloat16)


def diag_kernel(core, ens_ref, inc_ref, coords_ref, keep_ref, send_ref, sum_ref):
    members, levels, points = ens_ref.shape[1:]
    parts, _, step, _ = keep_ref.shape
    rows = members * levels
    half = points // 2
    places = coords_ref[0].astype(jnp.float32)
    left, right = left_rows(places), right_rows(places)
    upper = tile_of(left[:, :half], right)
    lower = tile_of(left[:, half:], right[:, half:])
    weighted = (ens_ref[0] * inc_ref[0][None]).reshape(rows, points)
    near, far = weighted[:, :half], weighted[:, half:]
    field_near = jnp.dot(near, upper[:, :half], preferred_element_type=jnp.float32) + lax.dot_general(
        far, upper[:, half:], (((1,), (1,)), ((), ())), preferred_element_type=jnp.float32
    )
    field_far = jnp.dot(near, upper[:, half:], preferred_element_type=jnp.float32) + jnp.dot(
        far, lower, preferred_element_type=jnp.float32
    )
    block = ens_ref[0].astype(jnp.float32)
    sum_ref[:, :half] = jnp.sum(block[:, :, :half] * field_near.reshape(members, levels, half), axis=0)
    sum_ref[:, half:] = jnp.sum(block[:, :, half:] * field_far.reshape(members, levels, half), axis=0)
    for part in range(parts):
        mine = pl.multiple_of((2 * part + core[0]) * step, step)
        other = pl.multiple_of((2 * part + 1 - core[0]) * step, step)
        keep_ref[part, 0] = sum_ref[pl.ds(mine, step), :]
        send_ref[part, 0] = sum_ref[pl.ds(other, step), :]


def diag(ensemble, increment, coords, core, parts):
    blocks, members, levels, points = ensemble.shape
    step = levels // (2 * parts)
    out = jax.ShapeDtypeStruct((parts, blocks, step, points), jnp.float32)
    return pl.pallas_call(
        diag_kernel,
        grid_spec=pltpu.PrefetchScalarGridSpec(
            num_scalar_prefetch=1,
            grid=(blocks,),
            in_specs=[
                pl.BlockSpec((1, members, levels, points), lambda b, c: (b, 0, 0, 0)),
                pl.BlockSpec((1, levels, points), lambda b, c: (b, 0, 0)),
                pl.BlockSpec((1, 2, points), lambda b, c: (b, 0, 0)),
            ],
            out_specs=[pl.BlockSpec((parts, 1, step, points), lambda b, c: (0, b, 0, 0))] * 2,
            scratch_shapes=[pltpu.VMEM((levels, points), jnp.float32)],
        ),
        out_shape=[out, out],
        compiler_params=pltpu.CompilerParams(vmem_limit_bytes=60 * MIB),
        cost_estimate=pl.CostEstimate(flops=20_000_000_000, bytes_accessed=8_000_000, transcendentals=0),
        name="diag",
    )(core, ensemble, increment, coords)


def merge_kernel(row, keep_ref, got_ref, own_ref, *send_refs):
    parts = keep_ref.shape[0]
    own_ref[...] = keep_ref[row[0]] + got_ref[row[0]]
    for shift, send_ref in enumerate(send_refs, 1):
        there = lax.rem(row[0] + shift, parts)
        send_ref[...] = (keep_ref[there] + got_ref[there]).astype(send_ref.dtype)


def merge(keep, got, row):
    parts = keep.shape[0]
    out = [jax.ShapeDtypeStruct(keep.shape[1:], jnp.float32)]
    out += [jax.ShapeDtypeStruct(keep.shape[1:], jnp.bfloat16)] * (parts - 1)
    return pl.pallas_call(
        merge_kernel,
        in_specs=[pl.BlockSpec(memory_space=pltpu.SMEM)] + [pl.BlockSpec(memory_space=pltpu.VMEM)] * 2,
        out_specs=[pl.BlockSpec(memory_space=pltpu.VMEM)] * parts,
        out_shape=out,
        compiler_params=pltpu.CompilerParams(vmem_limit_bytes=16 * MIB),
        name="merge",
    )(row, keep, got)


def total_kernel(own_ref, *refs):
    *part_refs, out_ref = refs
    total = own_ref[...]
    for part_ref in part_refs:
        total = total + part_ref[...].astype(jnp.float32)
    out_ref[...] = total


def total_of(own, parts):
    return pl.pallas_call(
        total_kernel,
        in_specs=[pl.BlockSpec(memory_space=pltpu.VMEM)] * (len(parts) + 1),
        out_specs=pl.BlockSpec(memory_space=pltpu.VMEM),
        out_shape=jax.ShapeDtypeStruct(own.shape, jnp.float32),
        compiler_params=pltpu.CompilerParams(vmem_limit_bytes=16 * MIB),
        name="total",
    )(own, *parts)


def tiles_kernel(pairs, first, places_ref, out_ref, tile_ref, sem):
    def copy(within):
        return pltpu.make_async_copy(tile_ref.at[within], out_ref.at[within], sem.at[within])

    for within in range(tile_ref.shape[0]):
        index = first[0] + within
        left = left_rows(places_ref[pairs[0, index]].astype(jnp.float32))
        right = right_rows(places_ref[pairs[1, index]].astype(jnp.float32))
        tile_ref[within] = tile_of(left, right)
        copy(within).start()
    for within in range(tile_ref.shape[0]):
        copy(within).wait()


def tiles(places, pairs, first):
    shape = (PAIR_GROUP, places.shape[2], places.shape[2])
    return pl.pallas_call(
        tiles_kernel,
        in_specs=[
            pl.BlockSpec(memory_space=pltpu.SMEM),
            pl.BlockSpec(memory_space=pltpu.SMEM),
            pl.BlockSpec(memory_space=pltpu.VMEM),
        ],
        out_specs=pl.BlockSpec(memory_space=pl.ANY),
        out_shape=pltpu.HBM(shape, jnp.bfloat16),
        scratch_shapes=[pltpu.VMEM(shape, jnp.bfloat16), pltpu.SemaphoreType.DMA((PAIR_GROUP,))],
        compiler_params=pltpu.CompilerParams(vmem_limit_bytes=60 * MIB),
        cost_estimate=pl.CostEstimate(flops=4_000_000_000, bytes_accessed=2_000_000, transcendentals=0),
        name="tiles",
    )(pairs, first, places)


def apply_kernel(
    pairs, count, core, got_ref, *refs,
):
    *stacks, out_ref, ens_ref, inc_ref, weighted_ref, field_ref, tiles_ref, ens_sem, inc_sem, tiles_sem = refs
    slot_total, sources, rows, points = ens_ref.shape
    step = inc_ref.shape[2]
    groups = len(stacks)
    lane_chunks = points // LANES
    every = sources * rows

    def ens_copies(slot):
        return [
            pltpu.make_async_copy(
                got_ref.at[slot, :, lane * rows : (lane + 1) * rows, :],
                ens_ref.at[slot, :, :, lane * LANES : (lane + 1) * LANES],
                ens_sem.at[slot, lane],
            )
            for lane in range(lane_chunks)
        ]

    inc_copy = pltpu.make_async_copy(got_ref.at[:, :lane_chunks, rows * lane_chunks :, :], inc_ref, inc_sem)

    def tile_copy(group):
        return pltpu.make_async_copy(stacks[group], tiles_ref.at[group], tiles_sem.at[group])

    inc_copy.start()
    for slot in range(slot_total):
        for copy in ens_copies(slot):
            copy.start()
    for group in range(groups):
        tile_copy(group).start()
    inc_copy.wait()
    for slot in range(slot_total):
        field_ref[slot] = jnp.zeros((every, points), jnp.float32)
        for copy in ens_copies(slot):
            copy.wait()
        for lane in range(lane_chunks):
            here = slice(lane * LANES, (lane + 1) * LANES)
            gain = inc_ref[slot, lane]
            block = ens_ref[slot, :, :, here].reshape(every // step, step, LANES)
            weighted_ref[slot, :, here] = (block * gain[None]).reshape(every, LANES)

    def some(group, row, within, number):
        products = []
        for each in range(number):
            first, second = pairs[0, row + each], pairs[1, row + each]
            tile = tiles_ref[group, within + each]
            to_first = lax.dot_general(
                weighted_ref[second], tile, (((1,), (1,)), ((), ())), preferred_element_type=jnp.float32
            )
            to_second = jnp.dot(weighted_ref[first], tile, preferred_element_type=jnp.float32)
            products += [(first, to_first), (second, to_second)]
        for slot, product in products:
            field_ref[slot] += product

    def turn(group, carry):
        away = core[0] * (groups // 2)
        row = PAIR_GROUP * jnp.where(group < groups // 2, group + away, group - away)
        live = count[0] - row
        pltpu.make_async_copy(stacks[0], tiles_ref.at[group], tiles_sem.at[group]).wait()

        @pl.when(live >= PAIR_GROUP)
        def _():
            some(group, row, 0, PAIR_GROUP)

        @pl.when(live < PAIR_GROUP)
        def _():
            def one(within, inner):
                some(group, row + within, within, 1)
                return inner

            lax.fori_loop(0, jnp.maximum(live, 0), one, 0)

        return carry

    lax.fori_loop(0, groups, turn, 0)

    for slot in range(slot_total):
        product = ens_ref[slot].reshape(every, points).astype(jnp.float32) * field_ref[slot]
        out_ref[slot] = jnp.sum(product.reshape(every // step, step, points), axis=0)


def apply_pairs(got, stacks, pairs, count, core, members, step):
    slot_total, sources, rows, _ = got.shape
    points = stacks[0].shape[2]
    lane_chunks = points // LANES
    every = sources * members * step
    return pl.pallas_call(
        apply_kernel,
        in_specs=[
            pl.BlockSpec(memory_space=pltpu.SMEM),
            pl.BlockSpec(memory_space=pltpu.SMEM),
            pl.BlockSpec(memory_space=pltpu.SMEM),
            pl.BlockSpec(memory_space=pl.ANY),
            *[pl.BlockSpec(memory_space=pl.ANY)] * len(stacks),
        ],
        out_specs=pl.BlockSpec(memory_space=pltpu.VMEM),
        scratch_shapes=[
            pltpu.VMEM((slot_total, sources, members * step, points), jnp.bfloat16),
            pltpu.VMEM((slot_total, lane_chunks, step, LANES), jnp.bfloat16),
            pltpu.VMEM((slot_total, every, points), jnp.bfloat16),
            pltpu.VMEM((slot_total, every, points), jnp.float32),
            pltpu.VMEM((len(stacks), *stacks[0].shape), jnp.bfloat16),
            pltpu.SemaphoreType.DMA((slot_total, lane_chunks)),
            pltpu.SemaphoreType.DMA,
            pltpu.SemaphoreType.DMA((len(stacks),)),
        ],
        out_shape=jax.ShapeDtypeStruct((slot_total, step, points), jnp.float32),
        compiler_params=pltpu.CompilerParams(vmem_limit_bytes=60 * MIB),
        cost_estimate=pl.CostEstimate(flops=9_000_000_000, bytes_accessed=22_000_000, transcendentals=0),
        name="apply",
    )(pairs, count, core, got, *stacks)


def finish_kernel(slots, own_ref, back_ref, out_ref, *, scale):
    out_ref[...] = own_ref[...] * scale
    for owner in range(back_ref.shape[0]):
        slot = slots[owner]
        out_ref[slot] = out_ref[slot] + back_ref[owner] * scale


def finish(own, back, slots, scale):
    return pl.pallas_call(
        functools.partial(finish_kernel, scale=scale),
        in_specs=[
            pl.BlockSpec(memory_space=pltpu.SMEM),
            pl.BlockSpec(memory_space=pltpu.VMEM),
            pl.BlockSpec(memory_space=pltpu.VMEM),
        ],
        out_specs=pl.BlockSpec(memory_space=pltpu.VMEM),
        out_shape=jax.ShapeDtypeStruct(own.shape, jnp.float32),
        compiler_params=pltpu.CompilerParams(vmem_limit_bytes=16 * MIB),
        name="finish",
    )(slots, own, back)


def per_device(ensemble, increment, coords, sent_slots, pair_list, pair_count):
    blocks, members, levels, points = ensemble.shape
    regions = lax.axis_size("region")
    groups = lax.axis_size("member")
    step = levels // groups
    slots = sent_slots.reshape(-1)
    pairs = pair_list.T
    own = lax.axis_index("member").reshape(1).astype(jnp.int32)
    places = select(coords, slots)
    own_places = lax.all_to_all(places, "region", 0, 0, tiled=True)
    big = pack(ensemble, increment, slots, own, groups)
    big, own_places = lax.optimization_barrier((big, own_places))
    got = lax.all_to_all(
        big.reshape(regions * groups, -1, LANES), ("region", "member"), 0, 0, tiled=True
    ).reshape(regions, groups, -1, LANES)
    swap = [(i, i ^ 1) for i in range(groups)]
    core, row = own & 1, own >> 1
    rows = groups // 2
    share = pairs.shape[1] // 2
    keep, send = diag(ensemble, increment, coords, core, rows)
    merged = merge(keep, lax.ppermute(send, "member", swap), row)
    parts = [
        lax.ppermute(part, "member", [(i, (i + 2 * hop) % groups) for i in range(groups)])
        for hop, part in enumerate(merged[1:], 1)
    ]
    diagonal = total_of(merged[0], parts)
    own_places, _ = lax.optimization_barrier((own_places, send))
    mine = []
    for start in range(0, share, PAIR_GROUP):
        if start == AFTER_MERGE * PAIR_GROUP:
            own_places, _ = lax.optimization_barrier((own_places, merged[0]))
        if start == AFTER_TOTAL * PAIR_GROUP:
            own_places, diagonal = lax.optimization_barrier((own_places, diagonal))
        mine.append(tiles(own_places, pairs, core * share + start))
    theirs = [lax.ppermute(stack, "member", swap) for stack in mine]
    got, diagonal = lax.optimization_barrier((got, diagonal))
    stacks = [in_hbm(stack) for stack in mine + theirs]
    partial = apply_pairs(in_hbm(got), stacks, pairs, pair_count, core, members, step)
    back = lax.all_to_all(partial, "region", 0, 0, tiled=True)
    return finish(diagonal, back, slots, 1.0 / (members * groups - 1))


def solution(mesh):
    in_specs = (
        P("region", "member", None, None),
        P("region", None, None),
        P("region", None, None),
        P("region", None, None),
        P("region", None),
        P("region"),
    )
    out_specs = P("region", "member", None)
    return jax.shard_map(
        per_device, mesh=mesh, in_specs=in_specs, out_specs=out_specs, check_vma=False
    )
```

```python
import functools

import jax
import jax.numpy as jnp
from jax import lax
from jax.experimental import pallas as pl
from jax.experimental.pallas import tpu as pltpu
from jax.sharding import PartitionSpec as P

LANES = 128
PAIR_GROUP = 4
MIB = 1024 * 1024
UNIT = 12.0**-0.2
UNIT2 = UNIT * UNIT
LEAST = UNIT2 * 2.0**-12


def select_kernel(slots, coords_ref, places_ref, sem):
    total = places_ref.shape[0]

    def copy(owner):
        return pltpu.make_async_copy(coords_ref.at[slots[owner]], places_ref.at[owner], sem.at[owner])

    for owner in range(total):
        copy(owner).start()
    for owner in range(total):
        copy(owner).wait()


def select(coords, slots):
    total = slots.shape[0]
    return pl.pallas_call(
        select_kernel,
        in_specs=[pl.BlockSpec(memory_space=pltpu.SMEM), pl.BlockSpec(memory_space=pl.ANY)],
        out_specs=pl.BlockSpec(memory_space=pl.ANY),
        out_shape=jax.ShapeDtypeStruct((total, *coords.shape[1:]), coords.dtype),
        scratch_shapes=[pltpu.SemaphoreType.DMA((total,))],
        compiler_params=pltpu.CompilerParams(vmem_limit_bytes=60 * MIB),
        name="select",
    )(slots, coords)


def pack_kernel(slots, own, ens_ref, inc_ref, big_ref, ens_buf, inc_buf, out_buf, in_sem, inc_sem, out_sem):
    total, members, levels, points = ens_buf.shape
    parts = out_buf.shape[1]
    step = levels // parts
    lane_chunks = points // LANES

    def ens_copy(owner):
        return pltpu.make_async_copy(ens_ref.at[slots[owner]], ens_buf.at[owner], in_sem.at[owner])

    def inc_copy(owner):
        return pltpu.make_async_copy(inc_ref.at[slots[owner]], inc_buf.at[owner], inc_sem.at[owner])

    def out_copy(owner):
        return pltpu.make_async_copy(out_buf.at[owner], big_ref.at[owner], out_sem.at[owner])

    for owner in range(total):
        ens_copy(owner).start()
        inc_copy(owner).start()
    chunk = pl.multiple_of(lax.rem(own[0], lane_chunks) * LANES, LANES)
    for owner in range(total):
        ens_copy(owner).wait()
        inc_copy(owner).wait()
        for part in range(parts):
            here = slice(part * step, (part + 1) * step)
            for lane in range(lane_chunks):
                out_buf[owner, part, lane * members * step : (lane + 1) * members * step, :] = ens_buf[
                    owner, :, here, lane * LANES : (lane + 1) * LANES
                ].reshape(members * step, LANES)
            out_buf[owner, part, members * step * lane_chunks :, :] = inc_buf[owner, here, pl.ds(chunk, LANES)]
        out_copy(owner).start()
    for owner in range(total):
        out_copy(owner).wait()


def pack(ensemble, increment, slots, own, parts):
    blocks, members, levels, points = ensemble.shape
    total = slots.shape[0]
    step = levels // parts
    rows = members * step * (points // LANES) + step
    return pl.pallas_call(
        pack_kernel,
        in_specs=[
            pl.BlockSpec(memory_space=pltpu.SMEM),
            pl.BlockSpec(memory_space=pltpu.SMEM),
            pl.BlockSpec(memory_space=pl.ANY),
            pl.BlockSpec(memory_space=pl.ANY),
        ],
        out_specs=pl.BlockSpec(memory_space=pl.ANY),
        out_shape=jax.ShapeDtypeStruct((total, parts, rows, LANES), ensemble.dtype),
        scratch_shapes=[
            pltpu.VMEM((total, members, levels, points), ensemble.dtype),
            pltpu.VMEM((total, levels, points), increment.dtype),
            pltpu.VMEM((total, parts, rows, LANES), ensemble.dtype),
            pltpu.SemaphoreType.DMA((total,)),
            pltpu.SemaphoreType.DMA((total,)),
            pltpu.SemaphoreType.DMA((total,)),
        ],
        compiler_params=pltpu.CompilerParams(vmem_limit_bytes=60 * MIB),
        name="pack",
    )(slots, own, ensemble, increment)


def in_hbm(value):
    return pltpu.with_memory_space_constraint(value, pltpu.HBM)


def three_parts(value):
    first = value.astype(jnp.bfloat16).astype(jnp.float32)
    rest = value - first
    second = rest.astype(jnp.bfloat16).astype(jnp.float32)
    return [first, second, rest - second]


def left_rows(places):
    east, north = places[0:1], places[1:2]
    one = jnp.ones_like(east)
    norm = UNIT2 * (east * east + north * north)
    rows = three_parts((-2.0 * UNIT2) * east) + three_parts((-2.0 * UNIT2) * north) + three_parts(norm)
    rows = rows + [one] * 3 + [jnp.zeros_like(east)] * 4
    return jnp.concatenate(rows, axis=0).astype(jnp.bfloat16)


def right_rows(places):
    east, north = places[0:1], places[1:2]
    one = jnp.ones_like(east)
    norm = UNIT2 * (east * east + north * north)
    rows = [east] * 3 + [north] * 3 + [one] * 3 + three_parts(norm) + [jnp.zeros_like(east)] * 4
    return jnp.concatenate(rows, axis=0).astype(jnp.bfloat16)


def tile_of(left, right):
    squared = lax.dot_general(left, right, (((0,), (0,)), ((), ())), preferred_element_type=jnp.float32)
    squared = jnp.maximum(squared, LEAST)
    inverse = lax.rsqrt(squared)
    z = squared * inverse
    outer = jnp.maximum(2.0 * UNIT - z, 0.0)
    inner = jnp.maximum(UNIT - z, 0.0)
    outer2 = outer * outer
    inner2 = inner * inner
    shifted = z + 2.0 * UNIT
    first = (outer2 * outer2) * (z * shifted - 0.5 * UNIT2)
    second = (inner2 * inner2) * (inner * shifted)
    return ((first + 4.0 * second) * inverse).astype(jnp.bfloat16)


def diag_kernel(core, ens_ref, inc_ref, coords_ref, keep_ref, send_ref, sum_ref):
    members, levels, points = ens_ref.shape[1:]
    parts, _, step, _ = keep_ref.shape
    rows = members * levels
    half = points // 2
    places = coords_ref[0].astype(jnp.float32)
    left, right = left_rows(places), right_rows(places)
    upper = tile_of(left[:, :half], right)
    lower = tile_of(left[:, half:], right[:, half:])
    weighted = (ens_ref[0] * inc_ref[0][None]).reshape(rows, points)
    near, far = weighted[:, :half], weighted[:, half:]
    field_near = jnp.dot(near, upper[:, :half], preferred_element_type=jnp.float32) + lax.dot_general(
        far, upper[:, half:], (((1,), (1,)), ((), ())), preferred_element_type=jnp.float32
    )
    field_far = jnp.dot(near, upper[:, half:], preferred_element_type=jnp.float32) + jnp.dot(
        far, lower, preferred_element_type=jnp.float32
    )
    block = ens_ref[0].astype(jnp.float32)
    sum_ref[:, :half] = jnp.sum(block[:, :, :half] * field_near.reshape(members, levels, half), axis=0)
    sum_ref[:, half:] = jnp.sum(block[:, :, half:] * field_far.reshape(members, levels, half), axis=0)
    for part in range(parts):
        mine = pl.multiple_of((2 * part + core[0]) * step, step)
        other = pl.multiple_of((2 * part + 1 - core[0]) * step, step)
        keep_ref[part, 0] = sum_ref[pl.ds(mine, step), :]
        send_ref[part, 0] = sum_ref[pl.ds(other, step), :]


def diag(ensemble, increment, coords, core, parts):
    blocks, members, levels, points = ensemble.shape
    step = levels // (2 * parts)
    out = jax.ShapeDtypeStruct((parts, blocks, step, points), jnp.float32)
    return pl.pallas_call(
        diag_kernel,
        grid_spec=pltpu.PrefetchScalarGridSpec(
            num_scalar_prefetch=1,
            grid=(blocks,),
            in_specs=[
                pl.BlockSpec((1, members, levels, points), lambda b, c: (b, 0, 0, 0)),
                pl.BlockSpec((1, levels, points), lambda b, c: (b, 0, 0)),
                pl.BlockSpec((1, 2, points), lambda b, c: (b, 0, 0)),
            ],
            out_specs=[pl.BlockSpec((parts, 1, step, points), lambda b, c: (0, b, 0, 0))] * 2,
            scratch_shapes=[pltpu.VMEM((levels, points), jnp.float32)],
        ),
        out_shape=[out, out],
        compiler_params=pltpu.CompilerParams(vmem_limit_bytes=60 * MIB),
        cost_estimate=pl.CostEstimate(flops=20_000_000_000, bytes_accessed=8_000_000, transcendentals=0),
        name="diag",
    )(core, ensemble, increment, coords)


def merge_kernel(row, keep_ref, got_ref, near_ref, far_ref):
    parts = near_ref.shape[0]
    for part in range(parts):
        near = 2 * part + (row[0] & 1)
        far = 2 * part + 1 - (row[0] & 1)
        near_ref[part] = keep_ref[near] + got_ref[near]
        far_ref[part] = (keep_ref[far] + got_ref[far]).astype(far_ref.dtype)


def merge(keep, got, row):
    shape = (keep.shape[0] // 2, *keep.shape[1:])
    return pl.pallas_call(
        merge_kernel,
        in_specs=[pl.BlockSpec(memory_space=pltpu.SMEM)] + [pl.BlockSpec(memory_space=pltpu.VMEM)] * 2,
        out_specs=[pl.BlockSpec(memory_space=pltpu.VMEM)] * 2,
        out_shape=[jax.ShapeDtypeStruct(shape, jnp.float32), jax.ShapeDtypeStruct(shape, jnp.bfloat16)],
        compiler_params=pltpu.CompilerParams(vmem_limit_bytes=16 * MIB),
        name="merge",
    )(row, keep, got)


def halve_kernel(row, near_ref, got_ref, own_ref, send_ref):
    mine = row[0] >> 1
    own_ref[...] = near_ref[mine] + got_ref[mine].astype(jnp.float32)
    send_ref[...] = (near_ref[1 - mine] + got_ref[1 - mine].astype(jnp.float32)).astype(send_ref.dtype)


def halve(near, got, row):
    shape = near.shape[1:]
    return pl.pallas_call(
        halve_kernel,
        in_specs=[pl.BlockSpec(memory_space=pltpu.SMEM)] + [pl.BlockSpec(memory_space=pltpu.VMEM)] * 2,
        out_specs=[pl.BlockSpec(memory_space=pltpu.VMEM)] * 2,
        out_shape=[jax.ShapeDtypeStruct(shape, jnp.float32), jax.ShapeDtypeStruct(shape, jnp.bfloat16)],
        compiler_params=pltpu.CompilerParams(vmem_limit_bytes=16 * MIB),
        name="halve",
    )(row, near, got)


def tiles_kernel(pairs, first, source_ref, out_ref, places_ref, tile_ref, sem, places_sem):
    fetch = pltpu.make_async_copy(source_ref, places_ref, places_sem)
    fetch.start()
    fetch.wait()

    def copy(within):
        return pltpu.make_async_copy(tile_ref.at[within], out_ref.at[within], sem.at[within])

    for within in range(tile_ref.shape[0]):
        index = first[0] + within
        left = left_rows(places_ref[pairs[0, index]].astype(jnp.float32))
        right = right_rows(places_ref[pairs[1, index]].astype(jnp.float32))
        tile_ref[within] = tile_of(left, right)
        copy(within).start()
    for within in range(tile_ref.shape[0]):
        copy(within).wait()


def tiles(places, pairs, first):
    shape = (PAIR_GROUP, places.shape[2], places.shape[2])
    return pl.pallas_call(
        tiles_kernel,
        in_specs=[
            pl.BlockSpec(memory_space=pltpu.SMEM),
            pl.BlockSpec(memory_space=pltpu.SMEM),
            pl.BlockSpec(memory_space=pl.ANY),
        ],
        out_specs=pl.BlockSpec(memory_space=pl.ANY),
        out_shape=pltpu.HBM(shape, jnp.bfloat16),
        scratch_shapes=[
            pltpu.VMEM(places.shape, places.dtype),
            pltpu.VMEM(shape, jnp.bfloat16),
            pltpu.SemaphoreType.DMA((PAIR_GROUP,)),
            pltpu.SemaphoreType.DMA,
        ],
        compiler_params=pltpu.CompilerParams(vmem_limit_bytes=60 * MIB),
        cost_estimate=pl.CostEstimate(flops=4_000_000_000, bytes_accessed=2_000_000, transcendentals=0),
        name="tiles",
    )(pairs, first, in_hbm(places))


def apply_kernel(
    pairs, count, core, got_ref, *refs,
):
    *stacks, out_ref, ens_ref, inc_ref, weighted_ref, field_ref, tiles_ref, ens_sem, inc_sem, tiles_sem = refs
    slot_total, sources, rows, points = ens_ref.shape
    step = inc_ref.shape[2]
    groups = len(stacks)
    lane_chunks = points // LANES
    every = sources * rows

    def ens_copies(slot):
        return [
            pltpu.make_async_copy(
                got_ref.at[slot, :, lane * rows : (lane + 1) * rows, :],
                ens_ref.at[slot, :, :, lane * LANES : (lane + 1) * LANES],
                ens_sem.at[slot, lane],
            )
            for lane in range(lane_chunks)
        ]

    inc_copy = pltpu.make_async_copy(got_ref.at[:, :lane_chunks, rows * lane_chunks :, :], inc_ref, inc_sem)

    def tile_copy(group):
        return pltpu.make_async_copy(stacks[group], tiles_ref.at[group], tiles_sem.at[group])

    inc_copy.start()
    for slot in range(slot_total):
        for copy in ens_copies(slot):
            copy.start()
    for group in range(groups):
        tile_copy(group).start()
    inc_copy.wait()
    for slot in range(slot_total):
        field_ref[slot] = jnp.zeros((every, points), jnp.float32)
        for copy in ens_copies(slot):
            copy.wait()
        for lane in range(lane_chunks):
            here = slice(lane * LANES, (lane + 1) * LANES)
            gain = inc_ref[slot, lane]
            block = ens_ref[slot, :, :, here].reshape(every // step, step, LANES)
            weighted_ref[slot, :, here] = (block * gain[None]).reshape(every, LANES)

    def some(group, row, within, number):
        products = []
        for each in range(number):
            first, second = pairs[0, row + each], pairs[1, row + each]
            tile = tiles_ref[group, within + each]
            to_first = lax.dot_general(
                weighted_ref[second], tile, (((1,), (1,)), ((), ())), preferred_element_type=jnp.float32
            )
            to_second = jnp.dot(weighted_ref[first], tile, preferred_element_type=jnp.float32)
            products += [(first, to_first), (second, to_second)]
        for slot, product in products:
            field_ref[slot] += product

    def turn(group, carry):
        away = core[0] * (groups // 2)
        row = PAIR_GROUP * jnp.where(group < groups // 2, group + away, group - away)
        live = count[0] - row
        pltpu.make_async_copy(stacks[0], tiles_ref.at[group], tiles_sem.at[group]).wait()

        @pl.when(live >= PAIR_GROUP)
        def _():
            some(group, row, 0, PAIR_GROUP)

        @pl.when(live < PAIR_GROUP)
        def _():
            def one(within, inner):
                some(group, row + within, within, 1)
                return inner

            lax.fori_loop(0, jnp.maximum(live, 0), one, 0)

        return carry

    lax.fori_loop(0, groups, turn, 0)

    for slot in range(slot_total):
        product = ens_ref[slot].reshape(every, points).astype(jnp.float32) * field_ref[slot]
        out_ref[slot] = jnp.sum(product.reshape(every // step, step, points), axis=0)


def apply_pairs(got, stacks, pairs, count, core, members, step):
    slot_total, sources, rows, _ = got.shape
    points = stacks[0].shape[2]
    lane_chunks = points // LANES
    every = sources * members * step
    return pl.pallas_call(
        apply_kernel,
        in_specs=[
            pl.BlockSpec(memory_space=pltpu.SMEM),
            pl.BlockSpec(memory_space=pltpu.SMEM),
            pl.BlockSpec(memory_space=pltpu.SMEM),
            pl.BlockSpec(memory_space=pl.ANY),
            *[pl.BlockSpec(memory_space=pl.ANY)] * len(stacks),
        ],
        out_specs=pl.BlockSpec(memory_space=pltpu.VMEM),
        scratch_shapes=[
            pltpu.VMEM((slot_total, sources, members * step, points), jnp.bfloat16),
            pltpu.VMEM((slot_total, lane_chunks, step, LANES), jnp.bfloat16),
            pltpu.VMEM((slot_total, every, points), jnp.bfloat16),
            pltpu.VMEM((slot_total, every, points), jnp.float32),
            pltpu.VMEM((len(stacks), *stacks[0].shape), jnp.bfloat16),
            pltpu.SemaphoreType.DMA((slot_total, lane_chunks)),
            pltpu.SemaphoreType.DMA,
            pltpu.SemaphoreType.DMA((len(stacks),)),
        ],
        out_shape=jax.ShapeDtypeStruct((slot_total, step, points), jnp.float32),
        compiler_params=pltpu.CompilerParams(vmem_limit_bytes=60 * MIB),
        cost_estimate=pl.CostEstimate(flops=9_000_000_000, bytes_accessed=22_000_000, transcendentals=0),
        name="apply",
    )(pairs, count, core, got, *stacks)


def finish_kernel(slots, own_ref, *refs, scale):
    *part_refs, back_ref, out_ref = refs
    total = own_ref[...]
    for part_ref in part_refs:
        total = total + part_ref[...].astype(jnp.float32)
    out_ref[...] = total * scale
    for owner in range(back_ref.shape[0]):
        slot = slots[owner]
        out_ref[slot] = out_ref[slot] + back_ref[owner] * scale


def finish(own, parts, back, slots, scale):
    return pl.pallas_call(
        functools.partial(finish_kernel, scale=scale),
        in_specs=[pl.BlockSpec(memory_space=pltpu.SMEM)] + [pl.BlockSpec(memory_space=pltpu.VMEM)] * (len(parts) + 2),
        out_specs=pl.BlockSpec(memory_space=pltpu.VMEM),
        out_shape=jax.ShapeDtypeStruct(own.shape, jnp.float32),
        compiler_params=pltpu.CompilerParams(vmem_limit_bytes=16 * MIB),
        name="finish",
    )(slots, own, *parts, back)


def per_device(ensemble, increment, coords, sent_slots, pair_list, pair_count):
    blocks, members, levels, points = ensemble.shape
    regions = lax.axis_size("region")
    groups = lax.axis_size("member")
    step = levels // groups
    slots = sent_slots.reshape(-1)
    pairs = pair_list.T
    own = lax.axis_index("member").reshape(1).astype(jnp.int32)
    places = select(coords, slots)
    own_places = lax.all_to_all(places, "region", 0, 0, tiled=True)
    big = pack(ensemble, increment, slots, own, groups)
    big, own_places = lax.optimization_barrier((big, own_places))
    got = lax.all_to_all(
        big.reshape(regions * groups, -1, LANES), ("region", "member"), 0, 0, tiled=True
    ).reshape(regions, groups, -1, LANES)
    swap = [(i, i ^ 1) for i in range(groups)]
    core, row = own & 1, own >> 1
    rows = groups // 2
    assert rows == 4
    share = pairs.shape[1] // 2
    keep, send = diag(ensemble, increment, coords, core, rows)
    near, far = merge(keep, lax.ppermute(send, "member", swap), row)
    beside = lax.ppermute(far, "member", [(i, i ^ 2) for i in range(groups)])
    own_places, _ = lax.optimization_barrier((own_places, send))
    mine = [tiles(own_places, pairs, core * share + start) for start in range(0, share, PAIR_GROUP)]
    theirs = [lax.ppermute(stack, "member", swap) for stack in mine]
    got, near, beside = lax.optimization_barrier((got, near, beside))
    stacks = [in_hbm(stack) for stack in mine + theirs]
    partial = apply_pairs(in_hbm(got), stacks, pairs, pair_count, core, members, step)
    partial, near, beside = lax.optimization_barrier((partial, near, beside))
    diagonal, send = halve(near, beside, row)
    opposite = lax.ppermute(send, "member", [(i, i ^ 4) for i in range(groups)])
    back = lax.all_to_all(partial, "region", 0, 0, tiled=True)
    return finish(diagonal, [opposite], back, slots, 1.0 / (members * groups - 1))


def solution(mesh):
    in_specs = (
        P("region", "member", None, None),
        P("region", None, None),
        P("region", None, None),
        P("region", None, None),
        P("region", None),
        P("region"),
    )
    out_specs = P("region", "member", None)
    return jax.shard_map(
        per_device, mesh=mesh, in_specs=in_specs, out_specs=out_specs, check_vma=False
    )
```

```python
import functools

import jax
import jax.numpy as jnp
from jax import lax
from jax.experimental import pallas as pl
from jax.experimental.pallas import tpu as pltpu
from jax.sharding import PartitionSpec as P

LANES = 128
PAIR_GROUP = 4
MIB = 1024 * 1024
UNIT = 12.0**-0.2
UNIT2 = UNIT * UNIT
LEAST = UNIT2 * 2.0**-12


def select_kernel(slots, own, inc_ref, coords_ref, out_ref, sem):
    total, rows, _ = out_ref.shape
    step = rows - coords_ref.shape[1]
    first = pl.multiple_of(own[0] * step, step)

    def copy(owner):
        return pltpu.make_async_copy(
            inc_ref.at[slots[owner], pl.ds(first, step), :], out_ref.at[owner, :step, :], sem.at[owner]
        )

    for owner in range(total):
        copy(owner).start()
    for owner in range(total):
        out_ref[owner, step:, :] = coords_ref[slots[owner]]
    for owner in range(total):
        copy(owner).wait()


def select(increment, coords, slots, own, step):
    total, points = slots.shape[0], coords.shape[2]
    return pl.pallas_call(
        select_kernel,
        in_specs=[
            pl.BlockSpec(memory_space=pltpu.SMEM),
            pl.BlockSpec(memory_space=pltpu.SMEM),
            pl.BlockSpec(memory_space=pl.ANY),
            pl.BlockSpec(memory_space=pltpu.VMEM),
        ],
        out_specs=pl.BlockSpec(memory_space=pltpu.VMEM),
        out_shape=jax.ShapeDtypeStruct((total, step + coords.shape[1], points), coords.dtype),
        scratch_shapes=[pltpu.SemaphoreType.DMA((total,))],
        compiler_params=pltpu.CompilerParams(vmem_limit_bytes=60 * MIB),
        name="select",
    )(slots, own, increment, coords)


def pack_kernel(slots, ens_ref, big_ref, ens_buf, out_buf, in_sem, out_sem):
    total, members, levels, points = ens_buf.shape
    parts = out_buf.shape[1]
    step = levels // parts
    lane_chunks = points // LANES

    def ens_copy(owner):
        return pltpu.make_async_copy(ens_ref.at[slots[owner]], ens_buf.at[owner], in_sem.at[owner])

    def out_copy(owner):
        return pltpu.make_async_copy(out_buf.at[owner], big_ref.at[owner], out_sem.at[owner])

    for owner in range(total):
        ens_copy(owner).start()
    for owner in range(total):
        ens_copy(owner).wait()
        for part in range(parts):
            here = slice(part * step, (part + 1) * step)
            for lane in range(lane_chunks):
                out_buf[owner, part, lane * members * step : (lane + 1) * members * step, :] = ens_buf[
                    owner, :, here, lane * LANES : (lane + 1) * LANES
                ].reshape(members * step, LANES)
        out_copy(owner).start()
    for owner in range(total):
        out_copy(owner).wait()


def pack(ensemble, slots, parts):
    blocks, members, levels, points = ensemble.shape
    total = slots.shape[0]
    rows = members * (levels // parts) * (points // LANES)
    return pl.pallas_call(
        pack_kernel,
        in_specs=[pl.BlockSpec(memory_space=pltpu.SMEM), pl.BlockSpec(memory_space=pl.ANY)],
        out_specs=pl.BlockSpec(memory_space=pl.ANY),
        out_shape=jax.ShapeDtypeStruct((total, parts, rows, LANES), ensemble.dtype),
        scratch_shapes=[
            pltpu.VMEM((total, members, levels, points), ensemble.dtype),
            pltpu.VMEM((total, parts, rows, LANES), ensemble.dtype),
            pltpu.SemaphoreType.DMA((total,)),
            pltpu.SemaphoreType.DMA((total,)),
        ],
        compiler_params=pltpu.CompilerParams(vmem_limit_bytes=60 * MIB),
        name="pack",
    )(slots, ensemble)


def in_hbm(value):
    return pltpu.with_memory_space_constraint(value, pltpu.HBM)


def three_parts(value):
    first = value.astype(jnp.bfloat16).astype(jnp.float32)
    rest = value - first
    second = rest.astype(jnp.bfloat16).astype(jnp.float32)
    return [first, second, rest - second]


def left_rows(places):
    east, north = places[0:1], places[1:2]
    one = jnp.ones_like(east)
    norm = UNIT2 * (east * east + north * north)
    rows = three_parts((-2.0 * UNIT2) * east) + three_parts((-2.0 * UNIT2) * north) + three_parts(norm)
    rows = rows + [one] * 3 + [jnp.zeros_like(east)] * 4
    return jnp.concatenate(rows, axis=0).astype(jnp.bfloat16)


def right_rows(places):
    east, north = places[0:1], places[1:2]
    one = jnp.ones_like(east)
    norm = UNIT2 * (east * east + north * north)
    rows = [east] * 3 + [north] * 3 + [one] * 3 + three_parts(norm) + [jnp.zeros_like(east)] * 4
    return jnp.concatenate(rows, axis=0).astype(jnp.bfloat16)


def tile_of(left, right):
    squared = lax.dot_general(left, right, (((0,), (0,)), ((), ())), preferred_element_type=jnp.float32)
    squared = jnp.maximum(squared, LEAST)
    inverse = lax.rsqrt(squared)
    z = squared * inverse
    outer = jnp.maximum(2.0 * UNIT - z, 0.0)
    inner = jnp.maximum(UNIT - z, 0.0)
    outer2 = outer * outer
    inner2 = inner * inner
    shifted = z + 2.0 * UNIT
    first = (outer2 * outer2) * (z * shifted - 0.5 * UNIT2)
    second = (inner2 * inner2) * (inner * shifted)
    return ((first + 4.0 * second) * inverse).astype(jnp.bfloat16)


def diag_kernel(core, ens_ref, inc_ref, coords_ref, keep_ref, send_ref, sum_ref):
    members, levels, points = ens_ref.shape[1:]
    parts, _, step, _ = keep_ref.shape
    rows = members * levels
    half = points // 2
    places = coords_ref[0].astype(jnp.float32)
    left, right = left_rows(places), right_rows(places)
    upper = tile_of(left[:, :half], right)
    lower = tile_of(left[:, half:], right[:, half:])
    weighted = (ens_ref[0] * inc_ref[0][None]).reshape(rows, points)
    near, far = weighted[:, :half], weighted[:, half:]
    field_near = jnp.dot(near, upper[:, :half], preferred_element_type=jnp.float32) + lax.dot_general(
        far, upper[:, half:], (((1,), (1,)), ((), ())), preferred_element_type=jnp.float32
    )
    field_far = jnp.dot(near, upper[:, half:], preferred_element_type=jnp.float32) + jnp.dot(
        far, lower, preferred_element_type=jnp.float32
    )
    block = ens_ref[0].astype(jnp.float32)
    sum_ref[:, :half] = jnp.sum(block[:, :, :half] * field_near.reshape(members, levels, half), axis=0)
    sum_ref[:, half:] = jnp.sum(block[:, :, half:] * field_far.reshape(members, levels, half), axis=0)
    for part in range(parts):
        mine = pl.multiple_of((2 * part + core[0]) * step, step)
        other = pl.multiple_of((2 * part + 1 - core[0]) * step, step)
        keep_ref[part, 0] = sum_ref[pl.ds(mine, step), :]
        send_ref[part, 0] = sum_ref[pl.ds(other, step), :]


def diag(ensemble, increment, coords, core, parts):
    blocks, members, levels, points = ensemble.shape
    step = levels // (2 * parts)
    out = jax.ShapeDtypeStruct((parts, blocks, step, points), jnp.float32)
    return pl.pallas_call(
        diag_kernel,
        grid_spec=pltpu.PrefetchScalarGridSpec(
            num_scalar_prefetch=1,
            grid=(blocks,),
            in_specs=[
                pl.BlockSpec((1, members, levels, points), lambda b, c: (b, 0, 0, 0)),
                pl.BlockSpec((1, levels, points), lambda b, c: (b, 0, 0)),
                pl.BlockSpec((1, 2, points), lambda b, c: (b, 0, 0)),
            ],
            out_specs=[pl.BlockSpec((parts, 1, step, points), lambda b, c: (0, b, 0, 0))] * 2,
            scratch_shapes=[pltpu.VMEM((levels, points), jnp.float32)],
        ),
        out_shape=[out, out],
        compiler_params=pltpu.CompilerParams(vmem_limit_bytes=60 * MIB),
        cost_estimate=pl.CostEstimate(flops=20_000_000_000, bytes_accessed=8_000_000, transcendentals=0),
        name="diag",
    )(core, ensemble, increment, coords)


def merge_kernel(row, keep_ref, got_ref, own_ref, *send_refs):
    parts = keep_ref.shape[0]
    own_ref[...] = keep_ref[row[0]] + got_ref[row[0]]
    for shift, send_ref in enumerate(send_refs, 1):
        there = lax.rem(row[0] + shift, parts)
        send_ref[...] = (keep_ref[there] + got_ref[there]).astype(send_ref.dtype)


def merge(keep, got, row):
    parts = keep.shape[0]
    out = [jax.ShapeDtypeStruct(keep.shape[1:], jnp.float32)]
    out += [jax.ShapeDtypeStruct(keep.shape[1:], jnp.bfloat16)] * (parts - 1)
    return pl.pallas_call(
        merge_kernel,
        in_specs=[pl.BlockSpec(memory_space=pltpu.SMEM)] + [pl.BlockSpec(memory_space=pltpu.VMEM)] * 2,
        out_specs=[pl.BlockSpec(memory_space=pltpu.VMEM)] * parts,
        out_shape=out,
        compiler_params=pltpu.CompilerParams(vmem_limit_bytes=16 * MIB),
        name="merge",
    )(row, keep, got)


def tiles_kernel(pairs, first, places_ref, out_ref, tile_ref, sem):
    def copy(within):
        return pltpu.make_async_copy(tile_ref.at[within], out_ref.at[within], sem.at[within])

    for within in range(tile_ref.shape[0]):
        index = first[0] + within
        left = left_rows(places_ref[pairs[0, index], -2:, :].astype(jnp.float32))
        right = right_rows(places_ref[pairs[1, index], -2:, :].astype(jnp.float32))
        tile_ref[within] = tile_of(left, right)
        copy(within).start()
    for within in range(tile_ref.shape[0]):
        copy(within).wait()


def tiles(places, pairs, first):
    shape = (PAIR_GROUP, places.shape[2], places.shape[2])
    return pl.pallas_call(
        tiles_kernel,
        in_specs=[
            pl.BlockSpec(memory_space=pltpu.SMEM),
            pl.BlockSpec(memory_space=pltpu.SMEM),
            pl.BlockSpec(memory_space=pltpu.VMEM),
        ],
        out_specs=pl.BlockSpec(memory_space=pl.ANY),
        out_shape=pltpu.HBM(shape, jnp.bfloat16),
        scratch_shapes=[pltpu.VMEM(shape, jnp.bfloat16), pltpu.SemaphoreType.DMA((PAIR_GROUP,))],
        compiler_params=pltpu.CompilerParams(vmem_limit_bytes=60 * MIB),
        cost_estimate=pl.CostEstimate(flops=4_000_000_000, bytes_accessed=2_000_000, transcendentals=0),
        name="tiles",
    )(pairs, first, places)


def apply_kernel(
    pairs, count, core, got_ref, small_ref, *refs,
):
    *stacks, out_ref, ens_ref, inc_ref, weighted_ref, field_ref, tiles_ref, ens_sem, inc_sem, tiles_sem = refs
    slot_total, sources, rows, points = ens_ref.shape
    step = inc_ref.shape[1]
    groups = len(stacks)
    lane_chunks = points // LANES
    every = sources * rows

    def ens_copies(slot):
        return [
            pltpu.make_async_copy(
                got_ref.at[slot, :, lane * rows : (lane + 1) * rows, :],
                ens_ref.at[slot, :, :, lane * LANES : (lane + 1) * LANES],
                ens_sem.at[slot, lane],
            )
            for lane in range(lane_chunks)
        ]

    inc_copy = pltpu.make_async_copy(small_ref.at[:, :step, :], inc_ref, inc_sem)

    def tile_copy(group):
        return pltpu.make_async_copy(stacks[group], tiles_ref.at[group], tiles_sem.at[group])

    inc_copy.start()
    for slot in range(slot_total):
        for copy in ens_copies(slot):
            copy.start()
    for group in range(groups):
        tile_copy(group).start()
    inc_copy.wait()
    for slot in range(slot_total):
        field_ref[slot] = jnp.zeros((every, points), jnp.float32)
        for copy in ens_copies(slot):
            copy.wait()
        block = ens_ref[slot].reshape(every // step, step, points)
        weighted_ref[slot] = (block * inc_ref[slot][None]).reshape(every, points)

    def some(group, row, within, number):
        products = []
        for each in range(number):
            first, second = pairs[0, row + each], pairs[1, row + each]
            tile = tiles_ref[group, within + each]
            to_first = lax.dot_general(
                weighted_ref[second], tile, (((1,), (1,)), ((), ())), preferred_element_type=jnp.float32
            )
            to_second = jnp.dot(weighted_ref[first], tile, preferred_element_type=jnp.float32)
            products += [(first, to_first), (second, to_second)]
        for slot, product in products:
            field_ref[slot] += product

    def turn(group, carry):
        away = core[0] * (groups // 2)
        row = PAIR_GROUP * jnp.where(group < groups // 2, group + away, group - away)
        live = count[0] - row
        pltpu.make_async_copy(stacks[0], tiles_ref.at[group], tiles_sem.at[group]).wait()

        @pl.when(live >= PAIR_GROUP)
        def _():
            some(group, row, 0, PAIR_GROUP)

        @pl.when(live < PAIR_GROUP)
        def _():
            def one(within, inner):
                some(group, row + within, within, 1)
                return inner

            lax.fori_loop(0, jnp.maximum(live, 0), one, 0)

        return carry

    lax.fori_loop(0, groups, turn, 0)

    for slot in range(slot_total):
        product = ens_ref[slot].reshape(every, points).astype(jnp.float32) * field_ref[slot]
        out_ref[slot] = jnp.sum(product.reshape(every // step, step, points), axis=0)


def apply_pairs(got, small, stacks, pairs, count, core, members, step):
    slot_total, sources, rows, _ = got.shape
    points = stacks[0].shape[2]
    lane_chunks = points // LANES
    every = sources * members * step
    return pl.pallas_call(
        apply_kernel,
        in_specs=[
            pl.BlockSpec(memory_space=pltpu.SMEM),
            pl.BlockSpec(memory_space=pltpu.SMEM),
            pl.BlockSpec(memory_space=pltpu.SMEM),
            pl.BlockSpec(memory_space=pl.ANY),
            *[pl.BlockSpec(memory_space=pl.ANY)] * (len(stacks) + 1),
        ],
        out_specs=pl.BlockSpec(memory_space=pltpu.VMEM),
        scratch_shapes=[
            pltpu.VMEM((slot_total, sources, members * step, points), jnp.bfloat16),
            pltpu.VMEM((slot_total, step, points), jnp.bfloat16),
            pltpu.VMEM((slot_total, every, points), jnp.bfloat16),
            pltpu.VMEM((slot_total, every, points), jnp.float32),
            pltpu.VMEM((len(stacks), *stacks[0].shape), jnp.bfloat16),
            pltpu.SemaphoreType.DMA((slot_total, lane_chunks)),
            pltpu.SemaphoreType.DMA,
            pltpu.SemaphoreType.DMA((len(stacks),)),
        ],
        out_shape=jax.ShapeDtypeStruct((slot_total, step, points), jnp.float32),
        compiler_params=pltpu.CompilerParams(vmem_limit_bytes=60 * MIB),
        cost_estimate=pl.CostEstimate(flops=9_000_000_000, bytes_accessed=22_000_000, transcendentals=0),
        name="apply",
    )(pairs, count, core, got, small, *stacks)


def finish_kernel(slots, own_ref, *refs, scale):
    *part_refs, back_ref, out_ref = refs
    total = own_ref[...]
    for part_ref in part_refs:
        total = total + part_ref[...].astype(jnp.float32)
    out_ref[...] = total * scale
    for owner in range(back_ref.shape[0]):
        slot = slots[owner]
        out_ref[slot] = out_ref[slot] + back_ref[owner] * scale


def finish(own, parts, back, slots, scale):
    return pl.pallas_call(
        functools.partial(finish_kernel, scale=scale),
        in_specs=[pl.BlockSpec(memory_space=pltpu.SMEM)] + [pl.BlockSpec(memory_space=pltpu.VMEM)] * (len(parts) + 2),
        out_specs=pl.BlockSpec(memory_space=pltpu.VMEM),
        out_shape=jax.ShapeDtypeStruct(own.shape, jnp.float32),
        compiler_params=pltpu.CompilerParams(vmem_limit_bytes=16 * MIB),
        name="finish",
    )(slots, own, *parts, back)


def per_device(ensemble, increment, coords, sent_slots, pair_list, pair_count):
    blocks, members, levels, points = ensemble.shape
    regions = lax.axis_size("region")
    groups = lax.axis_size("member")
    step = levels // groups
    slots = sent_slots.reshape(-1)
    pairs = pair_list.T
    own = lax.axis_index("member").reshape(1).astype(jnp.int32)
    small = lax.all_to_all(select(increment, coords, slots, own, step), "region", 0, 0, tiled=True)
    big = pack(ensemble, slots, groups)
    big, small = lax.optimization_barrier((big, small))
    got = lax.all_to_all(
        big.reshape(regions * groups, -1, LANES), ("region", "member"), 0, 0, tiled=True
    ).reshape(regions, groups, -1, LANES)
    swap = [(i, i ^ 1) for i in range(groups)]
    core, row = own & 1, own >> 1
    rows = groups // 2
    share = pairs.shape[1] // 2
    keep, send = diag(ensemble, increment, coords, core, rows)
    merged = merge(keep, lax.ppermute(send, "member", swap), row)
    small, _ = lax.optimization_barrier((small, send))
    mine = [tiles(small, pairs, core * share + start) for start in range(0, share, PAIR_GROUP)]
    theirs = [lax.ppermute(stack, "member", swap) for stack in mine]
    got, merged = lax.optimization_barrier((got, merged))
    stacks = [in_hbm(stack) for stack in mine + theirs]
    partial = apply_pairs(in_hbm(got), in_hbm(small), stacks, pairs, pair_count, core, members, step)
    partial, merged = lax.optimization_barrier((partial, merged))
    parts = [
        lax.ppermute(part, "member", [(i, (i + 2 * hop) % groups) for i in range(groups)])
        for hop, part in enumerate(merged[1:], 1)
    ]
    back = lax.all_to_all(partial, "region", 0, 0, tiled=True)
    return finish(merged[0], parts, back, slots, 1.0 / (members * groups - 1))


def solution(mesh):
    in_specs = (
        P("region", "member", None, None),
        P("region", None, None),
        P("region", None, None),
        P("region", None, None),
        P("region", None),
        P("region"),
    )
    out_specs = P("region", "member", None)
    return jax.shard_map(
        per_device, mesh=mesh, in_specs=in_specs, out_specs=out_specs, check_vma=False
    )
```

```python
import functools

import jax
import jax.numpy as jnp
from jax import lax
from jax.experimental import pallas as pl
from jax.experimental.pallas import tpu as pltpu
from jax.sharding import PartitionSpec as P

LANES = 128
PAIR_GROUP = 4
MIB = 1024 * 1024
UNIT = 12.0**-0.2
UNIT2 = UNIT * UNIT
LEAST = UNIT2 * 2.0**-12


def select_kernel(slots, own, inc_ref, coords_ref, out_ref, sem):
    total, rows, _ = out_ref.shape
    step = rows - coords_ref.shape[1]
    first = pl.multiple_of(own[0] * step, step)

    def copy(owner):
        return pltpu.make_async_copy(
            inc_ref.at[slots[owner], pl.ds(first, step), :], out_ref.at[owner, :step, :], sem.at[owner]
        )

    for owner in range(total):
        copy(owner).start()
    for owner in range(total):
        out_ref[owner, step:, :] = coords_ref[slots[owner]]
    for owner in range(total):
        copy(owner).wait()


def select(increment, coords, slots, own, step):
    total, points = slots.shape[0], coords.shape[2]
    return pl.pallas_call(
        select_kernel,
        in_specs=[
            pl.BlockSpec(memory_space=pltpu.SMEM),
            pl.BlockSpec(memory_space=pltpu.SMEM),
            pl.BlockSpec(memory_space=pl.ANY),
            pl.BlockSpec(memory_space=pltpu.VMEM),
        ],
        out_specs=pl.BlockSpec(memory_space=pltpu.VMEM),
        out_shape=jax.ShapeDtypeStruct((total, step + coords.shape[1], points), coords.dtype),
        scratch_shapes=[pltpu.SemaphoreType.DMA((total,))],
        compiler_params=pltpu.CompilerParams(vmem_limit_bytes=60 * MIB),
        name="select",
    )(slots, own, increment, coords)


def pack_kernel(slots, ens_ref, big_ref, ens_buf, out_buf, in_sem, out_sem):
    total, members, levels, points = ens_buf.shape
    parts = out_buf.shape[1]
    step = levels // parts
    lane_chunks = points // LANES

    def ens_copy(owner):
        return pltpu.make_async_copy(ens_ref.at[slots[owner]], ens_buf.at[owner], in_sem.at[owner])

    def out_copy(owner):
        return pltpu.make_async_copy(out_buf.at[owner], big_ref.at[owner], out_sem.at[owner])

    for owner in range(total):
        ens_copy(owner).start()
    for owner in range(total):
        ens_copy(owner).wait()
        for part in range(parts):
            here = slice(part * step, (part + 1) * step)
            for lane in range(lane_chunks):
                out_buf[owner, part, lane * members * step : (lane + 1) * members * step, :] = ens_buf[
                    owner, :, here, lane * LANES : (lane + 1) * LANES
                ].reshape(members * step, LANES)
        out_copy(owner).start()
    for owner in range(total):
        out_copy(owner).wait()


def pack(ensemble, slots, parts):
    blocks, members, levels, points = ensemble.shape
    total = slots.shape[0]
    rows = members * (levels // parts) * (points // LANES)
    return pl.pallas_call(
        pack_kernel,
        in_specs=[pl.BlockSpec(memory_space=pltpu.SMEM), pl.BlockSpec(memory_space=pl.ANY)],
        out_specs=pl.BlockSpec(memory_space=pl.ANY),
        out_shape=jax.ShapeDtypeStruct((total, parts, rows, LANES), ensemble.dtype),
        scratch_shapes=[
            pltpu.VMEM((total, members, levels, points), ensemble.dtype),
            pltpu.VMEM((total, parts, rows, LANES), ensemble.dtype),
            pltpu.SemaphoreType.DMA((total,)),
            pltpu.SemaphoreType.DMA((total,)),
        ],
        compiler_params=pltpu.CompilerParams(vmem_limit_bytes=60 * MIB),
        name="pack",
    )(slots, ensemble)


def in_hbm(value):
    return pltpu.with_memory_space_constraint(value, pltpu.HBM)


def three_parts(value):
    first = value.astype(jnp.bfloat16).astype(jnp.float32)
    rest = value - first
    second = rest.astype(jnp.bfloat16).astype(jnp.float32)
    return [first, second, rest - second]


def left_rows(places):
    east, north = places[0:1], places[1:2]
    one = jnp.ones_like(east)
    norm = UNIT2 * (east * east + north * north)
    rows = three_parts((-2.0 * UNIT2) * east) + three_parts((-2.0 * UNIT2) * north) + three_parts(norm)
    rows = rows + [one] * 3 + [jnp.zeros_like(east)] * 4
    return jnp.concatenate(rows, axis=0).astype(jnp.bfloat16)


def right_rows(places):
    east, north = places[0:1], places[1:2]
    one = jnp.ones_like(east)
    norm = UNIT2 * (east * east + north * north)
    rows = [east] * 3 + [north] * 3 + [one] * 3 + three_parts(norm) + [jnp.zeros_like(east)] * 4
    return jnp.concatenate(rows, axis=0).astype(jnp.bfloat16)


def tile_of(left, right):
    squared = lax.dot_general(left, right, (((0,), (0,)), ((), ())), preferred_element_type=jnp.float32)
    squared = jnp.maximum(squared, LEAST)
    inverse = lax.rsqrt(squared)
    z = squared * inverse
    outer = jnp.maximum(2.0 * UNIT - z, 0.0)
    inner = jnp.maximum(UNIT - z, 0.0)
    outer2 = outer * outer
    inner2 = inner * inner
    shifted = z + 2.0 * UNIT
    first = (outer2 * outer2) * (z * shifted - 0.5 * UNIT2)
    second = (inner2 * inner2) * (inner * shifted)
    return ((first + 4.0 * second) * inverse).astype(jnp.bfloat16)


def diag_kernel(core, ens_ref, inc_ref, coords_ref, keep_ref, send_ref, sum_ref):
    members, levels, points = ens_ref.shape[1:]
    parts, _, step, _ = keep_ref.shape
    rows = members * levels
    half = points // 2
    places = coords_ref[0].astype(jnp.float32)
    left, right = left_rows(places), right_rows(places)
    upper = tile_of(left[:, :half], right)
    lower = tile_of(left[:, half:], right[:, half:])
    weighted = (ens_ref[0] * inc_ref[0][None]).reshape(rows, points)
    near, far = weighted[:, :half], weighted[:, half:]
    field_near = jnp.dot(near, upper[:, :half], preferred_element_type=jnp.float32) + lax.dot_general(
        far, upper[:, half:], (((1,), (1,)), ((), ())), preferred_element_type=jnp.float32
    )
    field_far = jnp.dot(near, upper[:, half:], preferred_element_type=jnp.float32) + jnp.dot(
        far, lower, preferred_element_type=jnp.float32
    )
    block = ens_ref[0].astype(jnp.float32)
    sum_ref[:, :half] = jnp.sum(block[:, :, :half] * field_near.reshape(members, levels, half), axis=0)
    sum_ref[:, half:] = jnp.sum(block[:, :, half:] * field_far.reshape(members, levels, half), axis=0)
    for part in range(parts):
        mine = pl.multiple_of((2 * part + core[0]) * step, step)
        other = pl.multiple_of((2 * part + 1 - core[0]) * step, step)
        keep_ref[part, 0] = sum_ref[pl.ds(mine, step), :]
        send_ref[part, 0] = sum_ref[pl.ds(other, step), :]


def diag(ensemble, increment, coords, core, parts):
    blocks, members, levels, points = ensemble.shape
    step = levels // (2 * parts)
    out = jax.ShapeDtypeStruct((parts, blocks, step, points), jnp.float32)
    return pl.pallas_call(
        diag_kernel,
        grid_spec=pltpu.PrefetchScalarGridSpec(
            num_scalar_prefetch=1,
            grid=(blocks,),
            in_specs=[
                pl.BlockSpec((1, members, levels, points), lambda b, c: (b, 0, 0, 0)),
                pl.BlockSpec((1, levels, points), lambda b, c: (b, 0, 0)),
                pl.BlockSpec((1, 2, points), lambda b, c: (b, 0, 0)),
            ],
            out_specs=[pl.BlockSpec((parts, 1, step, points), lambda b, c: (0, b, 0, 0))] * 2,
            scratch_shapes=[pltpu.VMEM((levels, points), jnp.float32)],
        ),
        out_shape=[out, out],
        compiler_params=pltpu.CompilerParams(vmem_limit_bytes=60 * MIB),
        cost_estimate=pl.CostEstimate(flops=20_000_000_000, bytes_accessed=8_000_000, transcendentals=0),
        name="diag",
    )(core, ensemble, increment, coords)


def merge_kernel(row, keep_ref, got_ref, own_ref, *send_refs):
    parts = keep_ref.shape[0]
    own_ref[...] = keep_ref[row[0]] + got_ref[row[0]]
    for shift, send_ref in enumerate(send_refs, 1):
        there = lax.rem(row[0] + shift, parts)
        send_ref[...] = (keep_ref[there] + got_ref[there]).astype(send_ref.dtype)


def merge(keep, got, row):
    parts = keep.shape[0]
    out = [jax.ShapeDtypeStruct(keep.shape[1:], jnp.float32)]
    out += [jax.ShapeDtypeStruct(keep.shape[1:], jnp.bfloat16)] * (parts - 1)
    return pl.pallas_call(
        merge_kernel,
        in_specs=[pl.BlockSpec(memory_space=pltpu.SMEM)] + [pl.BlockSpec(memory_space=pltpu.VMEM)] * 2,
        out_specs=[pl.BlockSpec(memory_space=pltpu.VMEM)] * parts,
        out_shape=out,
        compiler_params=pltpu.CompilerParams(vmem_limit_bytes=16 * MIB),
        name="merge",
    )(row, keep, got)


def tiles_kernel(pairs, first, places_ref, out_ref, tile_ref, sem):
    def copy(within):
        return pltpu.make_async_copy(tile_ref.at[within], out_ref.at[within], sem.at[within])

    for within in range(tile_ref.shape[0]):
        index = first[0] + within
        left = left_rows(places_ref[pairs[0, index], -2:, :].astype(jnp.float32))
        right = right_rows(places_ref[pairs[1, index], -2:, :].astype(jnp.float32))
        tile_ref[within] = tile_of(left, right)
        copy(within).start()
    for within in range(tile_ref.shape[0]):
        copy(within).wait()


def tiles(places, pairs, first):
    shape = (PAIR_GROUP, places.shape[2], places.shape[2])
    return pl.pallas_call(
        tiles_kernel,
        in_specs=[
            pl.BlockSpec(memory_space=pltpu.SMEM),
            pl.BlockSpec(memory_space=pltpu.SMEM),
            pl.BlockSpec(memory_space=pltpu.VMEM),
        ],
        out_specs=pl.BlockSpec(memory_space=pl.ANY),
        out_shape=pltpu.HBM(shape, jnp.bfloat16),
        scratch_shapes=[pltpu.VMEM(shape, jnp.bfloat16), pltpu.SemaphoreType.DMA((PAIR_GROUP,))],
        compiler_params=pltpu.CompilerParams(vmem_limit_bytes=60 * MIB),
        cost_estimate=pl.CostEstimate(flops=4_000_000_000, bytes_accessed=2_000_000, transcendentals=0),
        name="tiles",
    )(pairs, first, places)


def apply_kernel(
    pairs, count, core, got_ref, small_ref, *refs,
):
    *stacks, out_ref, ens_ref, inc_ref, weighted_ref, field_ref, tiles_ref, ens_sem, inc_sem, tiles_sem = refs
    slot_total, sources, rows, points = ens_ref.shape
    step = inc_ref.shape[1]
    groups = len(stacks)
    lane_chunks = points // LANES
    every = sources * rows

    def ens_copies(slot):
        return [
            pltpu.make_async_copy(
                got_ref.at[slot, :, lane * rows : (lane + 1) * rows, :],
                ens_ref.at[slot, :, :, lane * LANES : (lane + 1) * LANES],
                ens_sem.at[slot, lane],
            )
            for lane in range(lane_chunks)
        ]

    inc_copy = pltpu.make_async_copy(small_ref.at[:, :step, :], inc_ref, inc_sem)

    def tile_copy(group):
        return pltpu.make_async_copy(stacks[group], tiles_ref.at[group], tiles_sem.at[group])

    inc_copy.start()
    for slot in range(slot_total):
        for copy in ens_copies(slot):
            copy.start()
    for group in range(groups):
        tile_copy(group).start()
    inc_copy.wait()
    for slot in range(slot_total):
        field_ref[slot] = jnp.zeros((every, points), jnp.float32)
        for copy in ens_copies(slot):
            copy.wait()
        block = ens_ref[slot].reshape(every // step, step, points)
        weighted_ref[slot] = (block * inc_ref[slot][None]).reshape(every, points)

    def some(group, row, within, number):
        products = []
        for each in range(number):
            first, second = pairs[0, row + each], pairs[1, row + each]
            tile = tiles_ref[group, within + each]
            to_first = lax.dot_general(
                weighted_ref[second], tile, (((1,), (1,)), ((), ())), preferred_element_type=jnp.float32
            )
            to_second = jnp.dot(weighted_ref[first], tile, preferred_element_type=jnp.float32)
            products += [(first, to_first), (second, to_second)]
        for slot, product in products:
            field_ref[slot] += product

    def turn(group, carry):
        away = core[0] * (groups // 2)
        row = PAIR_GROUP * jnp.where(group < groups // 2, group + away, group - away)
        live = count[0] - row
        pltpu.make_async_copy(stacks[0], tiles_ref.at[group], tiles_sem.at[group]).wait()

        @pl.when(live >= PAIR_GROUP)
        def _():
            some(group, row, 0, PAIR_GROUP)

        @pl.when(live < PAIR_GROUP)
        def _():
            def one(within, inner):
                some(group, row + within, within, 1)
                return inner

            lax.fori_loop(0, jnp.maximum(live, 0), one, 0)

        return carry

    lax.fori_loop(0, groups, turn, 0)

    for slot in range(slot_total):
        product = ens_ref[slot].reshape(every, points).astype(jnp.float32) * field_ref[slot]
        out_ref[slot] = jnp.sum(product.reshape(every // step, step, points), axis=0)


def apply_pairs(got, small, stacks, pairs, count, core, members, step):
    slot_total, sources, rows, _ = got.shape
    points = stacks[0].shape[2]
    lane_chunks = points // LANES
    every = sources * members * step
    return pl.pallas_call(
        apply_kernel,
        in_specs=[
            pl.BlockSpec(memory_space=pltpu.SMEM),
            pl.BlockSpec(memory_space=pltpu.SMEM),
            pl.BlockSpec(memory_space=pltpu.SMEM),
            pl.BlockSpec(memory_space=pl.ANY),
            *[pl.BlockSpec(memory_space=pl.ANY)] * (len(stacks) + 1),
        ],
        out_specs=pl.BlockSpec(memory_space=pltpu.VMEM),
        scratch_shapes=[
            pltpu.VMEM((slot_total, sources, members * step, points), jnp.bfloat16),
            pltpu.VMEM((slot_total, step, points), jnp.bfloat16),
            pltpu.VMEM((slot_total, every, points), jnp.bfloat16),
            pltpu.VMEM((slot_total, every, points), jnp.float32),
            pltpu.VMEM((len(stacks), *stacks[0].shape), jnp.bfloat16),
            pltpu.SemaphoreType.DMA((slot_total, lane_chunks)),
            pltpu.SemaphoreType.DMA,
            pltpu.SemaphoreType.DMA((len(stacks),)),
        ],
        out_shape=jax.ShapeDtypeStruct((slot_total, step, points), jnp.float32),
        compiler_params=pltpu.CompilerParams(vmem_limit_bytes=60 * MIB),
        cost_estimate=pl.CostEstimate(flops=9_000_000_000, bytes_accessed=22_000_000, transcendentals=0),
        name="apply",
    )(pairs, count, core, got, small, *stacks)


def finish_kernel(slots, own_ref, *refs, scale):
    *part_refs, back_ref, out_ref = refs
    total = own_ref[...]
    for part_ref in part_refs:
        total = total + part_ref[...].astype(jnp.float32)
    out_ref[...] = total * scale
    for owner in range(back_ref.shape[0]):
        slot = slots[owner]
        out_ref[slot] = out_ref[slot] + back_ref[owner] * scale


def finish(own, parts, back, slots, scale):
    return pl.pallas_call(
        functools.partial(finish_kernel, scale=scale),
        in_specs=[pl.BlockSpec(memory_space=pltpu.SMEM)] + [pl.BlockSpec(memory_space=pltpu.VMEM)] * (len(parts) + 2),
        out_specs=pl.BlockSpec(memory_space=pltpu.VMEM),
        out_shape=jax.ShapeDtypeStruct(own.shape, jnp.float32),
        compiler_params=pltpu.CompilerParams(vmem_limit_bytes=16 * MIB),
        name="finish",
    )(slots, own, *parts, back)


def per_device(ensemble, increment, coords, sent_slots, pair_list, pair_count):
    blocks, members, levels, points = ensemble.shape
    regions = lax.axis_size("region")
    groups = lax.axis_size("member")
    step = levels // groups
    slots = sent_slots.reshape(-1)
    pairs = pair_list.T
    own = lax.axis_index("member").reshape(1).astype(jnp.int32)
    small = lax.all_to_all(select(increment, coords, slots, own, step), "region", 0, 0, tiled=True)
    big = pack(ensemble, slots, groups)
    big, small = lax.optimization_barrier((big, small))
    got = lax.all_to_all(
        big.reshape(regions * groups, -1, LANES), ("region", "member"), 0, 0, tiled=True
    ).reshape(regions, groups, -1, LANES)
    swap = [(i, i ^ 1) for i in range(groups)]
    core, row = own & 1, own >> 1
    rows = groups // 2
    share = pairs.shape[1] // 2
    mine = [tiles(small, pairs, core * share + start) for start in range(0, share, PAIR_GROUP)]
    theirs = [lax.ppermute(stack, "member", swap) for stack in mine]
    keep, send = diag(ensemble, increment, coords, core, rows)
    merged = merge(keep, lax.ppermute(send, "member", swap), row)
    parts = [
        lax.ppermute(part, "member", [(i, (i + 2 * hop) % groups) for i in range(groups)])
        for hop, part in enumerate(merged[1:], 1)
    ]
    got, own_part = lax.optimization_barrier((got, merged[0]))
    stacks = [in_hbm(stack) for stack in mine + theirs]
    partial = apply_pairs(in_hbm(got), in_hbm(small), stacks, pairs, pair_count, core, members, step)
    partial, parts = lax.optimization_barrier((partial, parts))
    back = lax.all_to_all(partial, "region", 0, 0, tiled=True)
    return finish(own_part, parts, back, slots, 1.0 / (members * groups - 1))


def solution(mesh):
    in_specs = (
        P("region", "member", None, None),
        P("region", None, None),
        P("region", None, None),
        P("region", None, None),
        P("region", None),
        P("region"),
    )
    out_specs = P("region", "member", None)
    return jax.shard_map(
        per_device, mesh=mesh, in_specs=in_specs, out_specs=out_specs, check_vma=False
    )
```

```python
import functools

import jax
import jax.numpy as jnp
from jax import lax
from jax.experimental import pallas as pl
from jax.experimental.pallas import tpu as pltpu
from jax.sharding import PartitionSpec as P

LANES = 128
PAIR_GROUP = 4
MIB = 1024 * 1024
UNIT = 12.0**-0.2
UNIT2 = UNIT * UNIT
LEAST = UNIT2 * 2.0**-12


def select_kernel(slots, own, inc_ref, coords_ref, out_ref, sem):
    total, rows, _ = out_ref.shape
    step = rows - coords_ref.shape[1]
    first = pl.multiple_of(own[0] * step, step)

    def copy(owner):
        return pltpu.make_async_copy(
            inc_ref.at[slots[owner], pl.ds(first, step), :], out_ref.at[owner, :step, :], sem.at[owner]
        )

    for owner in range(total):
        copy(owner).start()
    for owner in range(total):
        out_ref[owner, step:, :] = coords_ref[slots[owner]]
    for owner in range(total):
        copy(owner).wait()


def select(increment, coords, slots, own, step):
    total, points = slots.shape[0], coords.shape[2]
    return pl.pallas_call(
        select_kernel,
        in_specs=[
            pl.BlockSpec(memory_space=pltpu.SMEM),
            pl.BlockSpec(memory_space=pltpu.SMEM),
            pl.BlockSpec(memory_space=pl.ANY),
            pl.BlockSpec(memory_space=pltpu.VMEM),
        ],
        out_specs=pl.BlockSpec(memory_space=pltpu.VMEM),
        out_shape=jax.ShapeDtypeStruct((total, step + coords.shape[1], points), coords.dtype),
        scratch_shapes=[pltpu.SemaphoreType.DMA((total,))],
        compiler_params=pltpu.CompilerParams(vmem_limit_bytes=60 * MIB),
        name="select",
    )(slots, own, increment, coords)


def pack_kernel(slots, ens_ref, big_ref, ens_buf, out_buf, in_sem, out_sem):
    total, members, levels, points = ens_buf.shape
    parts = out_buf.shape[1]
    step = levels // parts
    lane_chunks = points // LANES

    def ens_copy(owner):
        return pltpu.make_async_copy(ens_ref.at[slots[owner]], ens_buf.at[owner], in_sem.at[owner])

    def out_copy(owner):
        return pltpu.make_async_copy(out_buf.at[owner], big_ref.at[owner], out_sem.at[owner])

    for owner in range(total):
        ens_copy(owner).start()
    for owner in range(total):
        ens_copy(owner).wait()
        for part in range(parts):
            here = slice(part * step, (part + 1) * step)
            for lane in range(lane_chunks):
                out_buf[owner, part, lane * members * step : (lane + 1) * members * step, :] = ens_buf[
                    owner, :, here, lane * LANES : (lane + 1) * LANES
                ].reshape(members * step, LANES)
        out_copy(owner).start()
    for owner in range(total):
        out_copy(owner).wait()


def pack(ensemble, slots, parts):
    blocks, members, levels, points = ensemble.shape
    total = slots.shape[0]
    rows = members * (levels // parts) * (points // LANES)
    return pl.pallas_call(
        pack_kernel,
        in_specs=[pl.BlockSpec(memory_space=pltpu.SMEM), pl.BlockSpec(memory_space=pl.ANY)],
        out_specs=pl.BlockSpec(memory_space=pl.ANY),
        out_shape=jax.ShapeDtypeStruct((total, parts, rows, LANES), ensemble.dtype),
        scratch_shapes=[
            pltpu.VMEM((total, members, levels, points), ensemble.dtype),
            pltpu.VMEM((total, parts, rows, LANES), ensemble.dtype),
            pltpu.SemaphoreType.DMA((total,)),
            pltpu.SemaphoreType.DMA((total,)),
        ],
        compiler_params=pltpu.CompilerParams(vmem_limit_bytes=60 * MIB),
        name="pack",
    )(slots, ensemble)


def in_hbm(value):
    return pltpu.with_memory_space_constraint(value, pltpu.HBM)


def three_parts(value):
    first = value.astype(jnp.bfloat16).astype(jnp.float32)
    rest = value - first
    second = rest.astype(jnp.bfloat16).astype(jnp.float32)
    return [first, second, rest - second]


def left_rows(places):
    east, north = places[0:1], places[1:2]
    one = jnp.ones_like(east)
    norm = UNIT2 * (east * east + north * north)
    rows = three_parts((-2.0 * UNIT2) * east) + three_parts((-2.0 * UNIT2) * north) + three_parts(norm)
    rows = rows + [one] * 3 + [jnp.zeros_like(east)] * 4
    return jnp.concatenate(rows, axis=0).astype(jnp.bfloat16)


def right_rows(places):
    east, north = places[0:1], places[1:2]
    one = jnp.ones_like(east)
    norm = UNIT2 * (east * east + north * north)
    rows = [east] * 3 + [north] * 3 + [one] * 3 + three_parts(norm) + [jnp.zeros_like(east)] * 4
    return jnp.concatenate(rows, axis=0).astype(jnp.bfloat16)


def tile_of(left, right):
    squared = lax.dot_general(left, right, (((0,), (0,)), ((), ())), preferred_element_type=jnp.float32)
    squared = jnp.maximum(squared, LEAST)
    inverse = lax.rsqrt(squared)
    z = squared * inverse
    outer = jnp.maximum(2.0 * UNIT - z, 0.0)
    inner = jnp.maximum(UNIT - z, 0.0)
    outer2 = outer * outer
    inner2 = inner * inner
    shifted = z + 2.0 * UNIT
    first = (outer2 * outer2) * (z * shifted - 0.5 * UNIT2)
    second = (inner2 * inner2) * (inner * shifted)
    return ((first + 4.0 * second) * inverse).astype(jnp.bfloat16)


def diag_kernel(core, ens_ref, inc_ref, coords_ref, keep_ref, send_ref, sum_ref):
    members, levels, points = ens_ref.shape[1:]
    parts, _, step, _ = keep_ref.shape
    rows = members * levels
    half = points // 2
    places = coords_ref[0].astype(jnp.float32)
    left, right = left_rows(places), right_rows(places)
    upper = tile_of(left[:, :half], right)
    lower = tile_of(left[:, half:], right[:, half:])
    weighted = (ens_ref[0] * inc_ref[0][None]).reshape(rows, points)
    near, far = weighted[:, :half], weighted[:, half:]
    field_near = jnp.dot(near, upper[:, :half], preferred_element_type=jnp.float32) + lax.dot_general(
        far, upper[:, half:], (((1,), (1,)), ((), ())), preferred_element_type=jnp.float32
    )
    field_far = jnp.dot(near, upper[:, half:], preferred_element_type=jnp.float32) + jnp.dot(
        far, lower, preferred_element_type=jnp.float32
    )
    block = ens_ref[0].astype(jnp.float32)
    sum_ref[:, :half] = jnp.sum(block[:, :, :half] * field_near.reshape(members, levels, half), axis=0)
    sum_ref[:, half:] = jnp.sum(block[:, :, half:] * field_far.reshape(members, levels, half), axis=0)
    for part in range(parts):
        mine = pl.multiple_of((2 * part + core[0]) * step, step)
        other = pl.multiple_of((2 * part + 1 - core[0]) * step, step)
        keep_ref[part, 0] = sum_ref[pl.ds(mine, step), :]
        send_ref[part, 0] = sum_ref[pl.ds(other, step), :]


def diag(ensemble, increment, coords, core, parts):
    blocks, members, levels, points = ensemble.shape
    step = levels // (2 * parts)
    out = jax.ShapeDtypeStruct((parts, blocks, step, points), jnp.float32)
    return pl.pallas_call(
        diag_kernel,
        grid_spec=pltpu.PrefetchScalarGridSpec(
            num_scalar_prefetch=1,
            grid=(blocks,),
            in_specs=[
                pl.BlockSpec((1, members, levels, points), lambda b, c: (b, 0, 0, 0)),
                pl.BlockSpec((1, levels, points), lambda b, c: (b, 0, 0)),
                pl.BlockSpec((1, 2, points), lambda b, c: (b, 0, 0)),
            ],
            out_specs=[pl.BlockSpec((parts, 1, step, points), lambda b, c: (0, b, 0, 0))] * 2,
            scratch_shapes=[pltpu.VMEM((levels, points), jnp.float32)],
        ),
        out_shape=[out, out],
        compiler_params=pltpu.CompilerParams(vmem_limit_bytes=60 * MIB),
        cost_estimate=pl.CostEstimate(flops=20_000_000_000, bytes_accessed=8_000_000, transcendentals=0),
        name="diag",
    )(core, ensemble, increment, coords)


def merge_kernel(row, keep_ref, got_ref, own_ref, *send_refs):
    parts = keep_ref.shape[0]
    own_ref[...] = keep_ref[row[0]] + got_ref[row[0]]
    for shift, send_ref in enumerate(send_refs, 1):
        there = lax.rem(row[0] + shift, parts)
        send_ref[...] = (keep_ref[there] + got_ref[there]).astype(send_ref.dtype)


def merge(keep, got, row):
    parts = keep.shape[0]
    out = [jax.ShapeDtypeStruct(keep.shape[1:], jnp.float32)]
    out += [jax.ShapeDtypeStruct(keep.shape[1:], jnp.bfloat16)] * (parts - 1)
    return pl.pallas_call(
        merge_kernel,
        in_specs=[pl.BlockSpec(memory_space=pltpu.SMEM)] + [pl.BlockSpec(memory_space=pltpu.VMEM)] * 2,
        out_specs=[pl.BlockSpec(memory_space=pltpu.VMEM)] * parts,
        out_shape=out,
        compiler_params=pltpu.CompilerParams(vmem_limit_bytes=16 * MIB),
        name="merge",
    )(row, keep, got)


def tiles_kernel(pairs, first, places_ref, out_ref, tile_ref, sem):
    def copy(within):
        return pltpu.make_async_copy(tile_ref.at[within], out_ref.at[within], sem.at[within])

    for within in range(tile_ref.shape[0]):
        index = first[0] + within
        left = left_rows(places_ref[pairs[0, index], -2:, :].astype(jnp.float32))
        right = right_rows(places_ref[pairs[1, index], -2:, :].astype(jnp.float32))
        tile_ref[within] = tile_of(left, right)
        copy(within).start()
    for within in range(tile_ref.shape[0]):
        copy(within).wait()


def tiles(places, pairs, first):
    shape = (PAIR_GROUP, places.shape[2], places.shape[2])
    return pl.pallas_call(
        tiles_kernel,
        in_specs=[
            pl.BlockSpec(memory_space=pltpu.SMEM),
            pl.BlockSpec(memory_space=pltpu.SMEM),
            pl.BlockSpec(memory_space=pltpu.VMEM),
        ],
        out_specs=pl.BlockSpec(memory_space=pl.ANY),
        out_shape=pltpu.HBM(shape, jnp.bfloat16),
        scratch_shapes=[pltpu.VMEM(shape, jnp.bfloat16), pltpu.SemaphoreType.DMA((PAIR_GROUP,))],
        compiler_params=pltpu.CompilerParams(vmem_limit_bytes=60 * MIB),
        cost_estimate=pl.CostEstimate(flops=4_000_000_000, bytes_accessed=2_000_000, transcendentals=0),
        name="tiles",
    )(pairs, first, places)


def apply_kernel(
    pairs, count, core, got_ref, small_ref, *refs,
):
    *stacks, out_ref, ens_ref, inc_ref, weighted_ref, field_ref, tiles_ref, ens_sem, inc_sem, tiles_sem = refs
    slot_total, sources, rows, points = ens_ref.shape
    step = inc_ref.shape[1]
    groups = len(stacks)
    lane_chunks = points // LANES
    every = sources * rows

    def ens_copies(slot):
        return [
            pltpu.make_async_copy(
                got_ref.at[slot, :, lane * rows : (lane + 1) * rows, :],
                ens_ref.at[slot, :, :, lane * LANES : (lane + 1) * LANES],
                ens_sem.at[slot, lane],
            )
            for lane in range(lane_chunks)
        ]

    inc_copy = pltpu.make_async_copy(small_ref.at[:, :step, :], inc_ref, inc_sem)

    def tile_copy(group):
        return pltpu.make_async_copy(stacks[group], tiles_ref.at[group], tiles_sem.at[group])

    inc_copy.start()
    for slot in range(slot_total):
        for copy in ens_copies(slot):
            copy.start()
    for group in range(groups):
        tile_copy(group).start()
    inc_copy.wait()
    for slot in range(slot_total):
        field_ref[slot] = jnp.zeros((every, points), jnp.float32)
        for copy in ens_copies(slot):
            copy.wait()
        block = ens_ref[slot].reshape(every // step, step, points)
        weighted_ref[slot] = (block * inc_ref[slot][None]).reshape(every, points)

    def some(group, row, within, number):
        products = []
        for each in range(number):
            first, second = pairs[0, row + each], pairs[1, row + each]
            tile = tiles_ref[group, within + each]
            to_first = lax.dot_general(
                weighted_ref[second], tile, (((1,), (1,)), ((), ())), preferred_element_type=jnp.float32
            )
            to_second = jnp.dot(weighted_ref[first], tile, preferred_element_type=jnp.float32)
            products += [(first, to_first), (second, to_second)]
        for slot, product in products:
            field_ref[slot] += product

    def turn(group, carry):
        away = core[0] * (groups // 2)
        row = PAIR_GROUP * jnp.where(group < groups // 2, group + away, group - away)
        live = count[0] - row
        pltpu.make_async_copy(stacks[0], tiles_ref.at[group], tiles_sem.at[group]).wait()

        @pl.when(live >= PAIR_GROUP)
        def _():
            some(group, row, 0, PAIR_GROUP)

        @pl.when(live < PAIR_GROUP)
        def _():
            def one(within, inner):
                some(group, row + within, within, 1)
                return inner

            lax.fori_loop(0, jnp.maximum(live, 0), one, 0)

        return carry

    lax.fori_loop(0, groups, turn, 0)

    for slot in range(slot_total):
        product = ens_ref[slot].reshape(every, points).astype(jnp.float32) * field_ref[slot]
        out_ref[slot] = jnp.sum(product.reshape(every // step, step, points), axis=0).astype(out_ref.dtype)


def apply_pairs(got, small, stacks, pairs, count, core, members, step):
    slot_total, sources, rows, _ = got.shape
    points = stacks[0].shape[2]
    lane_chunks = points // LANES
    every = sources * members * step
    return pl.pallas_call(
        apply_kernel,
        in_specs=[
            pl.BlockSpec(memory_space=pltpu.SMEM),
            pl.BlockSpec(memory_space=pltpu.SMEM),
            pl.BlockSpec(memory_space=pltpu.SMEM),
            pl.BlockSpec(memory_space=pl.ANY),
            *[pl.BlockSpec(memory_space=pl.ANY)] * (len(stacks) + 1),
        ],
        out_specs=pl.BlockSpec(memory_space=pltpu.VMEM),
        scratch_shapes=[
            pltpu.VMEM((slot_total, sources, members * step, points), jnp.bfloat16),
            pltpu.VMEM((slot_total, step, points), jnp.bfloat16),
            pltpu.VMEM((slot_total, every, points), jnp.bfloat16),
            pltpu.VMEM((slot_total, every, points), jnp.float32),
            pltpu.VMEM((len(stacks), *stacks[0].shape), jnp.bfloat16),
            pltpu.SemaphoreType.DMA((slot_total, lane_chunks)),
            pltpu.SemaphoreType.DMA,
            pltpu.SemaphoreType.DMA((len(stacks),)),
        ],
        out_shape=jax.ShapeDtypeStruct((slot_total, step, points), jnp.bfloat16),
        compiler_params=pltpu.CompilerParams(vmem_limit_bytes=60 * MIB),
        cost_estimate=pl.CostEstimate(flops=100_000_000, bytes_accessed=22_000_000, transcendentals=0),
        name="apply",
    )(pairs, count, core, got, small, *stacks)


def finish_kernel(slots, own_ref, *refs, scale):
    *part_refs, back_ref, out_ref = refs
    total = own_ref[...]
    for part_ref in part_refs:
        total = total + part_ref[...].astype(jnp.float32)
    out_ref[...] = total * scale
    for owner in range(back_ref.shape[0]):
        slot = slots[owner]
        out_ref[slot] = out_ref[slot] + back_ref[owner].astype(jnp.float32) * scale


def finish(own, parts, back, slots, scale):
    return pl.pallas_call(
        functools.partial(finish_kernel, scale=scale),
        in_specs=[pl.BlockSpec(memory_space=pltpu.SMEM)] + [pl.BlockSpec(memory_space=pltpu.VMEM)] * (len(parts) + 2),
        out_specs=pl.BlockSpec(memory_space=pltpu.VMEM),
        out_shape=jax.ShapeDtypeStruct(own.shape, jnp.float32),
        compiler_params=pltpu.CompilerParams(vmem_limit_bytes=16 * MIB),
        name="finish",
    )(slots, own, *parts, back)


def per_device(ensemble, increment, coords, sent_slots, pair_list, pair_count):
    blocks, members, levels, points = ensemble.shape
    regions = lax.axis_size("region")
    groups = lax.axis_size("member")
    step = levels // groups
    slots = sent_slots.reshape(-1)
    pairs = pair_list.T
    own = lax.axis_index("member").reshape(1).astype(jnp.int32)
    small = lax.all_to_all(select(increment, coords, slots, own, step), "region", 0, 0, tiled=True)
    big = pack(ensemble, slots, groups)
    big, small = lax.optimization_barrier((big, small))
    got = lax.all_to_all(
        big.reshape(regions * groups, -1, LANES), ("region", "member"), 0, 0, tiled=True
    ).reshape(regions, groups, -1, LANES)
    swap = [(i, i ^ 1) for i in range(groups)]
    core, row = own & 1, own >> 1
    rows = groups // 2
    share = pairs.shape[1] // 2
    mine = [tiles(small, pairs, core * share + start) for start in range(0, share, PAIR_GROUP)]
    theirs = [lax.ppermute(stack, "member", swap) for stack in mine]
    keep, send = diag(ensemble, increment, coords, core, rows)
    merged = merge(keep, lax.ppermute(send, "member", swap), row)
    parts = [
        lax.ppermute(part, "member", [(i, (i + 2 * hop) % groups) for i in range(groups)])
        for hop, part in enumerate(merged[1:], 1)
    ]
    got, own_part = lax.optimization_barrier((got, merged[0]))
    stacks = [in_hbm(stack) for stack in mine + theirs]
    partial = apply_pairs(in_hbm(got), in_hbm(small), stacks, pairs, pair_count, core, members, step)
    partial, parts = lax.optimization_barrier((partial, parts))
    back = lax.all_to_all(partial, "region", 0, 0, tiled=True)
    return finish(own_part, parts, back, slots, 1.0 / (members * groups - 1))


def solution(mesh):
    in_specs = (
        P("region", "member", None, None),
        P("region", None, None),
        P("region", None, None),
        P("region", None, None),
        P("region", None),
        P("region"),
    )
    out_specs = P("region", "member", None)
    return jax.shard_map(
        per_device, mesh=mesh, in_specs=in_specs, out_specs=out_specs, check_vma=False
    )
```

```python
import functools

import jax
import jax.numpy as jnp
from jax import lax
from jax.experimental import pallas as pl
from jax.experimental.pallas import tpu as pltpu
from jax.sharding import PartitionSpec as P

LANES = 128
PAIR_GROUP = 4
DIAG_GROUP = 2
MIB = 1024 * 1024
UNIT = 12.0**-0.2
UNIT2 = UNIT * UNIT
LEAST = UNIT2 * 2.0**-12


def select_kernel(slots, own, inc_ref, coords_ref, out_ref, sem):
    total, rows, _ = out_ref.shape
    step = rows - coords_ref.shape[1]
    first = pl.multiple_of(own[0] * step, step)

    def copy(owner):
        return pltpu.make_async_copy(
            inc_ref.at[slots[owner], pl.ds(first, step), :], out_ref.at[owner, :step, :], sem.at[owner]
        )

    for owner in range(total):
        copy(owner).start()
    for owner in range(total):
        out_ref[owner, step:, :] = coords_ref[slots[owner]]
    for owner in range(total):
        copy(owner).wait()


def select(increment, coords, slots, own, step):
    total, points = slots.shape[0], coords.shape[2]
    return pl.pallas_call(
        select_kernel,
        in_specs=[
            pl.BlockSpec(memory_space=pltpu.SMEM),
            pl.BlockSpec(memory_space=pltpu.SMEM),
            pl.BlockSpec(memory_space=pl.ANY),
            pl.BlockSpec(memory_space=pltpu.VMEM),
        ],
        out_specs=pl.BlockSpec(memory_space=pltpu.VMEM),
        out_shape=jax.ShapeDtypeStruct((total, step + coords.shape[1], points), coords.dtype),
        scratch_shapes=[pltpu.SemaphoreType.DMA((total,))],
        compiler_params=pltpu.CompilerParams(vmem_limit_bytes=60 * MIB),
        name="select",
    )(slots, own, increment, coords)


def pack_kernel(slots, ens_ref, big_ref, ens_buf, out_buf, in_sem, out_sem):
    total, members, levels, points = ens_buf.shape
    parts = out_buf.shape[1]
    step = levels // parts
    lane_chunks = points // LANES

    def ens_copy(owner):
        return pltpu.make_async_copy(ens_ref.at[slots[owner]], ens_buf.at[owner], in_sem.at[owner])

    def out_copy(owner):
        return pltpu.make_async_copy(out_buf.at[owner], big_ref.at[owner], out_sem.at[owner])

    for owner in range(total):
        ens_copy(owner).start()
    for owner in range(total):
        ens_copy(owner).wait()
        for part in range(parts):
            here = slice(part * step, (part + 1) * step)
            for lane in range(lane_chunks):
                out_buf[owner, part, lane * members * step : (lane + 1) * members * step, :] = ens_buf[
                    owner, :, here, lane * LANES : (lane + 1) * LANES
                ].reshape(members * step, LANES)
        out_copy(owner).start()
    for owner in range(total):
        out_copy(owner).wait()


def pack(ensemble, slots, parts):
    blocks, members, levels, points = ensemble.shape
    total = slots.shape[0]
    rows = members * (levels // parts) * (points // LANES)
    return pl.pallas_call(
        pack_kernel,
        in_specs=[pl.BlockSpec(memory_space=pltpu.SMEM), pl.BlockSpec(memory_space=pl.ANY)],
        out_specs=pl.BlockSpec(memory_space=pl.ANY),
        out_shape=jax.ShapeDtypeStruct((total, parts, rows, LANES), ensemble.dtype),
        scratch_shapes=[
            pltpu.VMEM((total, members, levels, points), ensemble.dtype),
            pltpu.VMEM((total, parts, rows, LANES), ensemble.dtype),
            pltpu.SemaphoreType.DMA((total,)),
            pltpu.SemaphoreType.DMA((total,)),
        ],
        compiler_params=pltpu.CompilerParams(vmem_limit_bytes=60 * MIB),
        name="pack",
    )(slots, ensemble)


def in_hbm(value):
    return pltpu.with_memory_space_constraint(value, pltpu.HBM)


def three_parts(value):
    first = value.astype(jnp.bfloat16).astype(jnp.float32)
    rest = value - first
    second = rest.astype(jnp.bfloat16).astype(jnp.float32)
    return [first, second, rest - second]


def left_rows(places):
    east, north = places[0:1], places[1:2]
    one = jnp.ones_like(east)
    norm = UNIT2 * (east * east + north * north)
    rows = three_parts((-2.0 * UNIT2) * east) + three_parts((-2.0 * UNIT2) * north) + three_parts(norm)
    rows = rows + [one] * 3 + [jnp.zeros_like(east)] * 4
    return jnp.concatenate(rows, axis=0).astype(jnp.bfloat16)


def right_rows(places):
    east, north = places[0:1], places[1:2]
    one = jnp.ones_like(east)
    norm = UNIT2 * (east * east + north * north)
    rows = [east] * 3 + [north] * 3 + [one] * 3 + three_parts(norm) + [jnp.zeros_like(east)] * 4
    return jnp.concatenate(rows, axis=0).astype(jnp.bfloat16)


def tile_of(left, right):
    squared = lax.dot_general(left, right, (((0,), (0,)), ((), ())), preferred_element_type=jnp.float32)
    squared = jnp.maximum(squared, LEAST)
    inverse = lax.rsqrt(squared)
    z = squared * inverse
    outer = jnp.maximum(2.0 * UNIT - z, 0.0)
    inner = jnp.maximum(UNIT - z, 0.0)
    outer2 = outer * outer
    inner2 = inner * inner
    shifted = z + 2.0 * UNIT
    first = (outer2 * outer2) * (z * shifted - 0.5 * UNIT2)
    second = (inner2 * inner2) * (inner * shifted)
    return ((first + 4.0 * second) * inverse).astype(jnp.bfloat16)


def diag_block(block_index, core, ens_ref, inc_ref, coords_ref, keep_ref, send_ref, sum_ref):
    members, levels, points = ens_ref.shape[1:]
    parts, _, step, _ = keep_ref.shape
    rows = members * levels
    half = points // 2
    places = coords_ref[block_index].astype(jnp.float32)
    left, right = left_rows(places), right_rows(places)
    upper = tile_of(left[:, :half], right)
    lower = tile_of(left[:, half:], right[:, half:])
    weighted = (ens_ref[block_index] * inc_ref[block_index][None]).reshape(rows, points)
    near, far = weighted[:, :half], weighted[:, half:]
    field_near = jnp.dot(near, upper[:, :half], preferred_element_type=jnp.float32) + lax.dot_general(
        far, upper[:, half:], (((1,), (1,)), ((), ())), preferred_element_type=jnp.float32
    )
    field_far = jnp.dot(near, upper[:, half:], preferred_element_type=jnp.float32) + jnp.dot(
        far, lower, preferred_element_type=jnp.float32
    )
    block = ens_ref[block_index].astype(jnp.float32)
    sum_ref[block_index, :, :half] = jnp.sum(block[:, :, :half] * field_near.reshape(members, levels, half), axis=0)
    sum_ref[block_index, :, half:] = jnp.sum(block[:, :, half:] * field_far.reshape(members, levels, half), axis=0)
    for part in range(parts):
        mine = pl.multiple_of((2 * part + core[0]) * step, step)
        other = pl.multiple_of((2 * part + 1 - core[0]) * step, step)
        keep_ref[part, block_index] = sum_ref[block_index, pl.ds(mine, step), :]
        send_ref[part, block_index] = sum_ref[block_index, pl.ds(other, step), :]


def diag_kernel(core, ens_ref, *refs):
    for block_index in range(ens_ref.shape[0]):
        diag_block(block_index, core, ens_ref, *refs)


def diag(ensemble, increment, coords, core, parts):
    blocks, members, levels, points = ensemble.shape
    step = levels // (2 * parts)
    out = jax.ShapeDtypeStruct((parts, blocks, step, points), jnp.float32)
    return pl.pallas_call(
        diag_kernel,
        grid_spec=pltpu.PrefetchScalarGridSpec(
            num_scalar_prefetch=1,
            grid=(blocks // DIAG_GROUP,),
            in_specs=[
                pl.BlockSpec((DIAG_GROUP, members, levels, points), lambda b, c: (b, 0, 0, 0)),
                pl.BlockSpec((DIAG_GROUP, levels, points), lambda b, c: (b, 0, 0)),
                pl.BlockSpec((DIAG_GROUP, 2, points), lambda b, c: (b, 0, 0)),
            ],
            out_specs=[pl.BlockSpec((parts, DIAG_GROUP, step, points), lambda b, c: (0, b, 0, 0))] * 2,
            scratch_shapes=[pltpu.VMEM((DIAG_GROUP, levels, points), jnp.float32)],
        ),
        out_shape=[out, out],
        compiler_params=pltpu.CompilerParams(vmem_limit_bytes=60 * MIB),
        cost_estimate=pl.CostEstimate(flops=20_000_000_000, bytes_accessed=8_000_000, transcendentals=0),
        name="diag",
    )(core, ensemble, increment, coords)


def merge_kernel(row, keep_ref, got_ref, own_ref, *send_refs):
    parts = keep_ref.shape[0]
    own_ref[...] = keep_ref[row[0]] + got_ref[row[0]]
    for shift, send_ref in enumerate(send_refs, 1):
        there = lax.rem(row[0] + shift, parts)
        send_ref[...] = (keep_ref[there] + got_ref[there]).astype(send_ref.dtype)


def merge(keep, got, row):
    parts = keep.shape[0]
    out = [jax.ShapeDtypeStruct(keep.shape[1:], jnp.float32)]
    out += [jax.ShapeDtypeStruct(keep.shape[1:], jnp.bfloat16)] * (parts - 1)
    return pl.pallas_call(
        merge_kernel,
        in_specs=[pl.BlockSpec(memory_space=pltpu.SMEM)] + [pl.BlockSpec(memory_space=pltpu.VMEM)] * 2,
        out_specs=[pl.BlockSpec(memory_space=pltpu.VMEM)] * parts,
        out_shape=out,
        compiler_params=pltpu.CompilerParams(vmem_limit_bytes=16 * MIB),
        name="merge",
    )(row, keep, got)


def tiles_kernel(pairs, first, places_ref, out_ref, tile_ref, sem):
    def copy(within):
        return pltpu.make_async_copy(tile_ref.at[within], out_ref.at[within], sem.at[within])

    for within in range(tile_ref.shape[0]):
        index = first[0] + within
        left = left_rows(places_ref[pairs[0, index], -2:, :].astype(jnp.float32))
        right = right_rows(places_ref[pairs[1, index], -2:, :].astype(jnp.float32))
        tile_ref[within] = tile_of(left, right)
        copy(within).start()
    for within in range(tile_ref.shape[0]):
        copy(within).wait()


def tiles(places, pairs, first):
    shape = (PAIR_GROUP, places.shape[2], places.shape[2])
    return pl.pallas_call(
        tiles_kernel,
        in_specs=[
            pl.BlockSpec(memory_space=pltpu.SMEM),
            pl.BlockSpec(memory_space=pltpu.SMEM),
            pl.BlockSpec(memory_space=pltpu.VMEM),
        ],
        out_specs=pl.BlockSpec(memory_space=pl.ANY),
        out_shape=pltpu.HBM(shape, jnp.bfloat16),
        scratch_shapes=[pltpu.VMEM(shape, jnp.bfloat16), pltpu.SemaphoreType.DMA((PAIR_GROUP,))],
        compiler_params=pltpu.CompilerParams(vmem_limit_bytes=60 * MIB),
        cost_estimate=pl.CostEstimate(flops=4_000_000_000, bytes_accessed=2_000_000, transcendentals=0),
        name="tiles",
    )(pairs, first, places)


def apply_kernel(
    pairs, count, core, got_ref, small_ref, *refs,
):
    *stacks, out_ref, ens_ref, inc_ref, weighted_ref, field_ref, tiles_ref, ens_sem, inc_sem, tiles_sem = refs
    slot_total, sources, rows, points = ens_ref.shape
    step = inc_ref.shape[1]
    groups = len(stacks)
    lane_chunks = points // LANES
    every = sources * rows

    def ens_copies(slot):
        return [
            pltpu.make_async_copy(
                got_ref.at[slot, :, lane * rows : (lane + 1) * rows, :],
                ens_ref.at[slot, :, :, lane * LANES : (lane + 1) * LANES],
                ens_sem.at[slot, lane],
            )
            for lane in range(lane_chunks)
        ]

    inc_copy = pltpu.make_async_copy(small_ref.at[:, :step, :], inc_ref, inc_sem)

    def tile_copy(group):
        return pltpu.make_async_copy(stacks[group], tiles_ref.at[group], tiles_sem.at[group])

    inc_copy.start()
    for slot in range(slot_total):
        for copy in ens_copies(slot):
            copy.start()
    for group in range(2):
        tile_copy(group).start()
    inc_copy.wait()
    for slot in range(slot_total):
        field_ref[slot] = jnp.zeros((every, points), jnp.float32)
        for copy in ens_copies(slot):
            copy.wait()
        if slot % 2 == 1 and slot // 2 + 2 < groups:
            tile_copy(slot // 2 + 2).start()
        block = ens_ref[slot].reshape(every // step, step, points)
        weighted_ref[slot] = (block * inc_ref[slot][None]).reshape(every, points)

    def some(group, row, within, number):
        products = []
        for each in range(number):
            first, second = pairs[0, row + each], pairs[1, row + each]
            tile = tiles_ref[group, within + each]
            to_first = lax.dot_general(
                weighted_ref[second], tile, (((1,), (1,)), ((), ())), preferred_element_type=jnp.float32
            )
            to_second = jnp.dot(weighted_ref[first], tile, preferred_element_type=jnp.float32)
            products += [(first, to_first), (second, to_second)]
        for slot, product in products:
            field_ref[slot] += product

    def turn(group, carry):
        away = core[0] * (groups // 2)
        row = PAIR_GROUP * jnp.where(group < groups // 2, group + away, group - away)
        live = count[0] - row
        pltpu.make_async_copy(stacks[0], tiles_ref.at[group], tiles_sem.at[group]).wait()

        @pl.when(live >= PAIR_GROUP)
        def _():
            some(group, row, 0, PAIR_GROUP)

        @pl.when(live < PAIR_GROUP)
        def _():
            def one(within, inner):
                some(group, row + within, within, 1)
                return inner

            lax.fori_loop(0, jnp.maximum(live, 0), one, 0)

        return carry

    lax.fori_loop(0, groups, turn, 0)

    for slot in range(slot_total):
        product = ens_ref[slot].reshape(every, points).astype(jnp.float32) * field_ref[slot]
        out_ref[slot] = jnp.sum(product.reshape(every // step, step, points), axis=0).astype(out_ref.dtype)


def apply_pairs(got, small, stacks, pairs, count, core, members, step):
    slot_total, sources, rows, _ = got.shape
    points = stacks[0].shape[2]
    lane_chunks = points // LANES
    every = sources * members * step
    return pl.pallas_call(
        apply_kernel,
        in_specs=[
            pl.BlockSpec(memory_space=pltpu.SMEM),
            pl.BlockSpec(memory_space=pltpu.SMEM),
            pl.BlockSpec(memory_space=pltpu.SMEM),
            pl.BlockSpec(memory_space=pl.ANY),
            *[pl.BlockSpec(memory_space=pl.ANY)] * (len(stacks) + 1),
        ],
        out_specs=pl.BlockSpec(memory_space=pltpu.VMEM),
        scratch_shapes=[
            pltpu.VMEM((slot_total, sources, members * step, points), jnp.bfloat16),
            pltpu.VMEM((slot_total, step, points), jnp.bfloat16),
            pltpu.VMEM((slot_total, every, points), jnp.bfloat16),
            pltpu.VMEM((slot_total, every, points), jnp.float32),
            pltpu.VMEM((len(stacks), *stacks[0].shape), jnp.bfloat16),
            pltpu.SemaphoreType.DMA((slot_total, lane_chunks)),
            pltpu.SemaphoreType.DMA,
            pltpu.SemaphoreType.DMA((len(stacks),)),
        ],
        out_shape=jax.ShapeDtypeStruct((slot_total, step, points), jnp.bfloat16),
        compiler_params=pltpu.CompilerParams(vmem_limit_bytes=60 * MIB),
        cost_estimate=pl.CostEstimate(flops=100_000_000, bytes_accessed=22_000_000, transcendentals=0),
        name="apply",
    )(pairs, count, core, got, small, *stacks)


def finish_kernel(slots, own_ref, *refs, scale):
    *part_refs, back_ref, out_ref = refs
    total = own_ref[...]
    for part_ref in part_refs:
        total = total + part_ref[...].astype(jnp.float32)
    out_ref[...] = total * scale
    for owner in range(back_ref.shape[0]):
        slot = slots[owner]
        out_ref[slot] = out_ref[slot] + back_ref[owner].astype(jnp.float32) * scale


def finish(own, parts, back, slots, scale):
    return pl.pallas_call(
        functools.partial(finish_kernel, scale=scale),
        in_specs=[pl.BlockSpec(memory_space=pltpu.SMEM)] + [pl.BlockSpec(memory_space=pltpu.VMEM)] * (len(parts) + 2),
        out_specs=pl.BlockSpec(memory_space=pltpu.VMEM),
        out_shape=jax.ShapeDtypeStruct(own.shape, jnp.float32),
        compiler_params=pltpu.CompilerParams(vmem_limit_bytes=16 * MIB),
        name="finish",
    )(slots, own, *parts, back)


def per_device(ensemble, increment, coords, sent_slots, pair_list, pair_count):
    blocks, members, levels, points = ensemble.shape
    regions = lax.axis_size("region")
    groups = lax.axis_size("member")
    step = levels // groups
    slots = sent_slots.reshape(-1)
    pairs = pair_list.T
    own = lax.axis_index("member").reshape(1).astype(jnp.int32)
    small = lax.all_to_all(select(increment, coords, slots, own, step), "region", 0, 0, tiled=True)
    big = pack(ensemble, slots, groups)
    big, small = lax.optimization_barrier((big, small))
    got = lax.all_to_all(
        big.reshape(regions * groups, -1, LANES), ("region", "member"), 0, 0, tiled=True
    ).reshape(regions, groups, -1, LANES)
    swap = [(i, i ^ 1) for i in range(groups)]
    core, row = own & 1, own >> 1
    rows = groups // 2
    share = pairs.shape[1] // 2
    mine = [tiles(small, pairs, core * share + start) for start in range(0, share, PAIR_GROUP)]
    theirs = [lax.ppermute(stack, "member", swap) for stack in mine]
    keep, send = diag(ensemble, increment, coords, core, rows)
    merged = merge(keep, lax.ppermute(send, "member", swap), row)
    parts = [
        lax.ppermute(part, "member", [(i, (i + 2 * hop) % groups) for i in range(groups)])
        for hop, part in enumerate(merged[1:], 1)
    ]
    got, own_part = lax.optimization_barrier((got, merged[0]))
    stacks = [in_hbm(stack) for stack in mine + theirs]
    partial = apply_pairs(in_hbm(got), in_hbm(small), stacks, pairs, pair_count, core, members, step)
    partial, parts = lax.optimization_barrier((partial, parts))
    back = lax.all_to_all(partial, "region", 0, 0, tiled=True)
    return finish(own_part, parts, back, slots, 1.0 / (members * groups - 1))


def solution(mesh):
    in_specs = (
        P("region", "member", None, None),
        P("region", None, None),
        P("region", None, None),
        P("region", None, None),
        P("region", None),
        P("region"),
    )
    out_specs = P("region", "member", None)
    return jax.shard_map(
        per_device, mesh=mesh, in_specs=in_specs, out_specs=out_specs, check_vma=False
    )
```

```python
import functools

import jax
import jax.numpy as jnp
from jax import lax
from jax.experimental import pallas as pl
from jax.experimental.pallas import tpu as pltpu
from jax.sharding import PartitionSpec as P

LANES = 128
PAIR_GROUP = 4
DIAG_GROUP = 4
MIB = 1024 * 1024
UNIT = 12.0**-0.2
UNIT2 = UNIT * UNIT
LEAST = UNIT2 * 2.0**-12


def select_kernel(slots, own, inc_ref, coords_ref, out_ref, sem):
    total, rows, _ = out_ref.shape
    step = rows - coords_ref.shape[1]
    first = pl.multiple_of(own[0] * step, step)

    def copy(owner):
        return pltpu.make_async_copy(
            inc_ref.at[slots[owner], pl.ds(first, step), :], out_ref.at[owner, :step, :], sem.at[owner]
        )

    for owner in range(total):
        copy(owner).start()
    for owner in range(total):
        out_ref[owner, step:, :] = coords_ref[slots[owner]]
    for owner in range(total):
        copy(owner).wait()


def select(increment, coords, slots, own, step):
    total, points = slots.shape[0], coords.shape[2]
    return pl.pallas_call(
        select_kernel,
        in_specs=[
            pl.BlockSpec(memory_space=pltpu.SMEM),
            pl.BlockSpec(memory_space=pltpu.SMEM),
            pl.BlockSpec(memory_space=pl.ANY),
            pl.BlockSpec(memory_space=pltpu.VMEM),
        ],
        out_specs=pl.BlockSpec(memory_space=pltpu.VMEM),
        out_shape=jax.ShapeDtypeStruct((total, step + coords.shape[1], points), coords.dtype),
        scratch_shapes=[pltpu.SemaphoreType.DMA((total,))],
        compiler_params=pltpu.CompilerParams(vmem_limit_bytes=60 * MIB),
        name="select",
    )(slots, own, increment, coords)


def pack_kernel(slots, ens_ref, big_ref, ens_buf, out_buf, in_sem, out_sem):
    total, members, levels, points = ens_buf.shape
    parts = out_buf.shape[1]
    step = levels // parts
    lane_chunks = points // LANES

    def ens_copy(owner):
        return pltpu.make_async_copy(ens_ref.at[slots[owner]], ens_buf.at[owner], in_sem.at[owner])

    def out_copy(owner):
        return pltpu.make_async_copy(out_buf.at[owner], big_ref.at[owner], out_sem.at[owner])

    for owner in range(total):
        ens_copy(owner).start()
    for owner in range(total):
        ens_copy(owner).wait()
        for part in range(parts):
            here = slice(part * step, (part + 1) * step)
            for lane in range(lane_chunks):
                out_buf[owner, part, lane * members * step : (lane + 1) * members * step, :] = ens_buf[
                    owner, :, here, lane * LANES : (lane + 1) * LANES
                ].reshape(members * step, LANES)
        out_copy(owner).start()
    for owner in range(total):
        out_copy(owner).wait()


def pack(ensemble, slots, parts):
    blocks, members, levels, points = ensemble.shape
    total = slots.shape[0]
    rows = members * (levels // parts) * (points // LANES)
    return pl.pallas_call(
        pack_kernel,
        in_specs=[pl.BlockSpec(memory_space=pltpu.SMEM), pl.BlockSpec(memory_space=pl.ANY)],
        out_specs=pl.BlockSpec(memory_space=pl.ANY),
        out_shape=jax.ShapeDtypeStruct((total, parts, rows, LANES), ensemble.dtype),
        scratch_shapes=[
            pltpu.VMEM((total, members, levels, points), ensemble.dtype),
            pltpu.VMEM((total, parts, rows, LANES), ensemble.dtype),
            pltpu.SemaphoreType.DMA((total,)),
            pltpu.SemaphoreType.DMA((total,)),
        ],
        compiler_params=pltpu.CompilerParams(vmem_limit_bytes=60 * MIB),
        name="pack",
    )(slots, ensemble)


def in_hbm(value):
    return pltpu.with_memory_space_constraint(value, pltpu.HBM)


def three_parts(value):
    first = value.astype(jnp.bfloat16).astype(jnp.float32)
    rest = value - first
    second = rest.astype(jnp.bfloat16).astype(jnp.float32)
    return [first, second, rest - second]


def left_rows(places):
    east, north = places[0:1], places[1:2]
    one = jnp.ones_like(east)
    norm = UNIT2 * (east * east + north * north)
    rows = three_parts((-2.0 * UNIT2) * east) + three_parts((-2.0 * UNIT2) * north) + three_parts(norm)
    rows = rows + [one] * 3 + [jnp.zeros_like(east)] * 4
    return jnp.concatenate(rows, axis=0).astype(jnp.bfloat16)


def right_rows(places):
    east, north = places[0:1], places[1:2]
    one = jnp.ones_like(east)
    norm = UNIT2 * (east * east + north * north)
    rows = [east] * 3 + [north] * 3 + [one] * 3 + three_parts(norm) + [jnp.zeros_like(east)] * 4
    return jnp.concatenate(rows, axis=0).astype(jnp.bfloat16)


def tile_of(left, right):
    squared = lax.dot_general(left, right, (((0,), (0,)), ((), ())), preferred_element_type=jnp.float32)
    squared = jnp.maximum(squared, LEAST)
    inverse = lax.rsqrt(squared)
    z = squared * inverse
    outer = jnp.maximum(2.0 * UNIT - z, 0.0)
    inner = jnp.maximum(UNIT - z, 0.0)
    outer2 = outer * outer
    inner2 = inner * inner
    shifted = z + 2.0 * UNIT
    first = (outer2 * outer2) * (z * shifted - 0.5 * UNIT2)
    second = (inner2 * inner2) * (inner * shifted)
    return ((first + 4.0 * second) * inverse).astype(jnp.bfloat16)


def diag_block(block_index, core, ens_ref, inc_ref, coords_ref, keep_ref, send_ref, sum_ref):
    members, levels, points = ens_ref.shape[1:]
    parts, _, step, _ = keep_ref.shape
    rows = members * levels
    half = points // 2
    places = coords_ref[block_index].astype(jnp.float32)
    left, right = left_rows(places), right_rows(places)
    upper = tile_of(left[:, :half], right)
    lower = tile_of(left[:, half:], right[:, half:])
    weighted = (ens_ref[block_index] * inc_ref[block_index][None]).reshape(rows, points)
    near, far = weighted[:, :half], weighted[:, half:]
    field_near = jnp.dot(near, upper[:, :half], preferred_element_type=jnp.float32) + lax.dot_general(
        far, upper[:, half:], (((1,), (1,)), ((), ())), preferred_element_type=jnp.float32
    )
    field_far = jnp.dot(near, upper[:, half:], preferred_element_type=jnp.float32) + jnp.dot(
        far, lower, preferred_element_type=jnp.float32
    )
    block = ens_ref[block_index].astype(jnp.float32)
    sum_ref[block_index, :, :half] = jnp.sum(block[:, :, :half] * field_near.reshape(members, levels, half), axis=0)
    sum_ref[block_index, :, half:] = jnp.sum(block[:, :, half:] * field_far.reshape(members, levels, half), axis=0)
    for part in range(parts):
        mine = pl.multiple_of((2 * part + core[0]) * step, step)
        other = pl.multiple_of((2 * part + 1 - core[0]) * step, step)
        keep_ref[part, block_index] = sum_ref[block_index, pl.ds(mine, step), :]
        send_ref[part, block_index] = sum_ref[block_index, pl.ds(other, step), :]


def diag_kernel(core, ens_ref, *refs):
    for block_index in range(ens_ref.shape[0]):
        diag_block(block_index, core, ens_ref, *refs)


def diag(ensemble, increment, coords, core, parts):
    blocks, members, levels, points = ensemble.shape
    step = levels // (2 * parts)
    out = jax.ShapeDtypeStruct((parts, blocks, step, points), jnp.float32)
    return pl.pallas_call(
        diag_kernel,
        grid_spec=pltpu.PrefetchScalarGridSpec(
            num_scalar_prefetch=1,
            grid=(blocks // DIAG_GROUP,),
            in_specs=[
                pl.BlockSpec((DIAG_GROUP, members, levels, points), lambda b, c: (b, 0, 0, 0)),
                pl.BlockSpec((DIAG_GROUP, levels, points), lambda b, c: (b, 0, 0)),
                pl.BlockSpec((DIAG_GROUP, 2, points), lambda b, c: (b, 0, 0)),
            ],
            out_specs=[pl.BlockSpec((parts, DIAG_GROUP, step, points), lambda b, c: (0, b, 0, 0))] * 2,
            scratch_shapes=[pltpu.VMEM((DIAG_GROUP, levels, points), jnp.float32)],
        ),
        out_shape=[out, out],
        compiler_params=pltpu.CompilerParams(vmem_limit_bytes=60 * MIB),
        cost_estimate=pl.CostEstimate(flops=20_000_000_000, bytes_accessed=8_000_000, transcendentals=0),
        name="diag",
    )(core, ensemble, increment, coords)


def merge_kernel(row, keep_ref, got_ref, own_ref, *send_refs):
    parts = keep_ref.shape[0]
    own_ref[...] = keep_ref[row[0]] + got_ref[row[0]]
    for shift, send_ref in enumerate(send_refs, 1):
        there = lax.rem(row[0] + shift, parts)
        send_ref[...] = (keep_ref[there] + got_ref[there]).astype(send_ref.dtype)


def merge(keep, got, row):
    parts = keep.shape[0]
    out = [jax.ShapeDtypeStruct(keep.shape[1:], jnp.float32)]
    out += [jax.ShapeDtypeStruct(keep.shape[1:], jnp.bfloat16)] * (parts - 1)
    return pl.pallas_call(
        merge_kernel,
        in_specs=[pl.BlockSpec(memory_space=pltpu.SMEM)] + [pl.BlockSpec(memory_space=pltpu.VMEM)] * 2,
        out_specs=[pl.BlockSpec(memory_space=pltpu.VMEM)] * parts,
        out_shape=out,
        compiler_params=pltpu.CompilerParams(vmem_limit_bytes=16 * MIB),
        name="merge",
    )(row, keep, got)


def tiles_kernel(pairs, first, places_ref, out_ref, tile_ref, sem):
    def copy(within):
        return pltpu.make_async_copy(tile_ref.at[within], out_ref.at[within], sem.at[within])

    for within in range(tile_ref.shape[0]):
        index = first[0] + within
        left = left_rows(places_ref[pairs[0, index], -2:, :].astype(jnp.float32))
        right = right_rows(places_ref[pairs[1, index], -2:, :].astype(jnp.float32))
        tile_ref[within] = tile_of(left, right)
        copy(within).start()
    for within in range(tile_ref.shape[0]):
        copy(within).wait()


def tiles(places, pairs, first):
    shape = (PAIR_GROUP, places.shape[2], places.shape[2])
    return pl.pallas_call(
        tiles_kernel,
        in_specs=[
            pl.BlockSpec(memory_space=pltpu.SMEM),
            pl.BlockSpec(memory_space=pltpu.SMEM),
            pl.BlockSpec(memory_space=pltpu.VMEM),
        ],
        out_specs=pl.BlockSpec(memory_space=pl.ANY),
        out_shape=pltpu.HBM(shape, jnp.bfloat16),
        scratch_shapes=[pltpu.VMEM(shape, jnp.bfloat16), pltpu.SemaphoreType.DMA((PAIR_GROUP,))],
        compiler_params=pltpu.CompilerParams(vmem_limit_bytes=60 * MIB),
        cost_estimate=pl.CostEstimate(flops=4_000_000_000, bytes_accessed=2_000_000, transcendentals=0),
        name="tiles",
    )(pairs, first, places)


def apply_kernel(
    pairs, count, core, got_ref, small_ref, *refs,
):
    *stacks, out_ref, ens_ref, inc_ref, weighted_ref, field_ref, tiles_ref, ens_sem, inc_sem, tiles_sem = refs
    slot_total, sources, rows, points = ens_ref.shape
    step = inc_ref.shape[1]
    groups = len(stacks)
    lane_chunks = points // LANES
    every = sources * rows

    def ens_copies(slot):
        return [
            pltpu.make_async_copy(
                got_ref.at[slot, :, lane * rows : (lane + 1) * rows, :],
                ens_ref.at[slot, :, :, lane * LANES : (lane + 1) * LANES],
                ens_sem.at[slot, lane],
            )
            for lane in range(lane_chunks)
        ]

    inc_copy = pltpu.make_async_copy(small_ref.at[:, :step, :], inc_ref, inc_sem)

    def tile_copy(group):
        return pltpu.make_async_copy(stacks[group], tiles_ref.at[group], tiles_sem.at[group])

    inc_copy.start()
    for slot in range(slot_total):
        for copy in ens_copies(slot):
            copy.start()
    for group in range(2):
        tile_copy(group).start()
    inc_copy.wait()
    for slot in range(slot_total):
        field_ref[slot] = jnp.zeros((every, points), jnp.float32)
        for copy in ens_copies(slot):
            copy.wait()
        if slot % 2 == 1 and slot // 2 + 2 < groups:
            tile_copy(slot // 2 + 2).start()
        block = ens_ref[slot].reshape(every // step, step, points)
        weighted_ref[slot] = (block * inc_ref[slot][None]).reshape(every, points)

    def some(group, row, within, number):
        products = []
        for each in range(number):
            first, second = pairs[0, row + each], pairs[1, row + each]
            tile = tiles_ref[group + each // PAIR_GROUP, within + each % PAIR_GROUP]
            to_first = lax.dot_general(
                weighted_ref[second], tile, (((1,), (1,)), ((), ())), preferred_element_type=jnp.float32
            )
            to_second = jnp.dot(weighted_ref[first], tile, preferred_element_type=jnp.float32)
            products += [(first, to_first), (second, to_second)]
        for slot, product in products:
            field_ref[slot] += product

    def turn(couple, carry):
        group = 2 * couple
        away = core[0] * (groups // 2)
        row = PAIR_GROUP * jnp.where(group < groups // 2, group + away, group - away)
        live = count[0] - row
        for stack in range(2):
            pltpu.make_async_copy(stacks[0], tiles_ref.at[group + stack], tiles_sem.at[group + stack]).wait()

        @pl.when(live >= 2 * PAIR_GROUP)
        def _():
            some(group, row, 0, 2 * PAIR_GROUP)

        @pl.when(live < 2 * PAIR_GROUP)
        def _():
            half = live >= PAIR_GROUP

            @pl.when(half)
            def _():
                some(group, row, 0, PAIR_GROUP)

            start = jnp.where(half, PAIR_GROUP, 0)

            def one(within, inner):
                some(group + jnp.where(half, 1, 0), row + start + within, within, 1)
                return inner

            lax.fori_loop(0, jnp.maximum(live - start, 0), one, 0)

        return carry

    lax.fori_loop(0, groups // 2, turn, 0)

    for slot in range(slot_total):
        product = ens_ref[slot].reshape(every, points).astype(jnp.float32) * field_ref[slot]
        out_ref[slot] = jnp.sum(product.reshape(every // step, step, points), axis=0).astype(out_ref.dtype)


def apply_pairs(got, small, stacks, pairs, count, core, members, step):
    slot_total, sources, rows, _ = got.shape
    points = stacks[0].shape[2]
    lane_chunks = points // LANES
    every = sources * members * step
    return pl.pallas_call(
        apply_kernel,
        in_specs=[
            pl.BlockSpec(memory_space=pltpu.SMEM),
            pl.BlockSpec(memory_space=pltpu.SMEM),
            pl.BlockSpec(memory_space=pltpu.SMEM),
            pl.BlockSpec(memory_space=pl.ANY),
            *[pl.BlockSpec(memory_space=pl.ANY)] * (len(stacks) + 1),
        ],
        out_specs=pl.BlockSpec(memory_space=pltpu.VMEM),
        scratch_shapes=[
            pltpu.VMEM((slot_total, sources, members * step, points), jnp.bfloat16),
            pltpu.VMEM((slot_total, step, points), jnp.bfloat16),
            pltpu.VMEM((slot_total, every, points), jnp.bfloat16),
            pltpu.VMEM((slot_total, every, points), jnp.float32),
            pltpu.VMEM((len(stacks), *stacks[0].shape), jnp.bfloat16),
            pltpu.SemaphoreType.DMA((slot_total, lane_chunks)),
            pltpu.SemaphoreType.DMA,
            pltpu.SemaphoreType.DMA((len(stacks),)),
        ],
        out_shape=jax.ShapeDtypeStruct((slot_total, step, points), jnp.bfloat16),
        compiler_params=pltpu.CompilerParams(vmem_limit_bytes=60 * MIB),
        cost_estimate=pl.CostEstimate(flops=100_000_000, bytes_accessed=22_000_000, transcendentals=0),
        name="apply",
    )(pairs, count, core, got, small, *stacks)


def finish_kernel(slots, own_ref, *refs, scale):
    *part_refs, back_ref, out_ref = refs
    total = own_ref[...]
    for part_ref in part_refs:
        total = total + part_ref[...].astype(jnp.float32)
    out_ref[...] = total * scale
    for owner in range(back_ref.shape[0]):
        slot = slots[owner]
        out_ref[slot] = out_ref[slot] + back_ref[owner].astype(jnp.float32) * scale


def finish(own, parts, back, slots, scale):
    return pl.pallas_call(
        functools.partial(finish_kernel, scale=scale),
        in_specs=[pl.BlockSpec(memory_space=pltpu.SMEM)] + [pl.BlockSpec(memory_space=pltpu.VMEM)] * (len(parts) + 2),
        out_specs=pl.BlockSpec(memory_space=pltpu.VMEM),
        out_shape=jax.ShapeDtypeStruct(own.shape, jnp.float32),
        compiler_params=pltpu.CompilerParams(vmem_limit_bytes=16 * MIB),
        name="finish",
    )(slots, own, *parts, back)


def per_device(ensemble, increment, coords, sent_slots, pair_list, pair_count):
    blocks, members, levels, points = ensemble.shape
    regions = lax.axis_size("region")
    groups = lax.axis_size("member")
    step = levels // groups
    slots = sent_slots.reshape(-1)
    pairs = pair_list.T
    own = lax.axis_index("member").reshape(1).astype(jnp.int32)
    small = lax.all_to_all(select(increment, coords, slots, own, step), "region", 0, 0, tiled=True)
    big = pack(ensemble, slots, groups)
    big, small = lax.optimization_barrier((big, small))
    got = lax.all_to_all(
        big.reshape(regions * groups, -1, LANES), ("region", "member"), 0, 0, tiled=True
    ).reshape(regions, groups, -1, LANES)
    swap = [(i, i ^ 1) for i in range(groups)]
    core, row = own & 1, own >> 1
    rows = groups // 2
    share = pairs.shape[1] // 2
    mine = [tiles(small, pairs, core * share + start) for start in range(0, share, PAIR_GROUP)]
    theirs = [lax.ppermute(stack, "member", swap) for stack in mine]
    keep, send = diag(ensemble, increment, coords, core, rows)
    merged = merge(keep, lax.ppermute(send, "member", swap), row)
    parts = [
        lax.ppermute(part, "member", [(i, (i + 2 * hop) % groups) for i in range(groups)])
        for hop, part in enumerate(merged[1:], 1)
    ]
    got, own_part = lax.optimization_barrier((got, merged[0]))
    stacks = [in_hbm(stack) for stack in mine + theirs]
    partial = apply_pairs(in_hbm(got), in_hbm(small), stacks, pairs, pair_count, core, members, step)
    partial, parts = lax.optimization_barrier((partial, parts))
    back = lax.all_to_all(partial, "region", 0, 0, tiled=True)
    return finish(own_part, parts, back, slots, 1.0 / (members * groups - 1))


def solution(mesh):
    in_specs = (
        P("region", "member", None, None),
        P("region", None, None),
        P("region", None, None),
        P("region", None, None),
        P("region", None),
        P("region"),
    )
    out_specs = P("region", "member", None)
    return jax.shard_map(
        per_device, mesh=mesh, in_specs=in_specs, out_specs=out_specs, check_vma=False
    )
```

```python
import functools

import jax
import jax.numpy as jnp
from jax import lax
from jax.experimental import pallas as pl
from jax.experimental.pallas import tpu as pltpu
from jax.sharding import PartitionSpec as P

LANES = 128
PAIR_GROUP = 4
DIAG_GROUP = 4
MIB = 1024 * 1024
UNIT = 12.0**-0.2
UNIT2 = UNIT * UNIT
LEAST = UNIT2 * 2.0**-12


def select_kernel(slots, own, inc_ref, coords_ref, out_ref, sem):
    total, rows, _ = out_ref.shape
    step = rows - coords_ref.shape[1]
    first = pl.multiple_of(own[0] * step, step)

    def copy(owner):
        return pltpu.make_async_copy(
            inc_ref.at[slots[owner], pl.ds(first, step), :], out_ref.at[owner, :step, :], sem.at[owner]
        )

    for owner in range(total):
        copy(owner).start()
    for owner in range(total):
        out_ref[owner, step:, :] = coords_ref[slots[owner]]
    for owner in range(total):
        copy(owner).wait()


def select(increment, coords, slots, own, step):
    total, points = slots.shape[0], coords.shape[2]
    return pl.pallas_call(
        select_kernel,
        in_specs=[
            pl.BlockSpec(memory_space=pltpu.SMEM),
            pl.BlockSpec(memory_space=pltpu.SMEM),
            pl.BlockSpec(memory_space=pl.ANY),
            pl.BlockSpec(memory_space=pltpu.VMEM),
        ],
        out_specs=pl.BlockSpec(memory_space=pltpu.VMEM),
        out_shape=jax.ShapeDtypeStruct((total, step + coords.shape[1], points), coords.dtype),
        scratch_shapes=[pltpu.SemaphoreType.DMA((total,))],
        compiler_params=pltpu.CompilerParams(vmem_limit_bytes=60 * MIB),
        name="select",
    )(slots, own, increment, coords)


def pack_kernel(slots, ens_ref, big_ref, ens_buf, out_buf, in_sem, out_sem):
    total, members, levels, points = ens_buf.shape
    parts = out_buf.shape[1]
    step = levels // parts
    lane_chunks = points // LANES

    def ens_copy(owner):
        return pltpu.make_async_copy(ens_ref.at[slots[owner]], ens_buf.at[owner], in_sem.at[owner])

    def out_copy(owner):
        return pltpu.make_async_copy(out_buf.at[owner], big_ref.at[owner], out_sem.at[owner])

    for owner in range(total):
        ens_copy(owner).start()
    for owner in range(total):
        ens_copy(owner).wait()
        for part in range(parts):
            here = slice(part * step, (part + 1) * step)
            for lane in range(lane_chunks):
                out_buf[owner, part, lane * members * step : (lane + 1) * members * step, :] = ens_buf[
                    owner, :, here, lane * LANES : (lane + 1) * LANES
                ].reshape(members * step, LANES)
        out_copy(owner).start()
    for owner in range(total):
        out_copy(owner).wait()


def pack(ensemble, slots, parts):
    blocks, members, levels, points = ensemble.shape
    total = slots.shape[0]
    rows = members * (levels // parts) * (points // LANES)
    return pl.pallas_call(
        pack_kernel,
        in_specs=[pl.BlockSpec(memory_space=pltpu.SMEM), pl.BlockSpec(memory_space=pl.ANY)],
        out_specs=pl.BlockSpec(memory_space=pl.ANY),
        out_shape=jax.ShapeDtypeStruct((total, parts, rows, LANES), ensemble.dtype),
        scratch_shapes=[
            pltpu.VMEM((total, members, levels, points), ensemble.dtype),
            pltpu.VMEM((total, parts, rows, LANES), ensemble.dtype),
            pltpu.SemaphoreType.DMA((total,)),
            pltpu.SemaphoreType.DMA((total,)),
        ],
        compiler_params=pltpu.CompilerParams(vmem_limit_bytes=60 * MIB),
        name="pack",
    )(slots, ensemble)


def in_hbm(value):
    return pltpu.with_memory_space_constraint(value, pltpu.HBM)


def three_parts(value):
    first = value.astype(jnp.bfloat16).astype(jnp.float32)
    rest = value - first
    second = rest.astype(jnp.bfloat16).astype(jnp.float32)
    return [first, second, rest - second]


def left_rows(places):
    east, north = places[0:1], places[1:2]
    one = jnp.ones_like(east)
    norm = UNIT2 * (east * east + north * north)
    rows = three_parts((-2.0 * UNIT2) * east) + three_parts((-2.0 * UNIT2) * north) + three_parts(norm)
    rows = rows + [one] * 3 + [jnp.zeros_like(east)] * 4
    return jnp.concatenate(rows, axis=0).astype(jnp.bfloat16)


def right_rows(places):
    east, north = places[0:1], places[1:2]
    one = jnp.ones_like(east)
    norm = UNIT2 * (east * east + north * north)
    rows = [east] * 3 + [north] * 3 + [one] * 3 + three_parts(norm) + [jnp.zeros_like(east)] * 4
    return jnp.concatenate(rows, axis=0).astype(jnp.bfloat16)


def tile_of(left, right):
    squared = lax.dot_general(left, right, (((0,), (0,)), ((), ())), preferred_element_type=jnp.float32)
    squared = jnp.maximum(squared, LEAST)
    inverse = lax.rsqrt(squared)
    z = squared * inverse
    outer = jnp.maximum(2.0 * UNIT - z, 0.0)
    inner = jnp.maximum(UNIT - z, 0.0)
    outer2 = outer * outer
    inner2 = inner * inner
    shifted = z + 2.0 * UNIT
    first = (outer2 * outer2) * (z * shifted - 0.5 * UNIT2)
    second = (inner2 * inner2) * (inner * shifted)
    return ((first + 4.0 * second) * inverse).astype(jnp.bfloat16)


def diag_block(block_index, core, ens_ref, inc_ref, coords_ref, keep_ref, send_ref, sum_ref):
    members, levels, points = ens_ref.shape[1:]
    parts, _, step, _ = keep_ref.shape
    rows = members * levels
    half = points // 2
    places = coords_ref[block_index].astype(jnp.float32)
    left, right = left_rows(places), right_rows(places)
    upper = tile_of(left[:, :half], right)
    lower = tile_of(left[:, half:], right[:, half:])
    weighted = (ens_ref[block_index] * inc_ref[block_index][None]).reshape(rows, points)
    near, far = weighted[:, :half], weighted[:, half:]
    field_near = jnp.dot(near, upper[:, :half], preferred_element_type=jnp.float32) + lax.dot_general(
        far, upper[:, half:], (((1,), (1,)), ((), ())), preferred_element_type=jnp.float32
    )
    field_far = jnp.dot(near, upper[:, half:], preferred_element_type=jnp.float32) + jnp.dot(
        far, lower, preferred_element_type=jnp.float32
    )
    block = ens_ref[block_index].astype(jnp.float32)
    sum_ref[block_index, :, :half] = jnp.sum(block[:, :, :half] * field_near.reshape(members, levels, half), axis=0)
    sum_ref[block_index, :, half:] = jnp.sum(block[:, :, half:] * field_far.reshape(members, levels, half), axis=0)
    for part in range(parts):
        mine = pl.multiple_of((2 * part + core[0]) * step, step)
        other = pl.multiple_of((2 * part + 1 - core[0]) * step, step)
        keep_ref[part, block_index] = sum_ref[block_index, pl.ds(mine, step), :]
        send_ref[part, block_index] = sum_ref[block_index, pl.ds(other, step), :]


def diag_kernel(core, ens_ref, *refs):
    for block_index in range(ens_ref.shape[0]):
        diag_block(block_index, core, ens_ref, *refs)


def diag(ensemble, increment, coords, core, parts):
    blocks, members, levels, points = ensemble.shape
    step = levels // (2 * parts)
    out = jax.ShapeDtypeStruct((parts, blocks, step, points), jnp.float32)
    return pl.pallas_call(
        diag_kernel,
        grid_spec=pltpu.PrefetchScalarGridSpec(
            num_scalar_prefetch=1,
            grid=(blocks // DIAG_GROUP,),
            in_specs=[
                pl.BlockSpec((DIAG_GROUP, members, levels, points), lambda b, c: (b, 0, 0, 0)),
                pl.BlockSpec((DIAG_GROUP, levels, points), lambda b, c: (b, 0, 0)),
                pl.BlockSpec((DIAG_GROUP, 2, points), lambda b, c: (b, 0, 0)),
            ],
            out_specs=[pl.BlockSpec((parts, DIAG_GROUP, step, points), lambda b, c: (0, b, 0, 0))] * 2,
            scratch_shapes=[pltpu.VMEM((DIAG_GROUP, levels, points), jnp.float32)],
        ),
        out_shape=[out, out],
        compiler_params=pltpu.CompilerParams(vmem_limit_bytes=60 * MIB),
        cost_estimate=pl.CostEstimate(flops=20_000_000_000, bytes_accessed=8_000_000, transcendentals=0),
        name="diag",
    )(core, ensemble, increment, coords)


def merge_kernel(row, keep_ref, got_ref, own_ref, *send_refs):
    parts = keep_ref.shape[0]
    own_ref[...] = keep_ref[row[0]] + got_ref[row[0]]
    for shift, send_ref in enumerate(send_refs, 1):
        there = lax.rem(row[0] + shift, parts)
        send_ref[...] = (keep_ref[there] + got_ref[there]).astype(send_ref.dtype)


def merge(keep, got, row):
    parts = keep.shape[0]
    out = [jax.ShapeDtypeStruct(keep.shape[1:], jnp.float32)]
    out += [jax.ShapeDtypeStruct(keep.shape[1:], jnp.bfloat16)] * (parts - 1)
    return pl.pallas_call(
        merge_kernel,
        in_specs=[pl.BlockSpec(memory_space=pltpu.SMEM)] + [pl.BlockSpec(memory_space=pltpu.VMEM)] * 2,
        out_specs=[pl.BlockSpec(memory_space=pltpu.VMEM)] * parts,
        out_shape=out,
        compiler_params=pltpu.CompilerParams(vmem_limit_bytes=16 * MIB),
        name="merge",
    )(row, keep, got)


def tiles_kernel(pairs, first, places_ref, out_ref, tile_ref, sem):
    def copy(within):
        return pltpu.make_async_copy(tile_ref.at[within], out_ref.at[within], sem.at[within])

    for within in range(tile_ref.shape[0]):
        index = first[0] + within
        left = left_rows(places_ref[pairs[0, index], -2:, :].astype(jnp.float32))
        right = right_rows(places_ref[pairs[1, index], -2:, :].astype(jnp.float32))
        tile_ref[within] = tile_of(left, right)
        copy(within).start()
    for within in range(tile_ref.shape[0]):
        copy(within).wait()


def tiles(places, pairs, first):
    shape = (PAIR_GROUP, places.shape[2], places.shape[2])
    return pl.pallas_call(
        tiles_kernel,
        in_specs=[
            pl.BlockSpec(memory_space=pltpu.SMEM),
            pl.BlockSpec(memory_space=pltpu.SMEM),
            pl.BlockSpec(memory_space=pltpu.VMEM),
        ],
        out_specs=pl.BlockSpec(memory_space=pl.ANY),
        out_shape=pltpu.HBM(shape, jnp.bfloat16),
        scratch_shapes=[pltpu.VMEM(shape, jnp.bfloat16), pltpu.SemaphoreType.DMA((PAIR_GROUP,))],
        compiler_params=pltpu.CompilerParams(vmem_limit_bytes=60 * MIB),
        cost_estimate=pl.CostEstimate(flops=4_000_000_000, bytes_accessed=2_000_000, transcendentals=0),
        name="tiles",
    )(pairs, first, places)


def apply_kernel(
    pairs, count, core, got_ref, small_ref, *refs,
):
    *stacks, out_ref, ens_ref, inc_ref, weighted_ref, field_ref, tiles_ref, ens_sem, inc_sem, tiles_sem = refs
    slot_total, sources, rows, points = ens_ref.shape
    step = inc_ref.shape[1]
    groups = len(stacks)
    lane_chunks = points // LANES
    every = sources * rows

    def ens_copies(slot):
        return [
            pltpu.make_async_copy(
                got_ref.at[slot, :, lane * rows : (lane + 1) * rows, :],
                ens_ref.at[slot, :, :, lane * LANES : (lane + 1) * LANES],
                ens_sem.at[slot, lane],
            )
            for lane in range(lane_chunks)
        ]

    inc_copy = pltpu.make_async_copy(small_ref.at[:, :step, :], inc_ref, inc_sem)

    def tile_copy(group):
        return pltpu.make_async_copy(stacks[group], tiles_ref.at[group], tiles_sem.at[group])

    inc_copy.start()
    for slot in range(slot_total):
        for copy in ens_copies(slot):
            copy.start()
    for group in range(2):
        tile_copy(group).start()
    inc_copy.wait()
    for slot in range(slot_total):
        field_ref[slot] = jnp.zeros((every, points), jnp.float32)
        for copy in ens_copies(slot):
            copy.wait()
        if slot % 2 == 1 and slot // 2 + 2 < groups:
            tile_copy(slot // 2 + 2).start()
        block = ens_ref[slot].reshape(every // step, step, points)
        weighted_ref[slot] = (block * inc_ref[slot][None]).reshape(every, points)

    def some(group, row, within, number):
        products = []
        for each in range(number):
            first, second = pairs[0, row + each], pairs[1, row + each]
            tile = tiles_ref[group, within + each]
            to_first = lax.dot_general(
                weighted_ref[second], tile, (((1,), (1,)), ((), ())), preferred_element_type=jnp.float32
            )
            to_second = jnp.dot(weighted_ref[first], tile, preferred_element_type=jnp.float32)
            products += [(first, to_first), (second, to_second)]
        for slot, product in products:
            field_ref[slot] += product

    def turn(group, carry):
        away = core[0] * (groups // 2)
        row = PAIR_GROUP * jnp.where(group < groups // 2, group + away, group - away)
        live = count[0] - row
        pltpu.make_async_copy(stacks[0], tiles_ref.at[group], tiles_sem.at[group]).wait()

        @pl.when(live >= PAIR_GROUP)
        def _():
            some(group, row, 0, PAIR_GROUP)

        @pl.when(live < PAIR_GROUP)
        def _():
            def one(within, inner):
                some(group, row + within, within, 1)
                return inner

            lax.fori_loop(0, jnp.maximum(live, 0), one, 0)

        return carry

    lax.fori_loop(0, groups, turn, 0)

    for slot in range(slot_total):
        product = ens_ref[slot].reshape(every, points).astype(jnp.float32) * field_ref[slot]
        out_ref[slot] = jnp.sum(product.reshape(every // step, step, points), axis=0).astype(out_ref.dtype)


def apply_pairs(got, small, stacks, pairs, count, core, members, step):
    slot_total, sources, rows, _ = got.shape
    points = stacks[0].shape[2]
    lane_chunks = points // LANES
    every = sources * members * step
    return pl.pallas_call(
        apply_kernel,
        in_specs=[
            pl.BlockSpec(memory_space=pltpu.SMEM),
            pl.BlockSpec(memory_space=pltpu.SMEM),
            pl.BlockSpec(memory_space=pltpu.SMEM),
            pl.BlockSpec(memory_space=pl.ANY),
            *[pl.BlockSpec(memory_space=pl.ANY)] * (len(stacks) + 1),
        ],
        out_specs=pl.BlockSpec(memory_space=pltpu.VMEM),
        scratch_shapes=[
            pltpu.VMEM((slot_total, sources, members * step, points), jnp.bfloat16),
            pltpu.VMEM((slot_total, step, points), jnp.bfloat16),
            pltpu.VMEM((slot_total, every, points), jnp.bfloat16),
            pltpu.VMEM((slot_total, every, points), jnp.float32),
            pltpu.VMEM((len(stacks), *stacks[0].shape), jnp.bfloat16),
            pltpu.SemaphoreType.DMA((slot_total, lane_chunks)),
            pltpu.SemaphoreType.DMA,
            pltpu.SemaphoreType.DMA((len(stacks),)),
        ],
        out_shape=jax.ShapeDtypeStruct((slot_total, step, points), jnp.bfloat16),
        compiler_params=pltpu.CompilerParams(vmem_limit_bytes=60 * MIB),
        cost_estimate=pl.CostEstimate(flops=100_000_000, bytes_accessed=22_000_000, transcendentals=0),
        name="apply",
    )(pairs, count, core, got, small, *stacks)


def finish_kernel(slots, own_ref, *refs, scale):
    *part_refs, back_ref, out_ref = refs
    total = own_ref[...]
    for part_ref in part_refs:
        total = total + part_ref[...].astype(jnp.float32)
    out_ref[...] = total * scale
    for owner in range(back_ref.shape[0]):
        slot = slots[owner]
        out_ref[slot] = out_ref[slot] + back_ref[owner].astype(jnp.float32) * scale


def finish(own, parts, back, slots, scale):
    return pl.pallas_call(
        functools.partial(finish_kernel, scale=scale),
        in_specs=[pl.BlockSpec(memory_space=pltpu.SMEM)] + [pl.BlockSpec(memory_space=pltpu.VMEM)] * (len(parts) + 2),
        out_specs=pl.BlockSpec(memory_space=pltpu.VMEM),
        out_shape=jax.ShapeDtypeStruct(own.shape, jnp.float32),
        compiler_params=pltpu.CompilerParams(vmem_limit_bytes=16 * MIB),
        name="finish",
    )(slots, own, *parts, back)


def per_device(ensemble, increment, coords, sent_slots, pair_list, pair_count):
    blocks, members, levels, points = ensemble.shape
    regions = lax.axis_size("region")
    groups = lax.axis_size("member")
    step = levels // groups
    slots = sent_slots.reshape(-1)
    pairs = pair_list.T
    own = lax.axis_index("member").reshape(1).astype(jnp.int32)
    small = lax.all_to_all(select(increment, coords, slots, own, step), "region", 0, 0, tiled=True)
    big = pack(ensemble, slots, groups)
    big, small = lax.optimization_barrier((big, small))
    got = lax.all_to_all(
        big.reshape(regions * groups, -1, LANES), ("region", "member"), 0, 0, tiled=True
    ).reshape(regions, groups, -1, LANES)
    swap = [(i, i ^ 1) for i in range(groups)]
    core, row = own & 1, own >> 1
    rows = groups // 2
    share = pairs.shape[1] // 2
    mine = [tiles(small, pairs, core * share + start) for start in range(0, share, PAIR_GROUP)]
    theirs = [lax.ppermute(stack, "member", swap) for stack in mine]
    keep, send = diag(ensemble, increment, coords, core, rows)
    merged = merge(keep, lax.ppermute(send, "member", swap), row)
    parts = [
        lax.ppermute(part, "member", [(i, (i + 2 * hop) % groups) for i in range(groups)])
        for hop, part in enumerate(merged[1:], 1)
    ]
    got, own_part, theirs = lax.optimization_barrier((got, merged[0], theirs))
    stacks = [in_hbm(stack) for stack in mine + theirs]
    partial = apply_pairs(in_hbm(got), in_hbm(small), stacks, pairs, pair_count, core, members, step)
    partial, parts = lax.optimization_barrier((partial, parts))
    back = lax.all_to_all(partial, "region", 0, 0, tiled=True)
    return finish(own_part, parts, back, slots, 1.0 / (members * groups - 1))


def solution(mesh):
    in_specs = (
        P("region", "member", None, None),
        P("region", None, None),
        P("region", None, None),
        P("region", None, None),
        P("region", None),
        P("region"),
    )
    out_specs = P("region", "member", None)
    return jax.shard_map(
        per_device, mesh=mesh, in_specs=in_specs, out_specs=out_specs, check_vma=False
    )
```
